256 devices in a mesh: row: 8 (over z), col: 8 (over x, core), sub: 4 (over y).
Axes of the slice: x: 4, y: 4, z: 8, core: 2. Of those that a mesh axis runs over, the one named last changes fastest.
Arguments:
- front_entries: float32 [8192, 8192], P('row', ('col', 'sub')), may hold values from -1 to 4, as said below
- child_blocks: float32 [4, 2048, 2048], P('sub', 'row', 'col'), may hold values from -1 to 2, as said below
- child_map: int32 [4, 16], P('sub'), may hold values from 0 to 63, as said below
Outputs:
- factored: float32 [8192, 8192], P('row', ('col', 'sub'))
The draws below stay inside these ranges and needn't reach their ends.
Inputs may be any that keep to these rules, and one draw needn't show every extreme that they name: Each row of child_map lists 16 different parent blocks in increasing order and ends with block 63. In natural order front_entries is a symmetric matrix, and the assembled front is positive definite. `child_blocks`: in natural order each child's contribution block is a symmetric matrix.
All inputs are finite; a program needn't handle non-finite values.
Results may differ from the reference program's by a relative error of at most 0.00005.
Values sent between devices are 32-bit elements; how exact they have to be, the bound alone decides.
A program may use at most 128 MiB of HBM per device.

```python
import math
import jax
import jax.numpy as jnp
from jax import lax

BLK = 128
FB = 64
CBB = 16
NPIV = 6
NCHILD = 4
F = 8192
CB = 2048
N_ROW = 8
N_COL = 8


def natural_positions(order, groups):
    span = order // BLK // groups
    position = jnp.arange(order, dtype=jnp.int32)
    block = position // BLK
    return ((block % span * groups + block // span) * BLK + position % BLK).astype(jnp.int32)


def kernel_draw(key, order, noise_norm, diag_low, diag_high, amplitude):
    point_key, noise_key, diag_key = jax.random.split(key, 3)
    points = jax.random.uniform(point_key, (order,), jnp.float32, 0.0, order / 4.0)
    kernel = amplitude * jnp.exp(-jnp.abs(points[:, None] - points[None, :]))
    spread = noise_norm / (2.0 * math.sqrt(order))
    noise_field = jax.random.normal(noise_key, (order, order), jnp.float32) * spread
    diagonal = jax.random.uniform(diag_key, (order,), jnp.float32, diag_low, diag_high)
    symmetric = (noise_field + noise_field.T) * 0.7071
    return kernel + symmetric + jnp.diag(diagonal)


def draw_front_entries(key, part):
    matrix = kernel_draw(jax.random.fold_in(key, 11), F, 0.5, 1.0, 2.0, 1.0)
    row_places = natural_positions(F, N_ROW)
    col_places = natural_positions(F, N_COL)
    return matrix[row_places][:, col_places]


def draw_child_blocks(key, part):
    child_keys = jax.random.split(jax.random.fold_in(key, 23), NCHILD)
    row_places = natural_positions(CB, N_ROW)
    col_places = natural_positions(CB, N_COL)

    def draw_one_child(child_key):
        matrix = kernel_draw(child_key, CB, 0.25, 0.5, 1.0, 0.5)
        return matrix[row_places][:, col_places]
    return jax.vmap(draw_one_child)(child_keys)


def draw_child_map(key, part):
    child_keys = jax.random.split(jax.random.fold_in(key, 37), NCHILD)

    def draw_one_list(child_key):
        shuffled = jax.random.permutation(child_key, FB - 1).astype(jnp.int32)
        chosen = jnp.sort(shuffled[:CBB - 1])
        return jnp.concatenate([chosen, jnp.full((1,), FB - 1, jnp.int32)]).astype(jnp.int32)
    return jax.vmap(draw_one_list)(child_keys)


def setup_inputs(seed: int = 0) -> dict:
    arg_keys = jax.random.split(jax.random.key(seed), 4)
    front_entries = draw_front_entries(jax.random.fold_in(arg_keys[3], 71), 0)
    child_blocks = draw_child_blocks(jax.random.fold_in(arg_keys[3], 71), 0)
    child_map = draw_child_map(jax.random.fold_in(arg_keys[3], 71), 0)
    return dict(front_entries=front_entries, child_blocks=child_blocks, child_map=child_map)


def natural(stored, row_groups, col_groups):
    row_total, col_total = stored.shape
    row_span = row_total // BLK // row_groups
    col_span = col_total // BLK // col_groups
    reordered = stored.reshape(row_groups, row_span, BLK, col_total).transpose(1, 0, 2, 3).reshape(row_total, col_total)
    return reordered.reshape(row_total, col_groups, col_span, BLK).transpose(0, 2, 1, 3).reshape(row_total, col_total)

def stored_order(matrix, row_groups, col_groups):
    row_total, col_total = matrix.shape
    row_span = row_total // BLK // row_groups
    col_span = col_total // BLK // col_groups
    reordered = matrix.reshape(row_span, row_groups, BLK, col_total).transpose(1, 0, 2, 3).reshape(row_total, col_total)
    return reordered.reshape(row_total, col_span, col_groups, BLK).transpose(0, 2, 1, 3).reshape(row_total, col_total)

def reference(front_entries, child_blocks, child_map):
    assembled = natural(front_entries, N_ROW, N_COL)
    within = jnp.arange(BLK, dtype=jnp.int32)
    for child_number in range(NCHILD):
        child_natural = natural(child_blocks[child_number], N_ROW, N_COL)
        index_list = (child_map[child_number][:, None] * BLK + within[None, :]).reshape(-1).astype(jnp.int32)
        assembled = assembled.at[index_list[:, None], index_list[None, :]].add(child_natural)
    pivots = NPIV * BLK
    leading = jnp.linalg.cholesky(assembled[:pivots, :pivots])
    lower_left = jax.scipy.linalg.solve_triangular(leading, assembled[pivots:, :pivots].T, lower=True).T
    schur_block = assembled[pivots:, pivots:] - jnp.dot(lower_left, lower_left.T, precision=lax.Precision.HIGHEST)
    upper_half = jnp.concatenate([leading, jnp.zeros((pivots, F - pivots), jnp.float32)], axis=1)
    bottom = jnp.concatenate([lower_left, schur_block], axis=1)
    return stored_order(jnp.concatenate([upper_half, bottom], axis=0), N_ROW, N_COL)
```

```python
import jax
import jax.numpy as jnp
from jax import lax
from jax.experimental import pallas as pl
from jax.experimental.pallas import tpu as pltpu
from jax.sharding import PartitionSpec as P

BLK = 128
NPIV = 6
PIV = NPIV * BLK

highest = lax.Precision.HIGHEST
PLANE = ("col", "sub")


def place_kernel(map_ref, row_ref, buf_ref, acc_ref):
    acc_ref[...] = jnp.zeros_like(acc_ref)
    row = row_ref[0]

    def child_row(step, carry):
        q = step // 16
        block_row = step % 16
        i = map_ref[q, block_row]

        @pl.when(i % 8 == row)
        def _():
            slot = i // 8
            for block_col in range(16):
                j = map_ref[q, block_col]
                tile = buf_ref[block_row % 8, block_col % 8, q, block_row // 8, block_col // 8]
                acc_ref[j % 8, j // 16, slot, (j // 8) % 2] += tile

        return carry

    lax.fori_loop(0, 64, child_row, 0)


def place(maps, row, buf):
    return pl.pallas_call(
        place_kernel,
        out_shape=jax.ShapeDtypeStruct((8, 4, 8, 2, 4, BLK), jnp.float32),
        in_specs=[
            pl.BlockSpec(memory_space=pltpu.SMEM),
            pl.BlockSpec(memory_space=pltpu.SMEM),
            pl.BlockSpec(memory_space=pltpu.VMEM),
        ],
        out_specs=pl.BlockSpec(memory_space=pltpu.VMEM),
        name="place",
    )(maps, row, buf)


def factor(k):
    k = [[k[i * BLK : (i + 1) * BLK, j * BLK : (j + 1) * BLK] for j in range(NPIV)] for i in range(NPIV)]
    eye = jnp.eye(BLK, dtype=jnp.float32)
    zero = jnp.zeros((BLK, BLK), jnp.float32)
    low = [[zero] * NPIV for _ in range(NPIV)]
    inv = [[zero] * NPIV for _ in range(NPIV)]
    dot = lambda a, b: jnp.dot(a, b, precision=highest)
    for b in range(NPIV):
        d = k[b][b]
        for m in range(b):
            d = d - dot(low[b][m], low[b][m].T)
        lbb = jnp.linalg.cholesky(d)
        y = jax.scipy.linalg.solve_triangular(lbb, eye, lower=True)
        low[b][b] = lbb
        inv[b][b] = y
        for i in range(b + 1, NPIV):
            x = k[i][b]
            for m in range(b):
                x = x - dot(low[i][m], low[b][m].T)
            low[i][b] = dot(x, y.T)
        for j in range(b):
            x = zero
            for m in range(j, b):
                x = x + dot(low[b][m], inv[m][j])
            inv[b][j] = -dot(y, x)
    return jnp.block(low), jnp.block(inv)


def body(front, child, child_map):
    row = lax.axis_index("row")
    col = lax.axis_index("col")
    sub = lax.axis_index("sub")
    maps = lax.all_gather(child_map[0], "sub")
    shares = child.reshape(2, 32, 4, 2, BLK).transpose(1, 0, 3, 2, 4)
    shares = lax.all_to_all(shares, PLANE, 0, 0, tiled=True)
    panel = front[:, :BLK].reshape(8, 32, 4, BLK).transpose(1, 0, 2, 3)
    panel = lax.all_to_all(panel, PLANE, 0, 0, tiled=True)
    panel = panel.reshape(8, 4, 8, 4, BLK)[:NPIV, 0]
    buf = lax.all_gather(shares, "row").reshape(8, 8, 4, 2, 2, 4, BLK)
    acc = place(maps, row[None].astype(jnp.int32), buf)
    panel = panel + acc[:NPIV, 0, :, 0]
    moved = lax.all_to_all(acc.reshape(32, 8, 2, 4, BLK), PLANE, 0, 0, tiled=True)
    matrix = front + moved.transpose(1, 0, 3, 2, 4).reshape(1024, 256)
    rows = lax.all_gather(panel, PLANE)
    rows = rows.transpose(2, 0, 3, 1, 4).reshape(1024, PIV)
    top = lax.all_gather(jnp.concatenate([rows[:BLK], matrix[:BLK]], axis=1), "row")
    top = top[:NPIV].reshape(PIV, PIV + 256)
    low, inv = factor(top[:, :PIV])
    left = jnp.dot(rows, inv.T, precision=highest)
    right = jnp.dot(inv, top[:, PIV:], precision=highest)
    piv_row = row < NPIV
    own = lax.dynamic_slice(low, (jnp.minimum(row, NPIV - 1) * BLK, 0), (BLK, PIV))
    left = left.at[:BLK].set(jnp.where(piv_row, own, left[:BLK]))
    schur = matrix - jnp.dot(left, right, precision=highest)
    schur = schur.at[:BLK].set(jnp.where(piv_row, 0.0, schur[:BLK]))
    column = lax.dynamic_slice(left, (0, jnp.minimum(col, NPIV - 1) * BLK), (1024, BLK))
    owner = (sub == 0) & (col < NPIV)
    return schur.at[:, :BLK].set(jnp.where(owner, column, schur[:, :BLK]))


def solution(mesh):
    placed = (P("row", ("col", "sub")), P("sub", "row", "col"), P("sub", None))
    return jax.shard_map(
        body, mesh=mesh, in_specs=placed, out_specs=P("row", ("col", "sub")), check_vma=False
    )
```

```python
import jax
import jax.numpy as jnp
from jax import lax
from jax.experimental import pallas as pl
from jax.experimental.pallas import tpu as pltpu
from jax.sharding import PartitionSpec as P

BLK = 128
NPIV = 6
PIV = NPIV * BLK
PLANE = ("col", "sub")
HI = lax.Precision.HIGHEST
VM = pl.BlockSpec(memory_space=pltpu.VMEM)
SM = pl.BlockSpec(memory_space=pltpu.SMEM)


def nt(a, b, precision=HI):
    return lax.dot_general(a, b, (((1,), (1,)), ((), ())), precision=precision, preferred_element_type=jnp.float32)
def tn(a, b, precision=HI):
    return lax.dot_general(a, b, (((0,), (0,)), ((), ())), precision=precision, preferred_element_type=jnp.float32)

def rsqrt(x):
    return lax.rsqrt(x)

def eliminate(a_ref):
    sub = lax.broadcasted_iota(jnp.int32, (8, 256), 0)
    for g in range(16):
        rows = a_ref[8 * g : 8 * g + 8, :]
        left = rows[:, :BLK]
        e = {}
        for j in range(8):
            c = jnp.broadcast_to(left[:, 8 * g + j : 8 * g + j + 1], (8, BLK))
            for i in range(j, 8):
                e[j, i] = jnp.broadcast_to(c[i : i + 1, :], (8, BLK))
        r = [jnp.broadcast_to(rows[i : i + 1, :], (8, 256)) for i in range(8)]
        out = None
        for j in range(8):
            s = rsqrt(e[j, j])
            u = {i: e[j, i] * s for i in range(j + 1, 8)}
            for i in range(j + 1, 8):
                for m in range(i, 8):
                    e[i, m] = e[i, m] - u[i] * u[m]
            rj = r[j] * jnp.concatenate([s, s], axis=1)
            for i in range(j + 1, 8):
                r[i] = r[i] - jnp.concatenate([u[i], u[i]], axis=1) * rj
            out = rj if out is None else jnp.where(sub == j, rj, out)
        a_ref[8 * g : 8 * g + 8, :] = out
        if g < 15:
            t = tn(out[:, :BLK], out)
            a_ref[8 * g + 8 :, :] = a_ref[8 * g + 8 :, :] - t[8 * g + 8 :, :]

def factor_kernel(k_ref, l_ref, y_ref, a_ref, m_ref):
    eye = (lax.broadcasted_iota(jnp.int32, (BLK, BLK), 0) == lax.broadcasted_iota(jnp.int32, (BLK, BLK), 1)).astype(jnp.float32)
    low = lax.broadcasted_iota(jnp.int32, (BLK, BLK), 0) >= lax.broadcasted_iota(jnp.int32, (BLK, BLK), 1)
    m_ref[...] = k_ref[...]
    l_ref[...] = jnp.zeros_like(l_ref)
    def step(b, carry):
        at = pl.ds(pl.multiple_of(b * BLK, BLK), BLK)
        a_ref[:, :BLK] = m_ref[at, at]
        a_ref[:, BLK:] = eye
        eliminate(a_ref)
        y = a_ref[:, BLK:]
        y_ref[b] = y
        l_ref[at, at] = jnp.where(low, a_ref[:, :BLK].T, 0.0)
        def solve(i, c):
            rows = pl.ds(pl.multiple_of(i * BLK, BLK), BLK)
            l_ref[rows, at] = nt(m_ref[rows, at], y)
            return c
        lax.fori_loop(b + 1, NPIV, solve, 0)
        def update(i, c):
            rows = pl.ds(pl.multiple_of(i * BLK, BLK), BLK)
            m_ref[rows, :] = m_ref[rows, :] - nt(l_ref[rows, at], l_ref[:, at])
            return c
        lax.fori_loop(b + 1, NPIV, update, 0)
        return carry
    lax.fori_loop(0, NPIV, step, 0)

def factor(k):
    return pl.pallas_call(
        factor_kernel,
        out_shape=(jax.ShapeDtypeStruct((PIV, PIV), jnp.float32), jax.ShapeDtypeStruct((NPIV, BLK, BLK), jnp.float32)),
        in_specs=[pl.BlockSpec(memory_space=pltpu.VMEM)],
        out_specs=(pl.BlockSpec(memory_space=pltpu.VMEM),)*2,
        scratch_shapes=[pltpu.VMEM((BLK, 256), jnp.float32), pltpu.VMEM((PIV, PIV), jnp.float32)],
        cost_estimate=pl.CostEstimate(flops=60_000_000_000, bytes_accessed=200_000_000, transcendentals=0),
        name="factor",
    )(k)


def split(x):
    high = x.astype(jnp.bfloat16)
    return high, (x - high.astype(jnp.float32)).astype(jnp.bfloat16)


def dot3(a, b, dims):
    def one(x, y):
        return lax.dot_general(x, y, (dims, ((), ())), preferred_element_type=jnp.float32)

    return one(a[0], b[0]) + (one(a[0], b[1]) + one(a[1], b[0]))


NT = ((1,), (1,))
NN = ((1,), (0,))


def schur_kernel(
    where_ref, rows_ref, top_ref, matrix_ref, low_ref, inv_ref, out_ref,
    lh, ll, yh, yl, uh, ul, x_ref,
):
    tile = pl.program_id(0)
    row, col, sub = where_ref[0], where_ref[1], where_ref[2]

    @pl.when(tile == 0)
    def _():
        high, rest = split(low_ref[...])
        lh[...] = high
        ll[...] = rest
        zero = jnp.zeros((BLK, BLK), jnp.float32)
        for p in range(3):
            first, second = inv_ref[2 * p], inv_ref[2 * p + 1]
            at = 256 * p
            cross = jnp.dot(low_ref[at + BLK : at + 256, at : at + BLK], first, precision=HI)
            cross = -jnp.dot(second, cross, precision=HI)
            pair = jnp.concatenate(
                [jnp.concatenate([first, zero], axis=1), jnp.concatenate([cross, second], axis=1)], axis=0
            )
            high, rest = split(pair)
            yh[p] = high
            yl[p] = rest
        for p in range(3):
            at = 256 * p
            x = top_ref[at : at + 256, :]
            if p:
                x = x - dot3((lh[at : at + 256, :at], ll[at : at + 256, :at]), (uh[:at, :], ul[:at, :]), NN)
            high, rest = split(dot3((yh[p], yl[p]), split(x), NN))
            uh[at : at + 256, :] = high
            ul[at : at + 256, :] = rest

    acc = matrix_ref[...]
    xs = []
    for p in range(3):
        at = 256 * p
        x = rows_ref[:, at : at + 256]
        for m in range(p):
            cut = slice(256 * m, 256 * m + 256)
            x = x - dot3(xs[m], (lh[at : at + 256, cut], ll[at : at + 256, cut]), NT)
        x = dot3(split(x), (yh[p], yl[p]), NT)
        x_ref[:, at : at + 256] = x
        xs.append(split(x))
        acc = acc - dot3(xs[p], (uh[at : at + 256, :], ul[at : at + 256, :]), NN)
    out_ref[...] = acc

    @pl.when((tile == 0) & (row < NPIV))
    def _():
        out_ref[:BLK, :] = jnp.zeros((BLK, 256), jnp.float32)
        x_ref[:BLK, :] = low_ref[pl.ds(pl.multiple_of(row * BLK, BLK), BLK), :]

    @pl.when((sub == 0) & (col < NPIV))
    def _():
        out_ref[:, :BLK] = x_ref[:, pl.ds(pl.multiple_of(col * BLK, BLK), BLK)]


def schur(where, rows, top, matrix, low, inv):
    whole = lambda shape: pl.BlockSpec(shape, lambda t: (0,) * len(shape), pipeline_mode=pl.Buffered(1))
    return pl.pallas_call(
        schur_kernel,
        out_shape=jax.ShapeDtypeStruct((1024, 256), jnp.float32),
        grid=(4,),
        in_specs=[
            SM,
            pl.BlockSpec((256, PIV), lambda t: (t, 0)),
            whole((PIV, 256)),
            pl.BlockSpec((256, 256), lambda t: (t, 0)),
            whole((PIV, PIV)),
            whole((NPIV, BLK, BLK)),
        ],
        out_specs=pl.BlockSpec((256, 256), lambda t: (t, 0)),
        scratch_shapes=[
            pltpu.VMEM((PIV, PIV), jnp.bfloat16),
            pltpu.VMEM((PIV, PIV), jnp.bfloat16),
            pltpu.VMEM((3, 256, 256), jnp.bfloat16),
            pltpu.VMEM((3, 256, 256), jnp.bfloat16),
            pltpu.VMEM((PIV, 256), jnp.bfloat16),
            pltpu.VMEM((PIV, 256), jnp.bfloat16),
            pltpu.VMEM((256, PIV), jnp.float32),
        ],
        name="schur",
    )(where, rows, top, matrix, low, inv)


def place_kernel(map_ref, where_ref, buf_ref, acc_ref):
    acc_ref[...] = jnp.zeros_like(acc_ref)
    row = where_ref[0]

    def child_row(step, carry):
        q = step // 16
        block_row = step % 16
        i = map_ref[q, block_row]

        @pl.when(i % 8 == row)
        def _():
            slot = i // 8
            for block_col in range(16):
                j = map_ref[q, block_col]
                tile = buf_ref[block_row % 8, block_col % 8, q, block_row // 8, block_col // 8]
                acc_ref[j % 8, j // 16, slot, (j // 8) % 2] += tile

        return carry

    lax.fori_loop(0, 64, child_row, 0)


def place(maps, where, buf):
    return pl.pallas_call(
        place_kernel,
        out_shape=jax.ShapeDtypeStruct((8, 4, 8, 2, 4, BLK), jnp.float32),
        in_specs=[SM, SM, VM],
        out_specs=VM,
        name="place",
    )(maps, where, buf)


def place_pivot_kernel(map_ref, buf_ref, acc_ref):
    for i in range(NPIV):
        for j in range(NPIV):
            acc_ref[i, j] = buf_ref[i, 32 + j]

    def child_row(step, carry):
        q = step // NPIV
        block_row = step % NPIV
        i = map_ref[q, block_row]

        @pl.when(i < NPIV)
        def _():
            for block_col in range(NPIV):
                j = map_ref[q, block_col]

                @pl.when(j < NPIV)
                def _():
                    acc_ref[i, j] += buf_ref[block_row, block_col * 4 + q]

        return carry

    lax.fori_loop(0, 4 * NPIV, child_row, 0)


def place_pivot(maps, buf):
    return pl.pallas_call(
        place_pivot_kernel,
        out_shape=jax.ShapeDtypeStruct((NPIV, NPIV, 4, BLK), jnp.float32),
        in_specs=[SM, VM],
        out_specs=VM,
        name="place_pivot",
    )(maps, buf)


def body(front, child, child_map):
    where = jnp.stack([lax.axis_index(a) for a in ("row", "col", "sub")]).astype(jnp.int32)
    maps = lax.all_gather(child_map[0], "sub")
    shares = child.reshape(2, 32, 4, 2, BLK).transpose(1, 0, 3, 2, 4)
    shares = lax.all_to_all(shares, PLANE, 0, 0, tiled=True)
    panel = front[:, :BLK].reshape(8, 32, 4, BLK).transpose(1, 0, 2, 3)
    panel = lax.all_to_all(panel, PLANE, 0, 0, tiled=True)
    panel = panel.reshape(8, 4, 8, 4, BLK)[:NPIV, 0]
    pivot = jnp.concatenate([shares[:, 0, 0], panel[:, 0]], axis=0)
    pivot = place_pivot(maps, lax.all_gather(pivot, "row"))
    k = lax.all_gather(pivot, PLANE).transpose(1, 0, 3, 2, 4).reshape(PIV, PIV)
    shares, _ = lax.optimization_barrier((shares, pivot))
    low, inv = factor(k)
    buf = lax.all_gather(shares, "row").reshape(8, 8, 4, 2, 2, 4, BLK)
    acc = place(maps, where, buf)
    panel = panel + acc[:NPIV, 0, :, 0]
    rows = lax.all_gather(panel, PLANE)
    rows = rows.transpose(2, 0, 3, 1, 4).reshape(1024, PIV)
    moved = lax.all_to_all(acc.reshape(32, 8, 2, 4, BLK), PLANE, 0, 0, tiled=True)
    matrix = front + moved.transpose(1, 0, 3, 2, 4).reshape(1024, 256)
    top = lax.all_gather(matrix[:BLK], "row")[:NPIV].reshape(PIV, 256)
    return schur(where, rows, top, matrix, low, inv)


def solution(mesh):
    placed = (P("row", ("col", "sub")), P("sub", "row", "col"), P("sub", None))
    return jax.shard_map(
        body, mesh=mesh, in_specs=placed, out_specs=P("row", ("col", "sub")), check_vma=False
    )
```

```python
import jax
import jax.numpy as jnp
from jax import lax
from jax.experimental import pallas as pl
from jax.experimental.pallas import tpu as pltpu
from jax.sharding import PartitionSpec as P

BLK = 128
NPIV = 6
PIV = NPIV * BLK
PLANE = ("col", "sub")
HI = lax.Precision.HIGHEST
VM = pl.BlockSpec(memory_space=pltpu.VMEM)
SM = pl.BlockSpec(memory_space=pltpu.SMEM)


def nt(a, b, precision=HI):
    return lax.dot_general(a, b, (((1,), (1,)), ((), ())), precision=precision, preferred_element_type=jnp.float32)
def tn(a, b, precision=HI):
    return lax.dot_general(a, b, (((0,), (0,)), ((), ())), precision=precision, preferred_element_type=jnp.float32)

def rsqrt(x):
    return lax.rsqrt(x)

def eliminate(a_ref):
    sub = lax.broadcasted_iota(jnp.int32, (8, 256), 0)
    for g in range(16):
        rows = a_ref[8 * g : 8 * g + 8, :]
        left = rows[:, :BLK]
        e = {}
        for j in range(8):
            c = jnp.broadcast_to(left[:, 8 * g + j : 8 * g + j + 1], (8, BLK))
            for i in range(j, 8):
                e[j, i] = jnp.broadcast_to(c[i : i + 1, :], (8, BLK))
        r = [jnp.broadcast_to(rows[i : i + 1, :], (8, 256)) for i in range(8)]
        out = None
        for j in range(8):
            s = rsqrt(e[j, j])
            u = {i: e[j, i] * s for i in range(j + 1, 8)}
            for i in range(j + 1, 8):
                for m in range(i, 8):
                    e[i, m] = e[i, m] - u[i] * u[m]
            rj = r[j] * jnp.concatenate([s, s], axis=1)
            for i in range(j + 1, 8):
                r[i] = r[i] - jnp.concatenate([u[i], u[i]], axis=1) * rj
            out = rj if out is None else jnp.where(sub == j, rj, out)
        a_ref[8 * g : 8 * g + 8, :] = out
        if g < 15:
            t = tn(out[:, :BLK], out)
            a_ref[8 * g + 8 :, :] = a_ref[8 * g + 8 :, :] - t[8 * g + 8 :, :]

def factor_kernel(k_ref, l_ref, y_ref, a_ref, m_ref):
    eye = (lax.broadcasted_iota(jnp.int32, (BLK, BLK), 0) == lax.broadcasted_iota(jnp.int32, (BLK, BLK), 1)).astype(jnp.float32)
    low = lax.broadcasted_iota(jnp.int32, (BLK, BLK), 0) >= lax.broadcasted_iota(jnp.int32, (BLK, BLK), 1)
    for i in range(NPIV):
        for j in range(i + 1):
            m_ref[i * BLK : (i + 1) * BLK, j * BLK : (j + 1) * BLK] = k_ref[i * (i + 1) // 2 + j]
    l_ref[...] = jnp.zeros_like(l_ref)
    def step(b, carry):
        at = pl.ds(pl.multiple_of(b * BLK, BLK), BLK)
        a_ref[:, :BLK] = m_ref[at, at]
        a_ref[:, BLK:] = eye
        eliminate(a_ref)
        y = a_ref[:, BLK:]
        y_ref[b] = y
        l_ref[at, at] = jnp.where(low, a_ref[:, :BLK].T, 0.0)
        def solve(i, c):
            rows = pl.ds(pl.multiple_of(i * BLK, BLK), BLK)
            l_ref[rows, at] = nt(m_ref[rows, at], y)
            return c
        lax.fori_loop(b + 1, NPIV, solve, 0)
        def update(i, c):
            rows = pl.ds(pl.multiple_of(i * BLK, BLK), BLK)
            m_ref[rows, :] = m_ref[rows, :] - nt(l_ref[rows, at], l_ref[:, at])
            return c
        lax.fori_loop(b + 1, NPIV, update, 0)
        return carry
    lax.fori_loop(0, NPIV, step, 0)

def factor(k):
    return pl.pallas_call(
        factor_kernel,
        out_shape=(jax.ShapeDtypeStruct((PIV, PIV), jnp.float32), jax.ShapeDtypeStruct((NPIV, BLK, BLK), jnp.float32)),
        in_specs=[pl.BlockSpec(memory_space=pltpu.VMEM)],
        out_specs=(pl.BlockSpec(memory_space=pltpu.VMEM),)*2,
        scratch_shapes=[pltpu.VMEM((BLK, 256), jnp.float32), pltpu.VMEM((PIV, PIV), jnp.float32)],
        cost_estimate=pl.CostEstimate(flops=60_000_000_000, bytes_accessed=200_000_000, transcendentals=0),
        name="factor",
    )(k)


MESH = pl.DeviceIdType.MESH
TILES = [(i, j) for i in range(NPIV) for j in range(i + 1)]
NT_ = len(TILES)


def pivot_kernel(child_ref, front_ref, map_ref, k_ref, maps_ref, z_ref, acc_ref, send, got, z_got, k_got, p_got):
    r, c, s = lax.axis_index("row"), lax.axis_index("col"), lax.axis_index("sub")
    e = c * 4 + s
    x, core = c // 2, c % 2
    chip = x * 4 + s
    partner = (r, x * 2 + 1 - core, s)

    def plane_peer(d):
        p = (e + d) % 32
        return p, (r, p // 4, p % 4)

    def chip_peer(d):
        p = (chip + d) % 16
        c2 = (p // 4) * 2 + core
        return c2 * 4 + p % 4, (r, c2, p % 4)

    barrier = pltpu.get_barrier_semaphore()

    def greet_plane(d, carry):
        pl.semaphore_signal(barrier, inc=1, device_id=plane_peer(d)[1], device_id_type=MESH)
        return carry

    def greet_row(d, carry):
        pl.semaphore_signal(barrier, inc=1, device_id=((r + d) % 8, c, s), device_id_type=MESH)
        return carry

    lax.fori_loop(1, 32, greet_plane, 0)
    lax.fori_loop(1, 8, greet_row, 0)
    pl.semaphore_wait(barrier, 38)

    def push(src, dst, ssem, rsem, device):
        return pltpu.make_async_remote_copy(
            src_ref=src, dst_ref=dst, send_sem=ssem, recv_sem=rsem, device_id=device, device_id_type=MESH
        )

    has_child = (r < NPIV) & (c < NPIV)
    has_front = has_child & (s == 0)
    spot = jnp.minimum(r, NPIV - 1)
    seat = jnp.minimum(c, NPIV - 1)

    def child_copy(d):
        p, device = plane_peer(d)
        return push(child_ref.at[p], z_ref.at[spot, s * 6 + seat], send.at[0], got.at[0], device)

    def front_copy(d):
        p, device = plane_peer(d)
        return push(front_ref.at[p], z_ref.at[spot, 24 + seat], send.at[1], got.at[1], device)

    def map_copy(d):
        return push(map_ref, maps_ref.at[s], send.at[2], got.at[2], (r, c, (s + d) % 4))

    own_child = pltpu.make_async_copy(child_ref.at[e], z_ref.at[spot, s * 6 + seat], got.at[0])
    own_front = pltpu.make_async_copy(front_ref.at[e], z_ref.at[spot, 24 + seat], got.at[1])
    own_map = pltpu.make_async_copy(map_ref, maps_ref.at[s], got.at[2])

    @pl.when(has_child)
    def _():
        own_child.start()

        def one(d, carry):
            child_copy(d).start()
            return carry

        lax.fori_loop(1, 32, one, 0)

    @pl.when(has_front)
    def _():
        own_front.start()

        def one(d, carry):
            front_copy(d).start()
            return carry

        lax.fori_loop(1, 32, one, 0)

    own_map.start()
    for d in range(1, 4):
        map_copy(d).start()

    def z_copy(d):
        return push(z_ref.at[spot], z_ref.at[spot], send.at[3], z_got.at[spot], ((r + d) % 8, c, s))

    @pl.when(r < NPIV)
    def _():
        child_part = z_ref.at[spot, pl.ds(0, 24)]
        front_part = z_ref.at[spot, pl.ds(24, 6)]
        pltpu.make_async_copy(child_part, child_part, got.at[0]).wait()
        pltpu.make_async_copy(front_part, front_part, got.at[1]).wait()
        for d in (4, 3, 5, 2, 6, 1, 7):
            z_copy(d).start()

    pltpu.make_async_copy(maps_ref, maps_ref, got.at[2]).wait()
    for i in range(NPIV):
        @pl.when(r != i)
        def _():
            pltpu.make_async_copy(z_ref.at[i], z_ref.at[i], z_got.at[i]).wait()

    for t, (i, j) in enumerate(TILES):
        acc_ref[t] = z_ref[i, 24 + j]

    def add_child(q, carry):
        wanted = maps_ref[q][:NPIV]
        tiles = z_ref[:, pl.ds(q * 6, 6)]
        for j in range(NPIV):
            pick = jnp.where(wanted == float(j), 1.0, 0.0)[None, :, None, :]
            strip = jnp.sum(tiles * pick, axis=1)
            for i in range(j, NPIV):
                pick = jnp.where(wanted == float(i), 1.0, 0.0)[:, None, :]
                acc_ref[i * (i + 1) // 2 + j] += jnp.sum(strip * pick, axis=0)
        return carry

    lax.fori_loop(0, 4, add_child, 0)

    own_k = pltpu.make_async_copy(acc_ref, k_ref.at[:, e], got.at[3])
    own_k.start()

    def k_copy(d):
        return push(acc_ref, k_ref.at[:, e], send.at[4], k_got.at[d], chip_peer(d)[1])

    def pair_copy(d):
        spot_e = chip_peer(16 - d)[0]
        return push(k_ref.at[:, spot_e], k_ref.at[:, spot_e], send.at[5], p_got.at[d], partner)

    for d in range(1, 16):
        k_copy(d).start()
    own_k.wait()
    pair_copy(0).start()

    def forward(d, carry):
        k_copy(d).wait_recv()
        pair_copy(d).start()
        return carry

    lax.fori_loop(1, 16, forward, 0)

    def finish(d, carry):
        pair_copy(d).wait()
        return carry

    lax.fori_loop(0, 16, finish, 0)

    def sent(d, carry):
        k_copy(d).wait_send()
        return carry

    lax.fori_loop(1, 16, sent, 0)

    @pl.when(has_child)
    def _():
        lax.fori_loop(1, 32, lambda d, carry: (child_copy(d).wait_send(), carry)[1], 0)

    @pl.when(has_front)
    def _():
        lax.fori_loop(1, 32, lambda d, carry: (front_copy(d).wait_send(), carry)[1], 0)

    for d in range(1, 4):
        map_copy(d).wait_send()

    @pl.when(r < NPIV)
    def _():
        for d in range(1, 8):
            z_copy(d).wait_send()


def gather_pivot(child, front, child_map):
    return pl.pallas_call(
        pivot_kernel,
        out_shape=(
            jax.ShapeDtypeStruct((NT_, 32, 4, BLK), jnp.float32),
            jax.ShapeDtypeStruct((4, 16, BLK), jnp.float32),
        ),
        in_specs=[VM] * 3,
        out_specs=(VM, VM),
        scratch_shapes=[
            pltpu.VMEM((NPIV, 30, 4, BLK), jnp.float32),
            pltpu.VMEM((NT_, 4, BLK), jnp.float32),
            pltpu.SemaphoreType.DMA((6,)),
            pltpu.SemaphoreType.DMA((4,)),
            pltpu.SemaphoreType.DMA((NPIV,)),
            pltpu.SemaphoreType.DMA((16,)),
            pltpu.SemaphoreType.DMA((16,)),
        ],
        compiler_params=pltpu.CompilerParams(collective_id=0, has_side_effects=True),
        cost_estimate=pl.CostEstimate(flops=20_000_000_000, bytes_accessed=60_000_000, transcendentals=0),
        name="gather_pivot",
    )(child, front, child_map)


def split(x):
    high = x.astype(jnp.bfloat16)
    return high, (x - high.astype(jnp.float32)).astype(jnp.bfloat16)


def dot3(a, b, dims):
    def one(x, y):
        return lax.dot_general(x, y, (dims, ((), ())), preferred_element_type=jnp.float32)

    return one(a[0], b[0]) + (one(a[0], b[1]) + one(a[1], b[0]))


NT = ((1,), (1,))
NN = ((1,), (0,))


def schur_kernel(
    where_ref, rows_ref, top_ref, matrix_ref, low_ref, inv_ref, out_ref,
    lh, ll, yh, yl, uh, ul, x_ref,
):
    tile = pl.program_id(0)
    row, col, sub = where_ref[0], where_ref[1], where_ref[2]

    @pl.when(tile == 0)
    def _():
        high, rest = split(low_ref[...])
        lh[...] = high
        ll[...] = rest
        zero = jnp.zeros((BLK, BLK), jnp.float32)
        for p in range(3):
            first, second = inv_ref[2 * p], inv_ref[2 * p + 1]
            at = 256 * p
            cross = jnp.dot(low_ref[at + BLK : at + 256, at : at + BLK], first, precision=HI)
            cross = -jnp.dot(second, cross, precision=HI)
            pair = jnp.concatenate(
                [jnp.concatenate([first, zero], axis=1), jnp.concatenate([cross, second], axis=1)], axis=0
            )
            high, rest = split(pair)
            yh[p] = high
            yl[p] = rest
        for p in range(3):
            at = 256 * p
            x = top_ref[at : at + 256, :]
            if p:
                x = x - dot3((lh[at : at + 256, :at], ll[at : at + 256, :at]), (uh[:at, :], ul[:at, :]), NN)
            high, rest = split(dot3((yh[p], yl[p]), split(x), NN))
            uh[at : at + 256, :] = high
            ul[at : at + 256, :] = rest

    acc = matrix_ref[...]
    xs = []
    for p in range(3):
        at = 256 * p
        x = rows_ref[:, at : at + 256]
        for m in range(p):
            cut = slice(256 * m, 256 * m + 256)
            x = x - dot3(xs[m], (lh[at : at + 256, cut], ll[at : at + 256, cut]), NT)
        x = dot3(split(x), (yh[p], yl[p]), NT)
        x_ref[:, at : at + 256] = x
        xs.append(split(x))
        acc = acc - dot3(xs[p], (uh[at : at + 256, :], ul[at : at + 256, :]), NN)
    out_ref[...] = acc

    @pl.when((tile == 0) & (row < NPIV))
    def _():
        out_ref[:BLK, :] = jnp.zeros((BLK, 256), jnp.float32)
        x_ref[:BLK, :] = low_ref[pl.ds(pl.multiple_of(row * BLK, BLK), BLK), :]

    @pl.when((sub == 0) & (col < NPIV))
    def _():
        out_ref[:, :BLK] = x_ref[:, pl.ds(pl.multiple_of(col * BLK, BLK), BLK)]


def schur(where, rows, top, matrix, low, inv):
    whole = lambda shape: pl.BlockSpec(shape, lambda t: (0,) * len(shape), pipeline_mode=pl.Buffered(1))
    return pl.pallas_call(
        schur_kernel,
        out_shape=jax.ShapeDtypeStruct((1024, 256), jnp.float32),
        grid=(4,),
        in_specs=[
            SM,
            pl.BlockSpec((256, PIV), lambda t: (t, 0)),
            whole((PIV, 256)),
            pl.BlockSpec((256, 256), lambda t: (t, 0)),
            whole((PIV, PIV)),
            whole((NPIV, BLK, BLK)),
        ],
        out_specs=pl.BlockSpec((256, 256), lambda t: (t, 0)),
        scratch_shapes=[
            pltpu.VMEM((PIV, PIV), jnp.bfloat16),
            pltpu.VMEM((PIV, PIV), jnp.bfloat16),
            pltpu.VMEM((3, 256, 256), jnp.bfloat16),
            pltpu.VMEM((3, 256, 256), jnp.bfloat16),
            pltpu.VMEM((PIV, 256), jnp.bfloat16),
            pltpu.VMEM((PIV, 256), jnp.bfloat16),
            pltpu.VMEM((256, PIV), jnp.float32),
        ],
        name="schur",
    )(where, rows, top, matrix, low, inv)


def place_kernel(map_ref, where_ref, buf_ref, acc_ref):
    acc_ref[...] = jnp.zeros_like(acc_ref)
    row = where_ref[0]

    def child_row(step, carry):
        q = step // 16
        block_row = step % 16
        i = map_ref[q, block_row]

        @pl.when(i % 8 == row)
        def _():
            slot = i // 8
            for block_col in range(16):
                j = map_ref[q, block_col]
                tile = buf_ref[block_row % 8, block_col % 8, q, block_row // 8, block_col // 8]
                acc_ref[j % 8, j // 16, slot, (j // 8) % 2] += tile

        return carry

    lax.fori_loop(0, 64, child_row, 0)


def place(maps, where, buf):
    return pl.pallas_call(
        place_kernel,
        out_shape=jax.ShapeDtypeStruct((8, 4, 8, 2, 4, BLK), jnp.float32),
        in_specs=[SM, SM, VM],
        out_specs=VM,
        name="place",
    )(maps, where, buf)


def body(front, child, child_map):
    child = child[0]
    where = jnp.stack([lax.axis_index(a) for a in ("row", "col", "sub")]).astype(jnp.int32)
    wide = jnp.broadcast_to(child_map[0].astype(jnp.float32)[:, None], (16, BLK))
    k, maps = gather_pivot(child[:BLK, :BLK].reshape(32, 4, BLK), front[:BLK, :BLK].reshape(32, 4, BLK), wide)
    low, inv = factor(k.reshape(NT_, BLK, BLK))
    maps = maps[:, :, 0].astype(jnp.int32)
    shares = child.reshape(2, 32, 4, 2, BLK).transpose(1, 0, 3, 2, 4)
    shares = lax.all_to_all(shares, PLANE, 0, 0, tiled=True)
    panel = front[:, :BLK].reshape(8, 32, 4, BLK).transpose(1, 0, 2, 3)
    panel = lax.all_to_all(panel, PLANE, 0, 0, tiled=True)
    panel = panel.reshape(8, 4, 8, 4, BLK)[:NPIV, 0]
    buf = lax.all_gather(shares, "row").reshape(8, 8, 4, 2, 2, 4, BLK)
    acc = place(maps, where, buf)
    panel = panel + acc[:NPIV, 0, :, 0]
    rows = lax.all_gather(panel, PLANE)
    rows = rows.transpose(2, 0, 3, 1, 4).reshape(1024, PIV)
    moved = lax.all_to_all(acc.reshape(32, 8, 2, 4, BLK), PLANE, 0, 0, tiled=True)
    matrix = front + moved.transpose(1, 0, 3, 2, 4).reshape(1024, 256)
    top = lax.all_gather(matrix[:BLK], "row")[:NPIV].reshape(PIV, 256)
    return schur(where, rows, top, matrix, low, inv)


def solution(mesh):
    placed = (P("row", ("col", "sub")), P("sub", "row", "col"), P("sub", None))
    return jax.shard_map(
        body, mesh=mesh, in_specs=placed, out_specs=P("row", ("col", "sub")), check_vma=False
    )
```

```python
import jax
import jax.numpy as jnp
from jax import lax
from jax.experimental import pallas as pl
from jax.experimental.pallas import tpu as pltpu
from jax.sharding import PartitionSpec as P

BLK = 128
NPIV = 6
PIV = NPIV * BLK
PLANE = ("col", "sub")
HI = lax.Precision.HIGHEST
VM = pl.BlockSpec(memory_space=pltpu.VMEM)
SM = pl.BlockSpec(memory_space=pltpu.SMEM)


def nt(a, b, precision=HI):
    return lax.dot_general(a, b, (((1,), (1,)), ((), ())), precision=precision, preferred_element_type=jnp.float32)
def tn(a, b, precision=HI):
    return lax.dot_general(a, b, (((0,), (0,)), ((), ())), precision=precision, preferred_element_type=jnp.float32)

def rsqrt(x):
    return lax.rsqrt(x)

def eliminate(a_ref):
    sub = lax.broadcasted_iota(jnp.int32, (8, 256), 0)
    for g in range(16):
        rows = a_ref[8 * g : 8 * g + 8, :]
        left = rows[:, :BLK]
        e = {}
        for j in range(8):
            c = jnp.broadcast_to(left[:, 8 * g + j : 8 * g + j + 1], (8, BLK))
            for i in range(j, 8):
                e[j, i] = jnp.broadcast_to(c[i : i + 1, :], (8, BLK))
        r = [jnp.broadcast_to(rows[i : i + 1, :], (8, 256)) for i in range(8)]
        out = None
        for j in range(8):
            s = rsqrt(e[j, j])
            u = {i: e[j, i] * s for i in range(j + 1, 8)}
            for i in range(j + 1, 8):
                for m in range(i, 8):
                    e[i, m] = e[i, m] - u[i] * u[m]
            rj = r[j] * jnp.concatenate([s, s], axis=1)
            for i in range(j + 1, 8):
                r[i] = r[i] - jnp.concatenate([u[i], u[i]], axis=1) * rj
            out = rj if out is None else jnp.where(sub == j, rj, out)
        a_ref[8 * g : 8 * g + 8, :] = out
        if g < 15:
            t = tn(out[:, :BLK], out)
            a_ref[8 * g + 8 :, :] = a_ref[8 * g + 8 :, :] - t[8 * g + 8 :, :]

def factor_steps(k_ref, l_ref, y_ref, a_ref, m_ref, progress):
    r_iota = lax.broadcasted_iota(jnp.int32, (BLK, BLK), 0)
    c_iota = lax.broadcasted_iota(jnp.int32, (BLK, BLK), 1)
    for i in range(NPIV):
        for j in range(i + 1):
            m_ref[i * BLK : (i + 1) * BLK, j * BLK : (j + 1) * BLK] = k_ref[i * (i + 1) // 2 + j]
        if i < NPIV - 1:
            m_ref[i * BLK : (i + 1) * BLK, (i + 1) * BLK :] = jnp.zeros((BLK, PIV - (i + 1) * BLK), jnp.float32)
    l_ref[...] = jnp.zeros_like(l_ref)

    def step(b, carry):
        progress(b)
        at = pl.ds(pl.multiple_of(b * BLK, BLK), BLK)
        a_ref[:, :BLK] = m_ref[at, at]
        a_ref[:, BLK:] = jnp.where(r_iota == c_iota, 1.0, 0.0)
        eliminate(a_ref)
        y = a_ref[:, BLK:]
        y_ref[b] = y
        l_ref[at, at] = jnp.where(r_iota >= c_iota, a_ref[:, :BLK].T, 0.0)

        def solve(i, c):
            rows = pl.ds(pl.multiple_of(i * BLK, BLK), BLK)
            l_ref[rows, at] = nt(m_ref[rows, at], y)
            return c

        lax.fori_loop(b + 1, NPIV, solve, 0)

        def update(i, c):
            rows = pl.ds(pl.multiple_of(i * BLK, BLK), BLK)
            m_ref[rows, :] = m_ref[rows, :] - nt(l_ref[rows, at], l_ref[:, at])
            return c

        lax.fori_loop(b + 1, NPIV, update, 0)
        return carry

    lax.fori_loop(0, NPIV, step, 0)


MESH = pl.DeviceIdType.MESH
TILES = [(i, j) for i in range(NPIV) for j in range(i + 1)]
NTILE = len(TILES)


class Place:
    def __init__(self):
        self.r, self.c, self.s = (lax.axis_index(a) for a in ("row", "col", "sub"))
        self.e = self.c * 4 + self.s
        self.core = self.c % 2
        self.chip = (self.c // 2) * 4 + self.s
        self.partner = (self.r, self.c + 1 - 2 * self.core, self.s)

    def plane(self, d):
        p = (self.e + d) % 32
        return p, (self.r, p // 4, p % 4)

    def same_core(self, d):
        p = (self.chip + d) % 16
        c = (p // 4) * 2 + self.core
        return c * 4 + p % 4, (self.r, c, p % 4)

    def line(self, d):
        return ((self.r + d) % 8, self.c, self.s)

    def greet(self):
        barrier = pltpu.get_barrier_semaphore()

        def plane(d, carry):
            pl.semaphore_signal(barrier, inc=1, device_id=self.plane(d)[1], device_id_type=MESH)
            return carry

        def line(d, carry):
            pl.semaphore_signal(barrier, inc=1, device_id=self.line(d), device_id_type=MESH)
            return carry

        lax.fori_loop(1, 32, plane, 0)
        lax.fori_loop(1, 8, line, 0)
        pl.semaphore_wait(barrier, 38)


def push(src, dst, ssem, rsem, device):
    return pltpu.make_async_remote_copy(
        src_ref=src, dst_ref=dst, send_sem=ssem, recv_sem=rsem, device_id=device, device_id_type=MESH
    )


def arrive(ref, sem):
    pltpu.make_async_copy(ref, ref, sem).wait()


def loop(low, high, f):
    def one(d, carry):
        f(d)
        return carry

    lax.fori_loop(low, high, one, 0)


def gather_kernel(
    child_ref, front_ref, map_ref, k_ref, maps_ref, buf_ref, panel_ref,
    z_ref, acc_ref, send, got, z_got, f_got, k_got, p_got, right_got, left_got,
):
    at = Place()
    r, c, s, e = at.r, at.c, at.s, at.e
    at.greet()
    pivot_row = r < NPIV
    has_front = (c < NPIV) & (s == 0)
    spot = jnp.minimum(r, NPIV - 1)
    seat = jnp.minimum(c, NPIV - 1)

    def child_copy(d):
        p, device = at.plane(d)
        return push(child_ref.at[:, :, p], buf_ref.at[r, e], send.at[0], got.at[0], device)

    def front_copy(d):
        p, device = at.plane(d)
        return push(front_ref.at[:, p], panel_ref.at[seat], send.at[1], got.at[1], device)

    def map_copy(d):
        return push(map_ref, maps_ref.at[s], send.at[2], got.at[2], (r, c, (s + d) % 4))

    pltpu.make_async_copy(child_ref.at[:, :, e], buf_ref.at[r, e], got.at[0]).start()
    pltpu.make_async_copy(map_ref, maps_ref.at[s], got.at[2]).start()
    loop(1, 32, lambda d: child_copy(d).start())

    @pl.when(has_front)
    def _():
        pltpu.make_async_copy(front_ref.at[:, e], panel_ref.at[seat], got.at[1]).start()
        loop(1, 32, lambda d: front_copy(d).start())

    for d in range(1, 4):
        map_copy(d).start()

    def z_copy(d):
        return push(buf_ref.at[spot, pl.ds(0, 24), 0, 0], z_ref.at[spot, pl.ds(0, 24)], send.at[3], z_got.at[spot], at.line(d))

    def f_copy(d):
        return push(panel_ref.at[:, 0], z_ref.at[spot, pl.ds(24, 6)], send.at[4], f_got.at[spot], at.line(d))

    def right_copy(k):
        block = (r + 8 - k) % 8
        return push(buf_ref.at[block], buf_ref.at[block], send.at[5], right_got.at[k], at.line(1))

    def left_copy(k):
        block = (r + k) % 8
        return push(buf_ref.at[block], buf_ref.at[block], send.at[6], left_got.at[k], at.line(7))

    def right_wait(k):
        arrive(buf_ref.at[(r + 7 - k) % 8], right_got.at[k])

    def left_wait(k):
        arrive(buf_ref.at[(r + 1 + k) % 8], left_got.at[k])

    arrive(buf_ref.at[r], got.at[0])
    arrive(panel_ref, got.at[1])

    @pl.when(pivot_row)
    def _():
        pltpu.make_async_copy(buf_ref.at[spot, pl.ds(0, 24), 0, 0], z_ref.at[spot, pl.ds(0, 24)], z_got.at[spot]).start()
        pltpu.make_async_copy(panel_ref.at[:, 0], z_ref.at[spot, pl.ds(24, 6)], f_got.at[spot]).start()
        for d in (4, 3, 5, 2, 6, 1, 7):
            z_copy(d).start()
            f_copy(d).start()

    right_copy(0).start()
    left_copy(0).start()
    arrive(maps_ref, got.at[2])
    for i in range(NPIV):
        arrive(z_ref.at[i, pl.ds(0, 24)], z_got.at[i])
        arrive(z_ref.at[i, pl.ds(24, 6)], f_got.at[i])

    for t, (i, j) in enumerate(TILES):
        acc_ref[t] = z_ref[i, 24 + j]

    def add_child(q):
        wanted = maps_ref[q][:NPIV]
        strips = []
        for j in range(NPIV):
            strip = None
            for seat_j in range(j + 1):
                pick = jnp.where(wanted[seat_j : seat_j + 1] == float(j), 1.0, 0.0)[None]
                term = z_ref[:, seat_j * 4 + q] * pick
                strip = term if strip is None else strip + term
            strips.append(strip)
        for j in range(NPIV):
            for i in range(j, NPIV):
                pick = jnp.where(wanted == float(i), 1.0, 0.0)[:, None, :]
                acc_ref[i * (i + 1) // 2 + j] += jnp.sum(strips[j] * pick, axis=0)

    loop(0, 4, add_child)

    own_k = pltpu.make_async_copy(acc_ref, k_ref.at[:, e], got.at[3])
    own_k.start()

    def k_copy(d):
        return push(acc_ref, k_ref.at[:, e], send.at[7], k_got.at[d], at.same_core(d)[1])

    def pair_copy(d):
        where_e = at.same_core(16 - d)[0]
        return push(k_ref.at[:, where_e], k_ref.at[:, where_e], send.at[8], p_got.at[d], at.partner)

    def forward(d):
        k_copy(d).wait_recv()
        pair_copy(d).start()

    loop(1, 16, lambda d: k_copy(d).start())
    right_wait(0)
    right_copy(1).start()
    left_wait(0)
    left_copy(1).start()
    own_k.wait()
    pair_copy(0).start()
    right_wait(1)
    right_copy(2).start()
    left_wait(1)
    left_copy(2).start()
    loop(1, 16, forward)
    right_wait(2)
    right_copy(3).start()
    left_wait(2)
    loop(0, 16, lambda d: pair_copy(d).wait())
    right_wait(3)

    loop(1, 16, lambda d: k_copy(d).wait_send())
    loop(1, 32, lambda d: child_copy(d).wait_send())

    @pl.when(has_front)
    def _():
        loop(1, 32, lambda d: front_copy(d).wait_send())

    for d in range(1, 4):
        map_copy(d).wait_send()

    @pl.when(pivot_row)
    def _():
        for d in range(1, 8):
            z_copy(d).wait_send()
            f_copy(d).wait_send()

    for k in range(4):
        right_copy(k).wait_send()
    for k in range(3):
        left_copy(k).wait_send()


def gather_all(child, front, child_map):
    dma = pltpu.SemaphoreType.DMA
    return pl.pallas_call(
        gather_kernel,
        out_shape=(
            jax.ShapeDtypeStruct((NTILE, 32, 4, BLK), jnp.float32),
            jax.ShapeDtypeStruct((4, 16, BLK), jnp.float32),
            jax.ShapeDtypeStruct((8, 32, 2, 2, 4, BLK), jnp.float32),
            jax.ShapeDtypeStruct((NPIV, 8, 4, BLK), jnp.float32),
        ),
        in_specs=[VM] * 3,
        out_specs=(VM,) * 4,
        scratch_shapes=[
            pltpu.VMEM((NPIV, 30, 4, BLK), jnp.float32),
            pltpu.VMEM((NTILE, 4, BLK), jnp.float32),
            dma((9,)), dma((4,)), dma((NPIV,)), dma((NPIV,)), dma((16,)), dma((16,)), dma((4,)), dma((3,)),
        ],
        compiler_params=pltpu.CompilerParams(collective_id=0, has_side_effects=True),
        name="gather_all",
    )(child, front, child_map)


def factor_kernel(
    k_ref, acc_ref, panel_ref, front_ref, low_ref, inv_ref, rows_ref, moved_ref, top_ref,
    a_ref, m_ref, share_ref, w_ref, send, got, r_got, p_got, t_got,
):
    at = Place()
    r, c, s, e = at.r, at.c, at.s, at.e
    at.greet()
    spot = jnp.minimum(r, NPIV - 1)

    def move_copy(d):
        p, device = at.plane(d)
        return push(acc_ref.at[p], moved_ref.at[:, :, e], send.at[0], got.at[0], device)

    pltpu.make_async_copy(acc_ref.at[e], moved_ref.at[:, :, e], got.at[0]).start()
    loop(1, 32, lambda d: move_copy(d).start())

    for j in range(NPIV):
        for slot in range(8):
            share_ref[slot, j] = acc_ref[j * 4, slot, 0] + panel_ref[j, slot]

    own_rows = pltpu.make_async_copy(share_ref, rows_ref.at[:, :, e], got.at[1])

    def rows_copy(d):
        return push(share_ref, rows_ref.at[:, :, e], send.at[1], r_got.at[d], at.same_core(d)[1])

    def pair_copy(d):
        where_e = at.same_core(16 - d)[0]
        return push(rows_ref.at[:, :, where_e], rows_ref.at[:, :, where_e], send.at[2], p_got.at[d], at.partner)

    def top_copy(d):
        return push(w_ref, top_ref.at[spot], send.at[3], t_got.at[spot], at.line(d))

    own_rows.start()
    loop(1, 16, lambda d: rows_copy(d).start())

    def after_first():
        own_rows.wait()
        pair_copy(0).start()
        arrive(moved_ref, got.at[0])

        @pl.when(r < NPIV)
        def _():
            w_ref[...] = moved_ref[0] + front_ref[...]
            pltpu.make_async_copy(w_ref, top_ref.at[spot], t_got.at[spot]).start()
            for d in (4, 3, 5, 2, 6, 1, 7):
                top_copy(d).start()

    def forward(d):
        rows_copy(d).wait_recv()
        pair_copy(d).start()

    def progress(b):
        pl.when(b == 1)(after_first)
        pl.when(b == 3)(lambda: loop(1, 16, forward))

    factor_steps(k_ref, low_ref, inv_ref, a_ref, m_ref, progress)

    loop(0, 16, lambda d: pair_copy(d).wait())
    for i in range(NPIV):
        arrive(top_ref.at[i], t_got.at[i])
    loop(1, 16, lambda d: rows_copy(d).wait_send())
    loop(1, 32, lambda d: move_copy(d).wait_send())

    @pl.when(r < NPIV)
    def _():
        for d in range(1, 8):
            top_copy(d).wait_send()


def factor_all(k, acc, panel, front):
    dma = pltpu.SemaphoreType.DMA
    f32 = lambda *shape: jax.ShapeDtypeStruct(shape, jnp.float32)
    return pl.pallas_call(
        factor_kernel,
        out_shape=(
            f32(PIV, PIV),
            f32(NPIV, BLK, BLK),
            f32(8, NPIV, 32, 4, BLK),
            f32(8, 2, 32, 4, BLK),
            f32(NPIV, 2, 32, 4, BLK),
        ),
        in_specs=[VM] * 4,
        out_specs=(VM,) * 5,
        scratch_shapes=[
            pltpu.VMEM((BLK, 256), jnp.float32),
            pltpu.VMEM((PIV, PIV), jnp.float32),
            pltpu.VMEM((8, NPIV, 4, BLK), jnp.float32),
            pltpu.VMEM((2, 32, 4, BLK), jnp.float32),
            dma((4,)), dma((2,)), dma((16,)), dma((16,)), dma((NPIV,)),
        ],
        compiler_params=pltpu.CompilerParams(collective_id=1, has_side_effects=True, vmem_limit_bytes=40 * 1024 * 1024),
        name="factor_all",
    )(k, acc, panel, front)


def place_kernel(map_ref, where_ref, buf_ref, acc_ref):
    acc_ref[...] = jnp.zeros_like(acc_ref)
    row = where_ref[0]

    def child_row(step):
        q = step // 16
        block_row = step % 16
        i = map_ref[q, block_row]

        @pl.when(i % 8 == row)
        def _():
            slot = i // 8
            for block_col in range(16):
                j = map_ref[q, block_col]
                tile = buf_ref[block_row % 8, block_col % 8 * 4 + q, block_row // 8, block_col // 8]
                acc_ref[j % 8 * 4 + j // 16, slot, (j // 8) % 2] += tile

    loop(0, 64, child_row)


def place(maps, where, buf):
    return pl.pallas_call(
        place_kernel,
        out_shape=jax.ShapeDtypeStruct((32, 8, 2, 4, BLK), jnp.float32),
        in_specs=[SM, SM, VM],
        out_specs=VM,
        name="place",
    )(maps, where, buf)


def split(x):
    high = x.astype(jnp.bfloat16)
    return high, (x - high.astype(jnp.float32)).astype(jnp.bfloat16)


def dot3(a, b, dims):
    def one(x, y):
        return lax.dot_general(x, y, (dims, ((), ())), preferred_element_type=jnp.float32)

    return one(a[0], b[0]) + (one(a[0], b[1]) + one(a[1], b[0]))


NT = ((1,), (1,))
NN = ((1,), (0,))


def schur_kernel(
    where_ref, rows_ref, top_ref, moved_ref, front_ref, low_ref, inv_ref, out_ref,
    lh, ll, yh, yl, uh, ul, x_ref,
):
    tile = pl.program_id(0)
    row, col, sub = where_ref[0], where_ref[1], where_ref[2]

    @pl.when(tile == 0)
    def _():
        high, rest = split(low_ref[...])
        lh[...] = high
        ll[...] = rest
        zero = jnp.zeros((BLK, BLK), jnp.float32)
        for p in range(3):
            first, second = inv_ref[2 * p], inv_ref[2 * p + 1]
            at = 256 * p
            cross = jnp.dot(low_ref[at + BLK : at + 256, at : at + BLK], first, precision=HI)
            cross = -jnp.dot(second, cross, precision=HI)
            pair = jnp.concatenate(
                [jnp.concatenate([first, zero], axis=1), jnp.concatenate([cross, second], axis=1)], axis=0
            )
            high, rest = split(pair)
            yh[p] = high
            yl[p] = rest
        for p in range(3):
            at = 256 * p
            x = four(top_ref[2 * p, 0], top_ref[2 * p, 1], top_ref[2 * p + 1, 0], top_ref[2 * p + 1, 1])
            if p:
                x = x - dot3((lh[at : at + 256, :at], ll[at : at + 256, :at]), (uh[:at, :], ul[:at, :]), NN)
            high, rest = split(dot3((yh[p], yl[p]), split(x), NN))
            uh[at : at + 256, :] = high
            ul[at : at + 256, :] = rest

    acc = front_ref[...] + four(moved_ref[0, 0], moved_ref[0, 1], moved_ref[1, 0], moved_ref[1, 1])
    xs = []
    for p in range(3):
        at = 256 * p
        x = four(rows_ref[0, 2 * p], rows_ref[0, 2 * p + 1], rows_ref[1, 2 * p], rows_ref[1, 2 * p + 1])
        for m in range(p):
            cut = slice(256 * m, 256 * m + 256)
            x = x - dot3(xs[m], (lh[at : at + 256, cut], ll[at : at + 256, cut]), NT)
        x = dot3(split(x), (yh[p], yl[p]), NT)
        x_ref[:, at : at + 256] = x
        xs.append(split(x))
        acc = acc - dot3(xs[p], (uh[at : at + 256, :], ul[at : at + 256, :]), NN)
    out_ref[...] = acc

    @pl.when((tile == 0) & (row < NPIV))
    def _():
        out_ref[:BLK, :] = jnp.zeros((BLK, 256), jnp.float32)
        x_ref[:BLK, :] = low_ref[pl.ds(pl.multiple_of(row * BLK, BLK), BLK), :]

    @pl.when((sub == 0) & (col < NPIV))
    def _():
        out_ref[:, :BLK] = x_ref[:, pl.ds(pl.multiple_of(col * BLK, BLK), BLK)]


def four(a, b, c, d):
    return jnp.concatenate([jnp.concatenate([a, b], axis=1), jnp.concatenate([c, d], axis=1)], axis=0)


def schur(where, rows, top, moved, front, low, inv):
    whole = lambda *shape: pl.BlockSpec(shape, lambda t: (0,) * len(shape), pipeline_mode=pl.Buffered(1))
    return pl.pallas_call(
        schur_kernel,
        out_shape=jax.ShapeDtypeStruct((1024, 256), jnp.float32),
        grid=(4,),
        in_specs=[
            SM,
            pl.BlockSpec((2, NPIV, BLK, BLK), lambda t: (t, 0, 0, 0)),
            whole(NPIV, 2, BLK, BLK),
            pl.BlockSpec((2, 2, BLK, BLK), lambda t: (t, 0, 0, 0)),
            pl.BlockSpec((256, 256), lambda t: (t, 0)),
            whole(PIV, PIV),
            whole(NPIV, BLK, BLK),
        ],
        out_specs=pl.BlockSpec((256, 256), lambda t: (t, 0)),
        scratch_shapes=[
            pltpu.VMEM((PIV, PIV), jnp.bfloat16),
            pltpu.VMEM((PIV, PIV), jnp.bfloat16),
            pltpu.VMEM((3, 256, 256), jnp.bfloat16),
            pltpu.VMEM((3, 256, 256), jnp.bfloat16),
            pltpu.VMEM((PIV, 256), jnp.bfloat16),
            pltpu.VMEM((PIV, 256), jnp.bfloat16),
            pltpu.VMEM((256, PIV), jnp.float32),
        ],
        name="schur",
    )(where, rows, top, moved, front, low, inv)


def body(front, child, child_map):
    where = jnp.stack([lax.axis_index(a) for a in ("row", "col", "sub")]).astype(jnp.int32)
    wide = jnp.broadcast_to(child_map[0].astype(jnp.float32)[:, None], (16, BLK))
    shares = child[0].reshape(2, BLK, 2, BLK).transpose(0, 2, 1, 3).reshape(2, 2, 32, 4, BLK)
    k, maps, buf, panel = gather_all(shares, front[:, :BLK].reshape(8, 32, 4, BLK), wide)
    acc = place(maps[:, :, 0].astype(jnp.int32), where, buf)
    first = front[:BLK].reshape(BLK, 2, BLK).transpose(1, 0, 2).reshape(2, 32, 4, BLK)
    low, inv, rows, moved, top = factor_all(k.reshape(NTILE, BLK, BLK), acc, panel, first)
    return schur(
        where,
        rows.reshape(8, NPIV, BLK, BLK),
        top.reshape(NPIV, 2, BLK, BLK),
        moved.reshape(8, 2, BLK, BLK),
        front,
        low,
        inv,
    )


def solution(mesh):
    placed = (P("row", ("col", "sub")), P("sub", "row", "col"), P("sub", None))
    return jax.shard_map(
        body, mesh=mesh, in_specs=placed, out_specs=P("row", ("col", "sub")), check_vma=False
    )
```

```python
import jax
import jax.numpy as jnp
from jax import lax
from jax.experimental import pallas as pl
from jax.experimental.pallas import tpu as pltpu
from jax.sharding import PartitionSpec as P

BLK = 128
NPIV = 6
PIV = NPIV * BLK
PLANE = ("col", "sub")
HI = lax.Precision.HIGHEST
VM = pl.BlockSpec(memory_space=pltpu.VMEM)
SM = pl.BlockSpec(memory_space=pltpu.SMEM)


def nt(a, b, precision=HI):
    return lax.dot_general(a, b, (((1,), (1,)), ((), ())), precision=precision, preferred_element_type=jnp.float32)
def tn(a, b, precision=HI):
    return lax.dot_general(a, b, (((0,), (0,)), ((), ())), precision=precision, preferred_element_type=jnp.float32)

def split(x):
    high = x.astype(jnp.bfloat16)
    return high, (x - high.astype(jnp.float32)).astype(jnp.bfloat16)


def dot3(a, b, dims):
    def one(x, y):
        return lax.dot_general(x, y, (dims, ((), ())), preferred_element_type=jnp.float32)

    return one(a[0], b[0]) + (one(a[0], b[1]) + one(a[1], b[0]))


def tn3(a, b):
    return dot3(split(a), split(b), ((0,), (0,)))


def nt3(a, b):
    return dot3(split(a), split(b), ((1,), (1,)))


def rsqrt(x):
    return lax.rsqrt(x)

def wide(x):
    return jnp.concatenate([x, x], axis=1)

def eliminate(a_ref):
    sub = lax.broadcasted_iota(jnp.int32, (8, 256), 0)
    ahead = []
    for g in range(16):
        if g == 0:
            ahead = [a_ref[8 * h : 8 * h + 8, :] for h in range(2 + 1)]
        elif g + 2 < 16:
            ahead.append(a_ref[8 * (g + 2) : 8 * (g + 2) + 8, :])
        rows = ahead.pop(0)
        left = rows[:, :BLK]
        e = {}
        for j in range(8):
            c = jnp.broadcast_to(left[:, 8 * g + j : 8 * g + j + 1], (8, BLK))
            for i in range(j, 8):
                e[j, i] = jnp.broadcast_to(c[i : i + 1, :], (8, BLK))
        r = [jnp.broadcast_to(rows[i : i + 1, :], (8, 256)) for i in range(8)]
        cols = [[jnp.broadcast_to(n[:, 8 * g + j : 8 * g + j + 1], (8, BLK)) for j in range(8)] for n in ahead]
        out = None
        for j in range(8):
            s = rsqrt(e[j, j])
            u = {i: e[j, i] * s for i in range(j + 1, 8)}
            for i in range(j + 1, 8):
                for m in range(i, 8):
                    e[i, m] = e[i, m] - u[i] * u[m]
            rj = r[j] * wide(s)
            for i in range(j + 1, 8):
                r[i] = r[i] - wide(u[i]) * rj
            for h in range(len(ahead)):
                cj = cols[h][j] * s
                for m in range(j + 1, 8):
                    cols[h][m] = cols[h][m] - cj * u[m]
                ahead[h] = ahead[h] - wide(cj) * rj
            out = rj if out is None else jnp.where(sub == j, rj, out)
        a_ref[8 * g : 8 * g + 8, :] = out
        low = 8 * (g + 1 + 2)
        if low < BLK:
            t = tn3(out[:, :BLK], out)
            a_ref[low:, :] = a_ref[low:, :] - t[low:, :]

def factor_steps(k_ref, l_ref, y_ref, a_ref, m_ref, progress):
    r_iota = lax.broadcasted_iota(jnp.int32, (BLK, BLK), 0)
    c_iota = lax.broadcasted_iota(jnp.int32, (BLK, BLK), 1)
    for i in range(NPIV):
        for j in range(i + 1):
            m_ref[i * BLK : (i + 1) * BLK, j * BLK : (j + 1) * BLK] = k_ref[i * (i + 1) // 2 + j]
        if i < NPIV - 1:
            m_ref[i * BLK : (i + 1) * BLK, (i + 1) * BLK :] = jnp.zeros((BLK, PIV - (i + 1) * BLK), jnp.float32)
    l_ref[...] = jnp.zeros_like(l_ref)

    def step(b, carry):
        progress(b)
        at = pl.ds(pl.multiple_of(b * BLK, BLK), BLK)
        a_ref[:, :BLK] = m_ref[at, at]
        a_ref[:, BLK:] = jnp.where(r_iota == c_iota, 1.0, 0.0)
        eliminate(a_ref)
        y = a_ref[:, BLK:]
        y_ref[b] = y
        l_ref[at, at] = jnp.where(r_iota >= c_iota, a_ref[:, :BLK].T, 0.0)

        def solve(i, c):
            rows = pl.ds(pl.multiple_of(i * BLK, BLK), BLK)
            l_ref[rows, at] = nt(m_ref[rows, at], y)
            return c

        lax.fori_loop(b + 1, NPIV, solve, 0)

        def update(i, c):
            rows = pl.ds(pl.multiple_of(i * BLK, BLK), BLK)
            m_ref[rows, :] = m_ref[rows, :] - nt3(l_ref[rows, at], l_ref[:, at])
            return c

        lax.fori_loop(b + 1, NPIV, update, 0)
        return carry

    lax.fori_loop(0, NPIV, step, 0)


MESH = pl.DeviceIdType.MESH
TILES = [(i, j) for i in range(NPIV) for j in range(i + 1)]
NTILE = len(TILES)


class Place:
    def __init__(self):
        self.r, self.c, self.s = (lax.axis_index(a) for a in ("row", "col", "sub"))
        self.e = self.c * 4 + self.s
        self.core = self.c % 2
        self.chip = (self.c // 2) * 4 + self.s
        self.partner = (self.r, self.c + 1 - 2 * self.core, self.s)

    def plane(self, d):
        p = (self.e + d) % 32
        return p, (self.r, p // 4, p % 4)

    def same_core(self, d):
        p = (self.chip + d) % 16
        c = (p // 4) * 2 + self.core
        return c * 4 + p % 4, (self.r, c, p % 4)

    def line(self, d):
        return ((self.r + d) % 8, self.c, self.s)

    def greet(self):
        barrier = pltpu.get_barrier_semaphore()

        def plane(d, carry):
            pl.semaphore_signal(barrier, inc=1, device_id=self.plane(d)[1], device_id_type=MESH)
            return carry

        def line(d, carry):
            pl.semaphore_signal(barrier, inc=1, device_id=self.line(d), device_id_type=MESH)
            return carry

        lax.fori_loop(1, 32, plane, 0)
        lax.fori_loop(1, 8, line, 0)
        pl.semaphore_wait(barrier, 38)


def push(src, dst, ssem, rsem, device):
    return pltpu.make_async_remote_copy(
        src_ref=src, dst_ref=dst, send_sem=ssem, recv_sem=rsem, device_id=device, device_id_type=MESH
    )


def arrive(ref, sem):
    pltpu.make_async_copy(ref, ref, sem).wait()


def loop(low, high, f):
    def one(d, carry):
        f(d)
        return carry

    lax.fori_loop(low, high, one, 0)


def gather_kernel(
    child_ref, front_ref, map_ref, k_ref, maps_ref, buf_ref, panel_ref,
    z_ref, acc_ref, send, got, z_got, f_got, k_got, p_got, right_got, left_got,
):
    at = Place()
    r, c, s, e = at.r, at.c, at.s, at.e
    at.greet()
    pivot_row = r < NPIV
    has_front = (c < NPIV) & (s == 0)
    spot = jnp.minimum(r, NPIV - 1)
    seat = jnp.minimum(c, NPIV - 1)

    def child_copy(d):
        p, device = at.plane(d)
        return push(child_ref.at[:, :, p], buf_ref.at[r, e], send.at[0], got.at[0], device)

    def front_copy(d):
        p, device = at.plane(d)
        return push(front_ref.at[:, p], panel_ref.at[seat], send.at[1], got.at[1], device)

    def map_copy(d):
        return push(map_ref, maps_ref.at[s], send.at[2], got.at[2], (r, c, (s + d) % 4))

    pltpu.make_async_copy(child_ref.at[:, :, e], buf_ref.at[r, e], got.at[0]).start()
    pltpu.make_async_copy(map_ref, maps_ref.at[s], got.at[2]).start()
    loop(1, 32, lambda d: child_copy(d).start())

    @pl.when(has_front)
    def _():
        pltpu.make_async_copy(front_ref.at[:, e], panel_ref.at[seat], got.at[1]).start()
        loop(1, 32, lambda d: front_copy(d).start())

    for d in range(1, 4):
        map_copy(d).start()

    def z_copy(d):
        return push(buf_ref.at[spot, pl.ds(0, 24), 0, 0], z_ref.at[spot, pl.ds(0, 24)], send.at[3], z_got.at[spot], at.line(d))

    def f_copy(d):
        return push(panel_ref.at[:, 0], z_ref.at[spot, pl.ds(24, 6)], send.at[4], f_got.at[spot], at.line(d))

    def right_copy(k):
        block = (r + 8 - k) % 8
        return push(buf_ref.at[block], buf_ref.at[block], send.at[5], right_got.at[k], at.line(1))

    def left_copy(k):
        block = (r + k) % 8
        return push(buf_ref.at[block], buf_ref.at[block], send.at[6], left_got.at[k], at.line(7))

    def right_wait(k):
        arrive(buf_ref.at[(r + 7 - k) % 8], right_got.at[k])

    def left_wait(k):
        arrive(buf_ref.at[(r + 1 + k) % 8], left_got.at[k])

    arrive(buf_ref.at[r], got.at[0])
    arrive(panel_ref, got.at[1])

    @pl.when(pivot_row)
    def _():
        pltpu.make_async_copy(buf_ref.at[spot, pl.ds(0, 24), 0, 0], z_ref.at[spot, pl.ds(0, 24)], z_got.at[spot]).start()
        pltpu.make_async_copy(panel_ref.at[:, 0], z_ref.at[spot, pl.ds(24, 6)], f_got.at[spot]).start()
        for d in (4, 3, 5, 2, 6, 1, 7):
            z_copy(d).start()
            f_copy(d).start()

    right_copy(0).start()
    left_copy(0).start()
    arrive(maps_ref, got.at[2])
    for i in range(NPIV):
        arrive(z_ref.at[i, pl.ds(0, 24)], z_got.at[i])
        arrive(z_ref.at[i, pl.ds(24, 6)], f_got.at[i])

    for t, (i, j) in enumerate(TILES):
        acc_ref[t] = z_ref[i, 24 + j]

    def add_child(q):
        wanted = maps_ref[q][:NPIV]
        strips = []
        for j in range(NPIV):
            strip = None
            for seat_j in range(j + 1):
                pick = jnp.where(wanted[seat_j : seat_j + 1] == float(j), 1.0, 0.0)[None]
                term = z_ref[:, seat_j * 4 + q] * pick
                strip = term if strip is None else strip + term
            strips.append(strip)
        for j in range(NPIV):
            for i in range(j, NPIV):
                pick = jnp.where(wanted == float(i), 1.0, 0.0)[:, None, :]
                acc_ref[i * (i + 1) // 2 + j] += jnp.sum(strips[j] * pick, axis=0)

    loop(0, 4, add_child)

    own_k = pltpu.make_async_copy(acc_ref, k_ref.at[:, e], got.at[3])
    own_k.start()

    def k_copy(d):
        return push(acc_ref, k_ref.at[:, e], send.at[7], k_got.at[d], at.same_core(d)[1])

    def pair_copy(d):
        where_e = at.same_core(16 - d)[0]
        return push(k_ref.at[:, where_e], k_ref.at[:, where_e], send.at[8], p_got.at[d], at.partner)

    def forward(d):
        k_copy(d).wait_recv()
        pair_copy(d).start()

    loop(1, 16, lambda d: k_copy(d).start())
    right_wait(0)
    right_copy(1).start()
    left_wait(0)
    left_copy(1).start()
    own_k.wait()
    pair_copy(0).start()
    right_wait(1)
    right_copy(2).start()
    left_wait(1)
    left_copy(2).start()
    loop(1, 16, forward)
    right_wait(2)
    right_copy(3).start()
    left_wait(2)
    loop(0, 16, lambda d: pair_copy(d).wait())
    right_wait(3)

    loop(1, 16, lambda d: k_copy(d).wait_send())
    loop(1, 32, lambda d: child_copy(d).wait_send())

    @pl.when(has_front)
    def _():
        loop(1, 32, lambda d: front_copy(d).wait_send())

    for d in range(1, 4):
        map_copy(d).wait_send()

    @pl.when(pivot_row)
    def _():
        for d in range(1, 8):
            z_copy(d).wait_send()
            f_copy(d).wait_send()

    for k in range(4):
        right_copy(k).wait_send()
    for k in range(3):
        left_copy(k).wait_send()


def gather_all(child, front, child_map):
    dma = pltpu.SemaphoreType.DMA
    return pl.pallas_call(
        gather_kernel,
        out_shape=(
            jax.ShapeDtypeStruct((NTILE, 32, 4, BLK), jnp.float32),
            jax.ShapeDtypeStruct((4, 16, BLK), jnp.float32),
            jax.ShapeDtypeStruct((8, 32, 2, 2, 4, BLK), jnp.float32),
            jax.ShapeDtypeStruct((NPIV, 8, 4, BLK), jnp.float32),
        ),
        in_specs=[VM] * 3,
        out_specs=(VM,) * 4,
        scratch_shapes=[
            pltpu.VMEM((NPIV, 30, 4, BLK), jnp.float32),
            pltpu.VMEM((NTILE, 4, BLK), jnp.float32),
            dma((9,)), dma((4,)), dma((NPIV,)), dma((NPIV,)), dma((16,)), dma((16,)), dma((4,)), dma((3,)),
        ],
        compiler_params=pltpu.CompilerParams(collective_id=0, has_side_effects=True),
        name="gather_all",
    )(child, front, child_map)


def factor_kernel(
    k_ref, acc_ref, panel_ref, front_ref, low_ref, inv_ref, rows_ref, moved_ref, top_ref,
    a_ref, m_ref, share_ref, w_ref, send, got, r_got, p_got, t_got,
):
    at = Place()
    r, c, s, e = at.r, at.c, at.s, at.e
    at.greet()
    spot = jnp.minimum(r, NPIV - 1)

    def move_copy(d):
        p, device = at.plane(d)
        return push(acc_ref.at[p], moved_ref.at[:, :, e], send.at[0], got.at[0], device)

    pltpu.make_async_copy(acc_ref.at[e], moved_ref.at[:, :, e], got.at[0]).start()
    loop(1, 32, lambda d: move_copy(d).start())

    for j in range(NPIV):
        for slot in range(8):
            share_ref[slot, j] = acc_ref[j * 4, slot, 0] + panel_ref[j, slot]

    own_rows = pltpu.make_async_copy(share_ref, rows_ref.at[:, :, e], got.at[1])

    def rows_copy(d):
        return push(share_ref, rows_ref.at[:, :, e], send.at[1], r_got.at[d], at.same_core(d)[1])

    def pair_copy(d):
        where_e = at.same_core(16 - d)[0]
        return push(rows_ref.at[:, :, where_e], rows_ref.at[:, :, where_e], send.at[2], p_got.at[d], at.partner)

    def top_copy(d):
        return push(w_ref, top_ref.at[spot], send.at[3], t_got.at[spot], at.line(d))

    own_rows.start()
    loop(1, 16, lambda d: rows_copy(d).start())

    def after_first():
        own_rows.wait()
        pair_copy(0).start()
        arrive(moved_ref, got.at[0])

        @pl.when(r < NPIV)
        def _():
            w_ref[...] = moved_ref[0] + front_ref[...]
            pltpu.make_async_copy(w_ref, top_ref.at[spot], t_got.at[spot]).start()
            for d in (4, 3, 5, 2, 6, 1, 7):
                top_copy(d).start()

    def forward(d):
        rows_copy(d).wait_recv()
        pair_copy(d).start()

    def progress(b):
        pl.when(b == 1)(after_first)
        pl.when(b == 3)(lambda: loop(1, 16, forward))

    factor_steps(k_ref, low_ref, inv_ref, a_ref, m_ref, progress)

    loop(0, 16, lambda d: pair_copy(d).wait())
    for i in range(NPIV):
        arrive(top_ref.at[i], t_got.at[i])
    loop(1, 16, lambda d: rows_copy(d).wait_send())
    loop(1, 32, lambda d: move_copy(d).wait_send())

    @pl.when(r < NPIV)
    def _():
        for d in range(1, 8):
            top_copy(d).wait_send()


def factor_all(k, acc, panel, front):
    dma = pltpu.SemaphoreType.DMA
    f32 = lambda *shape: jax.ShapeDtypeStruct(shape, jnp.float32)
    return pl.pallas_call(
        factor_kernel,
        out_shape=(
            f32(PIV, PIV),
            f32(NPIV, BLK, BLK),
            f32(8, NPIV, 32, 4, BLK),
            f32(8, 2, 32, 4, BLK),
            f32(NPIV, 2, 32, 4, BLK),
        ),
        in_specs=[VM] * 4,
        out_specs=(VM,) * 5,
        scratch_shapes=[
            pltpu.VMEM((BLK, 256), jnp.float32),
            pltpu.VMEM((PIV, PIV), jnp.float32),
            pltpu.VMEM((8, NPIV, 4, BLK), jnp.float32),
            pltpu.VMEM((2, 32, 4, BLK), jnp.float32),
            dma((4,)), dma((2,)), dma((16,)), dma((16,)), dma((NPIV,)),
        ],
        compiler_params=pltpu.CompilerParams(collective_id=1, has_side_effects=True, vmem_limit_bytes=40 * 1024 * 1024),
        name="factor_all",
    )(k, acc, panel, front)


def place_kernel(map_ref, where_ref, buf_ref, acc_ref):
    acc_ref[...] = jnp.zeros_like(acc_ref)
    row = where_ref[0]

    def child_row(step):
        q = step // 16
        block_row = step % 16
        i = map_ref[q, block_row]

        @pl.when(i % 8 == row)
        def _():
            slot = i // 8
            for block_col in range(16):
                j = map_ref[q, block_col]
                tile = buf_ref[block_row % 8, block_col % 8 * 4 + q, block_row // 8, block_col // 8]
                acc_ref[j % 8 * 4 + j // 16, slot, (j // 8) % 2] += tile

    loop(0, 64, child_row)


def place(maps, where, buf):
    return pl.pallas_call(
        place_kernel,
        out_shape=jax.ShapeDtypeStruct((32, 8, 2, 4, BLK), jnp.float32),
        in_specs=[SM, SM, VM],
        out_specs=VM,
        name="place",
    )(maps, where, buf)


NT = ((1,), (1,))
NN = ((1,), (0,))


def four(a, b, c, d):
    return jnp.concatenate([jnp.concatenate([a, b], axis=1), jnp.concatenate([c, d], axis=1)], axis=0)


def schur_kernel(
    where_ref, rows_ref, top_ref, moved_ref, front_ref, low_ref, inv_ref, out_ref,
    lh, ll, yh, yl, uh, ul, x_ref,
):
    row, col, sub = where_ref[0], where_ref[1], where_ref[2]
    high, rest = split(low_ref[...])
    lh[...] = high
    ll[...] = rest
    zero = jnp.zeros((BLK, BLK), jnp.float32)
    for p in range(3):
        first, second = inv_ref[2 * p], inv_ref[2 * p + 1]
        at = 256 * p
        cross = jnp.dot(low_ref[at + BLK : at + 256, at : at + BLK], first, precision=HI)
        cross = -jnp.dot(second, cross, precision=HI)
        high, rest = split(four(first, zero, cross, second))
        yh[p] = high
        yl[p] = rest
    for p in range(3):
        at = 256 * p
        x = four(top_ref[2 * p, 0], top_ref[2 * p, 1], top_ref[2 * p + 1, 0], top_ref[2 * p + 1, 1])
        if p:
            x = x - dot3((lh[at : at + 256, :at], ll[at : at + 256, :at]), (uh[:at, :], ul[:at, :]), NN)
        high, rest = split(dot3((yh[p], yl[p]), split(x), NN))
        uh[at : at + 256, :] = high
        ul[at : at + 256, :] = rest

    def tile(t):
        here = pl.ds(pl.multiple_of(t * 256, 256), 256)
        a, b = 2 * t, 2 * t + 1
        acc = front_ref[here, :] + four(moved_ref[a, 0], moved_ref[a, 1], moved_ref[b, 0], moved_ref[b, 1])
        xs = []
        for p in range(3):
            at = 256 * p
            x = four(rows_ref[a, 2 * p], rows_ref[a, 2 * p + 1], rows_ref[b, 2 * p], rows_ref[b, 2 * p + 1])
            for m in range(p):
                cut = slice(256 * m, 256 * m + 256)
                x = x - dot3(xs[m], (lh[at : at + 256, cut], ll[at : at + 256, cut]), NT)
            x = dot3(split(x), (yh[p], yl[p]), NT)
            x_ref[here, at : at + 256] = x
            xs.append(split(x))
            acc = acc - dot3(xs[p], (uh[at : at + 256, :], ul[at : at + 256, :]), NN)
        out_ref[here, :] = acc

    loop(0, 4, tile)

    @pl.when(row < NPIV)
    def _():
        out_ref[:BLK, :] = jnp.zeros((BLK, 256), jnp.float32)
        x_ref[:BLK, :] = low_ref[pl.ds(pl.multiple_of(row * BLK, BLK), BLK), :]

    @pl.when((sub == 0) & (col < NPIV))
    def _():
        out_ref[:, :BLK] = x_ref[:, pl.ds(pl.multiple_of(col * BLK, BLK), BLK)]


def schur(where, rows, top, moved, front, low, inv):
    return pl.pallas_call(
        schur_kernel,
        out_shape=jax.ShapeDtypeStruct((1024, 256), jnp.float32),
        in_specs=[SM] + [VM] * 6,
        out_specs=VM,
        scratch_shapes=[
            pltpu.VMEM((PIV, PIV), jnp.bfloat16),
            pltpu.VMEM((PIV, PIV), jnp.bfloat16),
            pltpu.VMEM((3, 256, 256), jnp.bfloat16),
            pltpu.VMEM((3, 256, 256), jnp.bfloat16),
            pltpu.VMEM((PIV, 256), jnp.bfloat16),
            pltpu.VMEM((PIV, 256), jnp.bfloat16),
            pltpu.VMEM((1024, PIV), jnp.float32),
        ],
        compiler_params=pltpu.CompilerParams(vmem_limit_bytes=32 * 1024 * 1024),
        name="schur",
    )(where, rows, top, moved, front, low, inv)


def body(front, child, child_map):
    where = jnp.stack([lax.axis_index(a) for a in ("row", "col", "sub")]).astype(jnp.int32)
    wide = jnp.broadcast_to(child_map[0].astype(jnp.float32)[:, None], (16, BLK))
    shares = child[0].reshape(2, BLK, 2, BLK).transpose(0, 2, 1, 3).reshape(2, 2, 32, 4, BLK)
    k, maps, buf, panel = gather_all(shares, front[:, :BLK].reshape(8, 32, 4, BLK), wide)
    acc = place(maps[:, :, 0].astype(jnp.int32), where, buf)
    first = front[:BLK].reshape(BLK, 2, BLK).transpose(1, 0, 2).reshape(2, 32, 4, BLK)
    low, inv, rows, moved, top = factor_all(k.reshape(NTILE, BLK, BLK), acc, panel, first)
    return schur(
        where,
        rows.reshape(8, NPIV, BLK, BLK),
        top.reshape(NPIV, 2, BLK, BLK),
        moved.reshape(8, 2, BLK, BLK),
        front,
        low,
        inv,
    )


def solution(mesh):
    placed = (P("row", ("col", "sub")), P("sub", "row", "col"), P("sub", None))
    return jax.shard_map(
        body, mesh=mesh, in_specs=placed, out_specs=P("row", ("col", "sub")), check_vma=False
    )
```

```python
import jax
import jax.numpy as jnp
from jax import lax
from jax.experimental import pallas as pl
from jax.experimental.pallas import tpu as pltpu
from jax.sharding import PartitionSpec as P

BLK = 128
NPIV = 6
PIV = NPIV * BLK
PLANE = ("col", "sub")
HI = lax.Precision.HIGHEST
VM = pl.BlockSpec(memory_space=pltpu.VMEM)
SM = pl.BlockSpec(memory_space=pltpu.SMEM)


def nt(a, b, precision=HI):
    return lax.dot_general(a, b, (((1,), (1,)), ((), ())), precision=precision, preferred_element_type=jnp.float32)
def tn(a, b, precision=HI):
    return lax.dot_general(a, b, (((0,), (0,)), ((), ())), precision=precision, preferred_element_type=jnp.float32)

def split(x):
    high = x.astype(jnp.bfloat16)
    return high, (x - high.astype(jnp.float32)).astype(jnp.bfloat16)


def dot3(a, b, dims):
    def one(x, y):
        return lax.dot_general(x, y, (dims, ((), ())), preferred_element_type=jnp.float32)

    return one(a[0], b[0]) + (one(a[0], b[1]) + one(a[1], b[0]))


def tn3(a, b):
    return dot3(split(a), split(b), ((0,), (0,)))


def nt3(a, b):
    return dot3(split(a), split(b), ((1,), (1,)))


def rsqrt(x):
    return lax.rsqrt(x)

def wide(x):
    return jnp.concatenate([x, x], axis=1)

def eliminate(a_ref):
    sub = lax.broadcasted_iota(jnp.int32, (8, 256), 0)
    ahead = []
    for g in range(16):
        if g == 0:
            ahead = [a_ref[8 * h : 8 * h + 8, :] for h in range(2 + 1)]
        elif g + 2 < 16:
            ahead.append(a_ref[8 * (g + 2) : 8 * (g + 2) + 8, :])
        rows = ahead.pop(0)
        left = rows[:, :BLK]
        e = {}
        for j in range(8):
            c = jnp.broadcast_to(left[:, 8 * g + j : 8 * g + j + 1], (8, BLK))
            for i in range(j, 8):
                e[j, i] = jnp.broadcast_to(c[i : i + 1, :], (8, BLK))
        r = [jnp.broadcast_to(rows[i : i + 1, :], (8, 256)) for i in range(8)]
        cols = [[jnp.broadcast_to(n[:, 8 * g + j : 8 * g + j + 1], (8, BLK)) for j in range(8)] for n in ahead]
        out = None
        for j in range(8):
            s = rsqrt(e[j, j])
            u = {i: e[j, i] * s for i in range(j + 1, 8)}
            for i in range(j + 1, 8):
                for m in range(i, 8):
                    e[i, m] = e[i, m] - u[i] * u[m]
            rj = r[j] * wide(s)
            for i in range(j + 1, 8):
                r[i] = r[i] - wide(u[i]) * rj
            for h in range(len(ahead)):
                cj = cols[h][j] * s
                for m in range(j + 1, 8):
                    cols[h][m] = cols[h][m] - cj * u[m]
                ahead[h] = ahead[h] - wide(cj) * rj
            out = rj if out is None else jnp.where(sub == j, rj, out)
        a_ref[8 * g : 8 * g + 8, :] = out
        low = 8 * (g + 1 + 2)
        if low < BLK:
            t = tn3(out[:, :BLK], out)
            a_ref[low:, :] = a_ref[low:, :] - t[low:, :]

def factor_steps(k_ref, l_ref, y_ref, a_ref, m_ref, progress):
    r_iota = lax.broadcasted_iota(jnp.int32, (BLK, BLK), 0)
    c_iota = lax.broadcasted_iota(jnp.int32, (BLK, BLK), 1)
    for i in range(NPIV):
        for j in range(i + 1):
            m_ref[i * BLK : (i + 1) * BLK, j * BLK : (j + 1) * BLK] = k_ref[i * (i + 1) // 2 + j]
        if i < NPIV - 1:
            m_ref[i * BLK : (i + 1) * BLK, (i + 1) * BLK :] = jnp.zeros((BLK, PIV - (i + 1) * BLK), jnp.float32)
    l_ref[...] = jnp.zeros_like(l_ref)

    def step(b, carry):
        progress(b)
        at = pl.ds(pl.multiple_of(b * BLK, BLK), BLK)
        a_ref[:, :BLK] = m_ref[at, at]
        a_ref[:, BLK:] = jnp.where(r_iota == c_iota, 1.0, 0.0)
        eliminate(a_ref)
        y = a_ref[:, BLK:]
        y_ref[b] = y
        l_ref[at, at] = jnp.where(r_iota >= c_iota, a_ref[:, :BLK].T, 0.0)

        def solve(i, c):
            rows = pl.ds(pl.multiple_of(i * BLK, BLK), BLK)
            l_ref[rows, at] = nt(m_ref[rows, at], y)
            return c

        lax.fori_loop(b + 1, NPIV, solve, 0)

        def update(i, c):
            rows = pl.ds(pl.multiple_of(i * BLK, BLK), BLK)
            m_ref[rows, :] = m_ref[rows, :] - nt3(l_ref[rows, at], l_ref[:, at])
            return c

        lax.fori_loop(b + 1, NPIV, update, 0)
        return carry

    lax.fori_loop(0, NPIV, step, 0)


MESH = pl.DeviceIdType.MESH
TILES = [(i, j) for i in range(NPIV) for j in range(i + 1)]
NTILE = len(TILES)


class Place:
    def __init__(self):
        self.r, self.c, self.s = (lax.axis_index(a) for a in ("row", "col", "sub"))
        self.e = self.c * 4 + self.s
        self.core = self.c % 2
        self.chip = (self.c // 2) * 4 + self.s
        self.partner = (self.r, self.c + 1 - 2 * self.core, self.s)

    def plane(self, d):
        p = (self.e + d) % 32
        return p, (self.r, p // 4, p % 4)

    def same_core(self, d):
        p = (self.chip + d) % 16
        c = (p // 4) * 2 + self.core
        return c * 4 + p % 4, (self.r, c, p % 4)

    def line(self, d):
        return ((self.r + d) % 8, self.c, self.s)

    def greet(self):
        barrier = pltpu.get_barrier_semaphore()

        def plane(d, carry):
            pl.semaphore_signal(barrier, inc=1, device_id=self.plane(d)[1], device_id_type=MESH)
            return carry

        def line(d, carry):
            pl.semaphore_signal(barrier, inc=1, device_id=self.line(d), device_id_type=MESH)
            return carry

        lax.fori_loop(1, 32, plane, 0)
        lax.fori_loop(1, 8, line, 0)
        pl.semaphore_wait(barrier, 38)


def push(src, dst, ssem, rsem, device):
    return pltpu.make_async_remote_copy(
        src_ref=src, dst_ref=dst, send_sem=ssem, recv_sem=rsem, device_id=device, device_id_type=MESH
    )


def arrive(ref, sem):
    pltpu.make_async_copy(ref, ref, sem).wait()


def loop(low, high, f):
    def one(d, carry):
        f(d)
        return carry

    lax.fori_loop(low, high, one, 0)


def gather_kernel(
    child_ref, front_ref, map_ref, k_ref, maps_ref, buf_ref, panel_ref,
    z_ref, acc_ref, send, got, z_got, f_got, k_got, p_got, ring_got,
):
    at = Place()
    r, c, s, e = at.r, at.c, at.s, at.e
    at.greet()
    has_front = (c < NPIV) & (s == 0)
    seat = jnp.minimum(c, NPIV - 1)

    def child_copy(d):
        p, device = at.plane(d)
        return push(child_ref.at[:, :, p], buf_ref.at[r, e], send.at[0], got.at[0], device)

    def front_copy(d):
        p, device = at.plane(d)
        return push(front_ref.at[0, p], panel_ref.at[seat, 0], send.at[1], got.at[1], device)

    def rest_copy(d):
        p, device = at.plane(d)
        return push(front_ref.at[pl.ds(1, 7), p], panel_ref.at[seat, pl.ds(1, 7)], send.at[4], got.at[4], device)

    def map_copy(d):
        return push(map_ref, maps_ref.at[s], send.at[2], got.at[2], (r, c, (s + d) % 4))

    pltpu.make_async_copy(child_ref.at[:, :, e], buf_ref.at[r, e], got.at[0]).start()
    pltpu.make_async_copy(map_ref, maps_ref.at[s], got.at[2]).start()
    loop(1, 32, lambda d: child_copy(d).start())

    @pl.when(has_front)
    def _():
        pltpu.make_async_copy(front_ref.at[0, e], panel_ref.at[seat, 0], got.at[1]).start()
        loop(1, 32, lambda d: front_copy(d).start())

    for d in range(1, 4):
        map_copy(d).start()

    def z_copies(i, d):
        device = at.line(d)
        tiles, own = pl.ds(0, 4 * (i + 1)), pl.ds(0, i + 1)
        return (
            push(buf_ref.at[i, tiles, 0, 0], z_ref.at[i, tiles], send.at[3], z_got.at[i], device),
            push(panel_ref.at[own, 0], z_ref.at[i, pl.ds(24, i + 1)], send.at[3], f_got.at[i], device),
        )

    def ring_copy(way, k, h):
        block = (r + 8 - k) % 8 if way == 0 else (r + k) % 8
        half = buf_ref.at[block, :, h]
        return push(half, half, send.at[5 + way], ring_got.at[way, 2 * k + h], at.line(1 if way == 0 else 7))

    def ring_wait(way, k, h):
        block = (r + 7 - k) % 8 if way == 0 else (r + 1 + k) % 8
        arrive(buf_ref.at[block, :, h], ring_got.at[way, 2 * k + h])

    hops = [(way, k, h) for k in range(4) for h in range(2) for way in range(2) if k < 3 or h == way]

    def ring_step(k):
        for hop in hops:
            if hop[1] == k:
                if k:
                    ring_wait(hop[0], k - 1, hop[2])
                ring_copy(*hop).start()

    arrive(buf_ref.at[r], got.at[0])
    arrive(panel_ref.at[:, 0], got.at[1])

    for i in range(NPIV):
        @pl.when(r == i)
        def _():
            tiles, own = pl.ds(0, 4 * (i + 1)), pl.ds(0, i + 1)
            pltpu.make_async_copy(buf_ref.at[i, tiles, 0, 0], z_ref.at[i, tiles], z_got.at[i]).start()
            pltpu.make_async_copy(panel_ref.at[own, 0], z_ref.at[i, pl.ds(24, i + 1)], f_got.at[i]).start()
            for d in (4, 3, 5, 2, 6, 1, 7):
                for copy in z_copies(i, d):
                    copy.start()

    @pl.when(has_front)
    def _():
        pltpu.make_async_copy(front_ref.at[pl.ds(1, 7), e], panel_ref.at[seat, pl.ds(1, 7)], got.at[4]).start()
        loop(1, 32, lambda d: rest_copy(d).start())

    ring_step(0)
    for i in range(NPIV - 1):
        z_ref[i, 4 * (i + 1) : 24] = jnp.zeros((20 - 4 * i, 4, BLK), jnp.float32)
    arrive(maps_ref, got.at[2])
    for i in range(NPIV):
        arrive(z_ref.at[i, pl.ds(0, 4 * (i + 1))], z_got.at[i])
        arrive(z_ref.at[i, pl.ds(24, i + 1)], f_got.at[i])

    for t, (i, j) in enumerate(TILES):
        acc_ref[t] = z_ref[i, 24 + j]

    def add_child(q):
        wanted = maps_ref[q][:NPIV]
        strips = []
        for j in range(NPIV):
            strip = None
            for seat_j in range(j + 1):
                pick = jnp.where(wanted[seat_j : seat_j + 1] == j, 1.0, 0.0)[None]
                term = z_ref[:, seat_j * 4 + q] * pick
                strip = term if strip is None else strip + term
            strips.append(strip)
        for j in range(NPIV):
            for i in range(j, NPIV):
                pick = jnp.where(wanted == i, 1.0, 0.0)[:, None, :]
                acc_ref[i * (i + 1) // 2 + j] += jnp.sum(strips[j] * pick, axis=0)

    loop(0, 4, add_child)

    own_k = pltpu.make_async_copy(acc_ref, k_ref.at[:, e], got.at[3])
    own_k.start()

    def k_copy(d):
        return push(acc_ref, k_ref.at[:, e], send.at[7], k_got.at[d], at.same_core(d)[1])

    def pair_copy(d):
        where_e = at.same_core(16 - d)[0]
        return push(k_ref.at[:, where_e], k_ref.at[:, where_e], send.at[8], p_got.at[d], at.partner)

    def forward(d):
        k_copy(d).wait_recv()
        pair_copy(d).start()

    loop(1, 16, lambda d: k_copy(d).start())
    ring_step(1)
    own_k.wait()
    pair_copy(0).start()
    ring_step(2)
    loop(1, 16, forward)
    ring_step(3)
    loop(0, 16, lambda d: pair_copy(d).wait())
    arrive(panel_ref.at[:, pl.ds(1, 7)], got.at[4])
    ring_wait(0, 2, 1)
    ring_wait(1, 2, 0)
    ring_wait(0, 3, 0)
    ring_wait(1, 3, 1)

    loop(1, 16, lambda d: k_copy(d).wait_send())
    loop(1, 32, lambda d: child_copy(d).wait_send())

    @pl.when(has_front)
    def _():
        loop(1, 32, lambda d: front_copy(d).wait_send())
        loop(1, 32, lambda d: rest_copy(d).wait_send())

    for d in range(1, 4):
        map_copy(d).wait_send()
    for i in range(NPIV):
        @pl.when(r == i)
        def _():
            for d in range(1, 8):
                for copy in z_copies(i, d):
                    copy.wait_send()

    for hop in hops:
        ring_copy(*hop).wait_send()


def gather_all(child, front, child_map):
    dma = pltpu.SemaphoreType.DMA
    return pl.pallas_call(
        gather_kernel,
        out_shape=(
            jax.ShapeDtypeStruct((NTILE, 32, 4, BLK), jnp.float32),
            jax.ShapeDtypeStruct((4, 16, BLK), jnp.int32),
            jax.ShapeDtypeStruct((8, 32, 2, 2, 4, BLK), jnp.float32),
            jax.ShapeDtypeStruct((NPIV, 8, 4, BLK), jnp.float32),
        ),
        in_specs=[VM] * 3,
        out_specs=(VM,) * 4,
        scratch_shapes=[
            pltpu.VMEM((NPIV, 30, 4, BLK), jnp.float32),
            pltpu.VMEM((NTILE, 4, BLK), jnp.float32),
            dma((9,)), dma((5,)), dma((NPIV,)), dma((NPIV,)), dma((16,)), dma((16,)), dma((2, 8)),
        ],
        compiler_params=pltpu.CompilerParams(collective_id=0, has_side_effects=True),
        name="gather_all",
    )(child, front, child_map)


def factor_kernel(
    k_ref, acc_ref, panel_ref, front_ref, low_ref, inv_ref, rows_ref, moved_ref, top_ref,
    a_ref, m_ref, share_ref, w_ref, send, got, r_got, p_got, t_got,
):
    at = Place()
    r, c, s, e = at.r, at.c, at.s, at.e
    at.greet()
    spot = jnp.minimum(r, NPIV - 1)

    def move_copy(d):
        p, device = at.plane(d)
        return push(acc_ref.at[p], moved_ref.at[:, :, e], send.at[0], got.at[0], device)

    pltpu.make_async_copy(acc_ref.at[e], moved_ref.at[:, :, e], got.at[0]).start()
    loop(1, 32, lambda d: move_copy(d).start())

    for j in range(NPIV):
        for slot in range(8):
            share_ref[slot, j] = acc_ref[j * 4, slot, 0] + panel_ref[j, slot]

    own_rows = pltpu.make_async_copy(share_ref, rows_ref.at[:, :, e], got.at[1])

    def rows_copy(d):
        return push(share_ref, rows_ref.at[:, :, e], send.at[1], r_got.at[d], at.same_core(d)[1])

    def pair_copy(d):
        where_e = at.same_core(16 - d)[0]
        return push(rows_ref.at[:, :, where_e], rows_ref.at[:, :, where_e], send.at[2], p_got.at[d], at.partner)

    def top_copy(d):
        return push(w_ref, top_ref.at[spot], send.at[3], t_got.at[spot], at.line(d))

    own_rows.start()
    loop(1, 16, lambda d: rows_copy(d).start())

    def after_first():
        own_rows.wait()
        pair_copy(0).start()
        arrive(moved_ref, got.at[0])

        @pl.when(r < NPIV)
        def _():
            w_ref[...] = moved_ref[0] + front_ref[...]
            pltpu.make_async_copy(w_ref, top_ref.at[spot], t_got.at[spot]).start()
            for d in (4, 3, 5, 2, 6, 1, 7):
                top_copy(d).start()

    def forward(d):
        rows_copy(d).wait_recv()
        pair_copy(d).start()

    def progress(b):
        pl.when(b == 2)(after_first)
        pl.when(b == 4)(lambda: loop(1, 16, forward))

    factor_steps(k_ref, low_ref, inv_ref, a_ref, m_ref, progress)

    loop(0, 16, lambda d: pair_copy(d).wait())
    for i in range(NPIV):
        arrive(top_ref.at[i], t_got.at[i])
    loop(1, 16, lambda d: rows_copy(d).wait_send())
    loop(1, 32, lambda d: move_copy(d).wait_send())

    @pl.when(r < NPIV)
    def _():
        for d in range(1, 8):
            top_copy(d).wait_send()


def factor_all(k, acc, panel, front):
    dma = pltpu.SemaphoreType.DMA
    f32 = lambda *shape: jax.ShapeDtypeStruct(shape, jnp.float32)
    return pl.pallas_call(
        factor_kernel,
        out_shape=(
            f32(PIV, PIV),
            f32(NPIV, BLK, BLK),
            f32(8, NPIV, 32, 4, BLK),
            f32(8, 2, 32, 4, BLK),
            f32(NPIV, 2, 32, 4, BLK),
        ),
        in_specs=[VM] * 4,
        out_specs=(VM,) * 5,
        scratch_shapes=[
            pltpu.VMEM((BLK, 256), jnp.float32),
            pltpu.VMEM((PIV, PIV), jnp.float32),
            pltpu.VMEM((8, NPIV, 4, BLK), jnp.float32),
            pltpu.VMEM((2, 32, 4, BLK), jnp.float32),
            dma((4,)), dma((2,)), dma((16,)), dma((16,)), dma((NPIV,)),
        ],
        compiler_params=pltpu.CompilerParams(collective_id=1, has_side_effects=True, vmem_limit_bytes=40 * 1024 * 1024),
        name="factor_all",
    )(k, acc, panel, front)


def place_kernel(map_ref, buf_ref, acc_ref):
    acc_ref[...] = jnp.zeros_like(acc_ref)
    row = lax.axis_index("row")

    def child_row(step):
        q = step // 16
        block_row = step % 16
        i = map_ref[q, block_row, 0]

        @pl.when(i % 8 == row)
        def _():
            slot = i // 8
            for block_col in range(16):
                j = map_ref[q, block_col, 0]
                tile = buf_ref[block_row % 8, block_col % 8 * 4 + q, block_row // 8, block_col // 8]
                acc_ref[j % 8 * 4 + j // 16, slot, (j // 8) % 2] += tile

    loop(0, 64, child_row)


def place(maps, buf):
    return pl.pallas_call(
        place_kernel,
        out_shape=jax.ShapeDtypeStruct((32, 8, 2, 4, BLK), jnp.float32),
        in_specs=[SM, VM],
        out_specs=VM,
        name="place",
    )(maps, buf)


NT = ((1,), (1,))
NN = ((1,), (0,))


def four(a, b, c, d):
    return jnp.concatenate([jnp.concatenate([a, b], axis=1), jnp.concatenate([c, d], axis=1)], axis=0)


def schur_kernel(
    rows_ref, top_ref, moved_ref, front_ref, low_ref, inv_ref, out_ref,
    lh, ll, yh, yl, uh, ul, x_ref,
):
    row, col, sub = (lax.axis_index(a) for a in ("row", "col", "sub"))
    high, rest = split(low_ref[...])
    lh[...] = high
    ll[...] = rest
    zero = jnp.zeros((BLK, BLK), jnp.float32)
    for p in range(3):
        first, second = inv_ref[2 * p], inv_ref[2 * p + 1]
        at = 256 * p
        cross = jnp.dot(low_ref[at + BLK : at + 256, at : at + BLK], first, precision=HI)
        cross = -jnp.dot(second, cross, precision=HI)
        high, rest = split(four(first, zero, cross, second))
        yh[p] = high
        yl[p] = rest
    for p in range(3):
        at = 256 * p
        x = four(top_ref[2 * p, 0], top_ref[2 * p, 1], top_ref[2 * p + 1, 0], top_ref[2 * p + 1, 1])
        if p:
            x = x - dot3((lh[at : at + 256, :at], ll[at : at + 256, :at]), (uh[:at, :], ul[:at, :]), NN)
        high, rest = split(dot3((yh[p], yl[p]), split(x), NN))
        uh[at : at + 256, :] = high
        ul[at : at + 256, :] = rest

    def tile(t):
        here = pl.ds(pl.multiple_of(t * 256, 256), 256)
        a, b = 2 * t, 2 * t + 1
        acc = front_ref[here, :] + four(moved_ref[a, 0], moved_ref[a, 1], moved_ref[b, 0], moved_ref[b, 1])
        xs = []
        for p in range(3):
            at = 256 * p
            x = four(rows_ref[a, 2 * p], rows_ref[a, 2 * p + 1], rows_ref[b, 2 * p], rows_ref[b, 2 * p + 1])
            for m in range(p):
                cut = slice(256 * m, 256 * m + 256)
                x = x - dot3(xs[m], (lh[at : at + 256, cut], ll[at : at + 256, cut]), NT)
            x = dot3(split(x), (yh[p], yl[p]), NT)
            x_ref[here, at : at + 256] = x
            xs.append(split(x))
            acc = acc - dot3(xs[p], (uh[at : at + 256, :], ul[at : at + 256, :]), NN)
        out_ref[here, :] = acc

    loop(0, 4, tile)

    @pl.when(row < NPIV)
    def _():
        out_ref[:BLK, :] = jnp.zeros((BLK, 256), jnp.float32)
        x_ref[:BLK, :] = low_ref[pl.ds(pl.multiple_of(row * BLK, BLK), BLK), :]

    @pl.when((sub == 0) & (col < NPIV))
    def _():
        out_ref[:, :BLK] = x_ref[:, pl.ds(pl.multiple_of(col * BLK, BLK), BLK)]


def schur(rows, top, moved, front, low, inv):
    return pl.pallas_call(
        schur_kernel,
        out_shape=jax.ShapeDtypeStruct((1024, 256), jnp.float32),
        in_specs=[VM] * 6,
        out_specs=VM,
        scratch_shapes=[
            pltpu.VMEM((PIV, PIV), jnp.bfloat16),
            pltpu.VMEM((PIV, PIV), jnp.bfloat16),
            pltpu.VMEM((3, 256, 256), jnp.bfloat16),
            pltpu.VMEM((3, 256, 256), jnp.bfloat16),
            pltpu.VMEM((PIV, 256), jnp.bfloat16),
            pltpu.VMEM((PIV, 256), jnp.bfloat16),
            pltpu.VMEM((1024, PIV), jnp.float32),
        ],
        compiler_params=pltpu.CompilerParams(vmem_limit_bytes=32 * 1024 * 1024),
        name="schur",
    )(rows, top, moved, front, low, inv)


def body(front, child, child_map):
    wide = jnp.broadcast_to(child_map[0][:, None], (16, BLK))
    shares = child[0].reshape(2, BLK, 2, BLK).transpose(0, 2, 1, 3).reshape(2, 2, 32, 4, BLK)
    k, maps, buf, panel = gather_all(shares, front[:, :BLK].reshape(8, 32, 4, BLK), wide)
    acc = place(maps, buf)
    first = front[:BLK].reshape(BLK, 2, BLK).transpose(1, 0, 2).reshape(2, 32, 4, BLK)
    low, inv, rows, moved, top = factor_all(k.reshape(NTILE, BLK, BLK), acc, panel, first)
    return schur(
        rows.reshape(8, NPIV, BLK, BLK),
        top.reshape(NPIV, 2, BLK, BLK),
        moved.reshape(8, 2, BLK, BLK),
        front,
        low,
        inv,
    )


def solution(mesh):
    placed = (P("row", ("col", "sub")), P("sub", "row", "col"), P("sub", None))
    return jax.shard_map(
        body, mesh=mesh, in_specs=placed, out_specs=P("row", ("col", "sub")), check_vma=False
    )
```

```python
import jax
import jax.numpy as jnp
from jax import lax
from jax.experimental import pallas as pl
from jax.experimental.pallas import tpu as pltpu
from jax.sharding import PartitionSpec as P

BLK = 128
NPIV = 6
PIV = NPIV * BLK
PLANE = ("col", "sub")
HI = lax.Precision.HIGHEST
VM = pl.BlockSpec(memory_space=pltpu.VMEM)
SM = pl.BlockSpec(memory_space=pltpu.SMEM)


def nt(a, b, precision=HI):
    return lax.dot_general(a, b, (((1,), (1,)), ((), ())), precision=precision, preferred_element_type=jnp.float32)
def tn(a, b, precision=HI):
    return lax.dot_general(a, b, (((0,), (0,)), ((), ())), precision=precision, preferred_element_type=jnp.float32)

def split(x):
    high = x.astype(jnp.bfloat16)
    return high, (x - high.astype(jnp.float32)).astype(jnp.bfloat16)


def dot3(a, b, dims):
    def one(x, y):
        return lax.dot_general(x, y, (dims, ((), ())), preferred_element_type=jnp.float32)

    return one(a[0], b[0]) + (one(a[0], b[1]) + one(a[1], b[0]))


def tn3(a, b):
    return dot3(split(a), split(b), ((0,), (0,)))


def nt3(a, b):
    return dot3(split(a), split(b), ((1,), (1,)))


def rsqrt(x):
    return lax.rsqrt(x)

def wide(x):
    return jnp.concatenate([x, x], axis=1)

def eliminate(a_ref):
    sub = lax.broadcasted_iota(jnp.int32, (8, 256), 0)
    ahead = []
    for g in range(16):
        if g == 0:
            ahead = [a_ref[8 * h : 8 * h + 8, :] for h in range(2 + 1)]
        elif g + 2 < 16:
            ahead.append(a_ref[8 * (g + 2) : 8 * (g + 2) + 8, :])
        rows = ahead.pop(0)
        left = rows[:, :BLK]
        e = {}
        for j in range(8):
            c = jnp.broadcast_to(left[:, 8 * g + j : 8 * g + j + 1], (8, BLK))
            for i in range(j, 8):
                e[j, i] = jnp.broadcast_to(c[i : i + 1, :], (8, BLK))
        r = [jnp.broadcast_to(rows[i : i + 1, :], (8, 256)) for i in range(8)]
        cols = [[jnp.broadcast_to(n[:, 8 * g + j : 8 * g + j + 1], (8, BLK)) for j in range(8)] for n in ahead]
        out = None
        for j in range(8):
            s = rsqrt(e[j, j])
            u = {i: e[j, i] * s for i in range(j + 1, 8)}
            for i in range(j + 1, 8):
                for m in range(i, 8):
                    e[i, m] = e[i, m] - u[i] * u[m]
            rj = r[j] * wide(s)
            for i in range(j + 1, 8):
                r[i] = r[i] - wide(u[i]) * rj
            for h in range(len(ahead)):
                cj = cols[h][j] * s
                for m in range(j + 1, 8):
                    cols[h][m] = cols[h][m] - cj * u[m]
                ahead[h] = ahead[h] - wide(cj) * rj
            out = rj if out is None else jnp.where(sub == j, rj, out)
        a_ref[8 * g : 8 * g + 8, :] = out
        low = 8 * (g + 1 + 2)
        if low < BLK:
            t = tn3(out[:, :BLK], out)
            a_ref[low:, :] = a_ref[low:, :] - t[low:, :]

def factor_begin(l_ref, m_ref):
    for i in range(NPIV - 1):
        m_ref[i * BLK : (i + 1) * BLK, (i + 1) * BLK :] = jnp.zeros((BLK, PIV - (i + 1) * BLK), jnp.float32)
    l_ref[...] = jnp.zeros_like(l_ref)


def factor_steps(l_ref, y_ref, a_ref, m_ref, progress):
    r_iota = lax.broadcasted_iota(jnp.int32, (BLK, BLK), 0)
    c_iota = lax.broadcasted_iota(jnp.int32, (BLK, BLK), 1)

    def step(b, carry):
        progress(b)
        at = pl.ds(pl.multiple_of(b * BLK, BLK), BLK)
        a_ref[:, :BLK] = m_ref[at, at]
        a_ref[:, BLK:] = jnp.where(r_iota == c_iota, 1.0, 0.0)
        eliminate(a_ref)
        y = a_ref[:, BLK:]
        y_ref[b] = y
        l_ref[at, at] = jnp.where(r_iota >= c_iota, a_ref[:, :BLK].T, 0.0)

        def solve(i, c):
            rows = pl.ds(pl.multiple_of(i * BLK, BLK), BLK)
            l_ref[rows, at] = nt(m_ref[rows, at], y)
            return c

        lax.fori_loop(b + 1, NPIV, solve, 0)

        def update(i, c):
            rows = pl.ds(pl.multiple_of(i * BLK, BLK), BLK)
            m_ref[rows, :] = m_ref[rows, :] - nt3(l_ref[rows, at], l_ref[:, at])
            return c

        lax.fori_loop(b + 1, NPIV, update, 0)
        return carry

    lax.fori_loop(0, NPIV, step, 0)


MESH = pl.DeviceIdType.MESH
TILES = [(i, j) for i in range(NPIV) for j in range(i + 1)]
NTILE = len(TILES)


class Place:
    def __init__(self):
        self.r, self.c, self.s = (lax.axis_index(a) for a in ("row", "col", "sub"))
        self.e = self.c * 4 + self.s
        self.core = self.c % 2
        self.chip = (self.c // 2) * 4 + self.s
        self.partner = (self.r, self.c + 1 - 2 * self.core, self.s)

    def plane(self, d):
        p = (self.e + d) % 32
        return p, (self.r, p // 4, p % 4)

    def same_core(self, d):
        p = (self.chip + d) % 16
        c = (p // 4) * 2 + self.core
        return c * 4 + p % 4, (self.r, c, p % 4)

    def line(self, d):
        return ((self.r + d) % 8, self.c, self.s)

    def greet(self, meanwhile):
        barrier = pltpu.get_barrier_semaphore()

        def plane(d, carry):
            pl.semaphore_signal(barrier, inc=1, device_id=self.plane(d)[1], device_id_type=MESH)
            return carry

        def line(d, carry):
            pl.semaphore_signal(barrier, inc=1, device_id=self.line(d), device_id_type=MESH)
            return carry

        lax.fori_loop(1, 32, plane, 0)
        lax.fori_loop(1, 8, line, 0)
        meanwhile()
        pl.semaphore_wait(barrier, 38)


def push(src, dst, ssem, rsem, device):
    return pltpu.make_async_remote_copy(
        src_ref=src, dst_ref=dst, send_sem=ssem, recv_sem=rsem, device_id=device, device_id_type=MESH
    )


def arrive(ref, sem):
    pltpu.make_async_copy(ref, ref, sem).wait()


def loop(low, high, f):
    def one(d, carry):
        f(d)
        return carry

    lax.fori_loop(low, high, one, 0)


def gather_kernel(
    tile_ref, whole_ref, list_ref, k_ref, maps_ref, buf_ref, panel_ref,
    child_ref, strip_ref, front_ref, map_ref, z_ref, acc_ref, send, got, z_got, f_got, k_got, p_got, ring_got,
):
    at = Place()
    r, c, s, e = at.r, at.c, at.s, at.e
    has_front = (c < NPIV) & (s == 0)

    def prepare():
        fetch = pltpu.make_async_copy(whole_ref.at[:, pl.ds(0, BLK)], strip_ref, got.at[5])
        fetch.start()
        for i in range(2):
            for j in range(2):
                child_ref[:, i, j] = tile_ref[0, i * BLK : (i + 1) * BLK, j * BLK : (j + 1) * BLK].reshape(32, 4, BLK)
        for i in range(16):
            map_ref[i : i + 1, :] = jnp.full((1, BLK), list_ref[0, i], jnp.int32)
        for i in range(NPIV - 1):
            z_ref[i, 4 * (i + 1) : 24] = jnp.zeros((20 - 4 * i, 4, BLK), jnp.float32)
        fetch.wait()

        @pl.when(has_front)
        def _():
            for i in range(8):
                front_ref[i] = strip_ref[i * BLK : (i + 1) * BLK, :].reshape(32, 4, BLK)

    at.greet(prepare)
    seat = jnp.minimum(c, NPIV - 1)

    def child_copy(d):
        p, device = at.plane(d)
        return push(child_ref.at[p], buf_ref.at[r, e], send.at[0], got.at[0], device)

    def front_copy(d):
        p, device = at.plane(d)
        return push(front_ref.at[0, p], panel_ref.at[seat, 0], send.at[1], got.at[1], device)

    def rest_copy(d):
        p, device = at.plane(d)
        return push(front_ref.at[pl.ds(1, 7), p], panel_ref.at[seat, pl.ds(1, 7)], send.at[4], got.at[4], device)

    def map_copy(d):
        return push(map_ref, maps_ref.at[s], send.at[2], got.at[2], (r, c, (s + d) % 4))

    pltpu.make_async_copy(child_ref.at[e], buf_ref.at[r, e], got.at[0]).start()
    pltpu.make_async_copy(map_ref, maps_ref.at[s], got.at[2]).start()
    loop(1, 32, lambda d: child_copy(d).start())

    @pl.when(has_front)
    def _():
        pltpu.make_async_copy(front_ref.at[0, e], panel_ref.at[seat, 0], got.at[1]).start()
        loop(1, 32, lambda d: front_copy(d).start())

    for d in range(1, 4):
        map_copy(d).start()

    def z_copies(i, d):
        device = at.line(d)
        tiles, own = pl.ds(0, 4 * (i + 1)), pl.ds(0, i + 1)
        return (
            push(buf_ref.at[i, tiles, 0, 0], z_ref.at[i, tiles], send.at[3], z_got.at[i], device),
            push(panel_ref.at[own, 0], z_ref.at[i, pl.ds(24, i + 1)], send.at[3], f_got.at[i], device),
        )

    def ring_copy(way, k, h):
        block = (r + 8 - k) % 8 if way == 0 else (r + k) % 8
        half = buf_ref.at[block, :, h]
        return push(half, half, send.at[5 + way], ring_got.at[way, 2 * k + h], at.line(1 if way == 0 else 7))

    def ring_wait(way, k, h):
        block = (r + 7 - k) % 8 if way == 0 else (r + 1 + k) % 8
        arrive(buf_ref.at[block, :, h], ring_got.at[way, 2 * k + h])

    hops = [(way, k, h) for k in range(4) for h in range(2) for way in range(2) if k < 3 or h == way]

    def ring_step(k):
        for hop in hops:
            if hop[1] == k:
                if k:
                    ring_wait(hop[0], k - 1, hop[2])
                ring_copy(*hop).start()

    arrive(buf_ref.at[r], got.at[0])
    arrive(panel_ref.at[:, 0], got.at[1])

    for i in range(NPIV):
        @pl.when(r == i)
        def _():
            tiles, own = pl.ds(0, 4 * (i + 1)), pl.ds(0, i + 1)
            pltpu.make_async_copy(buf_ref.at[i, tiles, 0, 0], z_ref.at[i, tiles], z_got.at[i]).start()
            pltpu.make_async_copy(panel_ref.at[own, 0], z_ref.at[i, pl.ds(24, i + 1)], f_got.at[i]).start()
            for d in (4, 3, 5, 2, 6, 1, 7):
                for copy in z_copies(i, d):
                    copy.start()

    @pl.when(has_front)
    def _():
        pltpu.make_async_copy(front_ref.at[pl.ds(1, 7), e], panel_ref.at[seat, pl.ds(1, 7)], got.at[4]).start()
        loop(1, 32, lambda d: rest_copy(d).start())

    ring_step(0)
    arrive(maps_ref, got.at[2])
    for i in range(NPIV):
        arrive(z_ref.at[i, pl.ds(0, 4 * (i + 1))], z_got.at[i])
        arrive(z_ref.at[i, pl.ds(24, i + 1)], f_got.at[i])

    for t, (i, j) in enumerate(TILES):
        acc_ref[t] = z_ref[i, 24 + j]

    def add_child(q):
        wanted = maps_ref[q][:NPIV]
        strips = []
        for j in range(NPIV):
            strip = None
            for seat_j in range(j + 1):
                pick = jnp.where(wanted[seat_j : seat_j + 1] == j, 1.0, 0.0)[None]
                term = z_ref[:, seat_j * 4 + q] * pick
                strip = term if strip is None else strip + term
            strips.append(strip)
        for j in range(NPIV):
            for i in range(j, NPIV):
                pick = jnp.where(wanted == i, 1.0, 0.0)[:, None, :]
                acc_ref[i * (i + 1) // 2 + j] += jnp.sum(strips[j] * pick, axis=0)

    loop(0, 4, add_child)

    own_k = pltpu.make_async_copy(acc_ref, k_ref.at[:, e], got.at[3])
    own_k.start()

    def k_copy(d):
        return push(acc_ref, k_ref.at[:, e], send.at[7], k_got.at[d], at.same_core(d)[1])

    def pair_copy(d):
        where_e = at.same_core(16 - d)[0]
        return push(k_ref.at[:, where_e], k_ref.at[:, where_e], send.at[8], p_got.at[d], at.partner)

    def forward(d):
        k_copy(d).wait_recv()
        pair_copy(d).start()

    loop(1, 16, lambda d: k_copy(d).start())
    ring_step(1)
    own_k.wait()
    pair_copy(0).start()
    ring_step(2)
    loop(1, 16, forward)
    ring_step(3)
    loop(0, 16, lambda d: pair_copy(d).wait())
    arrive(panel_ref.at[:, pl.ds(1, 7)], got.at[4])
    ring_wait(0, 2, 1)
    ring_wait(1, 2, 0)
    ring_wait(0, 3, 0)
    ring_wait(1, 3, 1)

    loop(1, 16, lambda d: k_copy(d).wait_send())
    loop(1, 32, lambda d: child_copy(d).wait_send())

    @pl.when(has_front)
    def _():
        loop(1, 32, lambda d: front_copy(d).wait_send())
        loop(1, 32, lambda d: rest_copy(d).wait_send())

    for d in range(1, 4):
        map_copy(d).wait_send()
    for i in range(NPIV):
        @pl.when(r == i)
        def _():
            for d in range(1, 8):
                for copy in z_copies(i, d):
                    copy.wait_send()

    for hop in hops:
        ring_copy(*hop).wait_send()


def gather_all(child, front, child_map):
    dma = pltpu.SemaphoreType.DMA
    return pl.pallas_call(
        gather_kernel,
        out_shape=(
            jax.ShapeDtypeStruct((NTILE, 32, 4, BLK), jnp.float32),
            jax.ShapeDtypeStruct((4, 16, BLK), jnp.int32),
            jax.ShapeDtypeStruct((8, 32, 2, 2, 4, BLK), jnp.float32),
            jax.ShapeDtypeStruct((NPIV, 8, 4, BLK), jnp.float32),
        ),
        in_specs=[VM, pl.BlockSpec(memory_space=pltpu.HBM), SM],
        out_specs=(VM,) * 4,
        scratch_shapes=[
            pltpu.VMEM((32, 2, 2, 4, BLK), jnp.float32),
            pltpu.VMEM((1024, BLK), jnp.float32),
            pltpu.VMEM((8, 32, 4, BLK), jnp.float32),
            pltpu.VMEM((16, BLK), jnp.int32),
            pltpu.VMEM((NPIV, 30, 4, BLK), jnp.float32),
            pltpu.VMEM((NTILE, 4, BLK), jnp.float32),
            dma((9,)), dma((6,)), dma((NPIV,)), dma((NPIV,)), dma((16,)), dma((16,)), dma((2, 8)),
        ],
        compiler_params=pltpu.CompilerParams(collective_id=0, has_side_effects=True),
        name="gather_all",
    )(child, front, child_map)


def factor_kernel(
    k_ref, acc_ref, panel_ref, front_ref, low_ref, inv_ref, rows_ref, moved_ref, top_ref,
    a_ref, m_ref, piece_ref, share_ref, w_ref, send, got, r_got, p_got, t_got,
):
    at = Place()
    r, c, s, e = at.r, at.c, at.s, at.e
    spot = jnp.minimum(r, NPIV - 1)

    def prepare():
        fetch = [pltpu.make_async_copy(acc_ref.at[4 * j, :, 0], piece_ref.at[j], got.at[2 + j]) for j in range(NPIV)]
        tiles = [
            pltpu.make_async_copy(
                k_ref.at[t], m_ref.at[pl.ds(i * BLK, BLK), pl.ds(j * BLK, BLK)], got.at[2 + NPIV + t]
            )
            for t, (i, j) in enumerate(TILES)
        ]
        for copy in fetch + tiles:
            copy.start()
        factor_begin(low_ref, m_ref)
        for copy in fetch:
            copy.wait()
        for j in range(NPIV):
            for slot in range(8):
                share_ref[slot, j] = piece_ref[j, slot] + panel_ref[j, slot]
        for copy in tiles:
            copy.wait()

    at.greet(prepare)

    def move_copy(d):
        p, device = at.plane(d)
        return push(acc_ref.at[p], moved_ref.at[:, :, e], send.at[0], got.at[0], device)

    pltpu.make_async_copy(acc_ref.at[e], moved_ref.at[:, :, e], got.at[0]).start()
    loop(1, 32, lambda d: move_copy(d).start())

    own_rows = pltpu.make_async_copy(share_ref, rows_ref.at[:, :, e], got.at[1])

    def rows_copy(d):
        return push(share_ref, rows_ref.at[:, :, e], send.at[1], r_got.at[d], at.same_core(d)[1])

    def pair_copy(d):
        where_e = at.same_core(16 - d)[0]
        return push(rows_ref.at[:, :, where_e], rows_ref.at[:, :, where_e], send.at[2], p_got.at[d], at.partner)

    def top_copy(d):
        return push(w_ref, top_ref.at[spot], send.at[3], t_got.at[spot], at.line(d))

    own_rows.start()
    loop(1, 16, lambda d: rows_copy(d).start())

    def after_first():
        own_rows.wait()
        pair_copy(0).start()
        arrive(moved_ref, got.at[0])

        @pl.when(r < NPIV)
        def _():
            for i in range(2):
                w_ref[i] = moved_ref[0, i] + front_ref[:BLK, i * BLK : (i + 1) * BLK].reshape(32, 4, BLK)
            pltpu.make_async_copy(w_ref, top_ref.at[spot], t_got.at[spot]).start()
            for d in (4, 3, 5, 2, 6, 1, 7):
                top_copy(d).start()

    def forward(d):
        rows_copy(d).wait_recv()
        pair_copy(d).start()

    def progress(b):
        pl.when(b == 2)(after_first)
        pl.when(b == 4)(lambda: loop(1, 16, forward))

    factor_steps(low_ref, inv_ref, a_ref, m_ref, progress)

    loop(0, 16, lambda d: pair_copy(d).wait())
    for i in range(NPIV):
        arrive(top_ref.at[i], t_got.at[i])
    loop(1, 16, lambda d: rows_copy(d).wait_send())
    loop(1, 32, lambda d: move_copy(d).wait_send())

    @pl.when(r < NPIV)
    def _():
        for d in range(1, 8):
            top_copy(d).wait_send()


def factor_all(k, acc, panel, front):
    dma = pltpu.SemaphoreType.DMA
    f32 = lambda *shape: jax.ShapeDtypeStruct(shape, jnp.float32)
    return pl.pallas_call(
        factor_kernel,
        out_shape=(
            f32(PIV, PIV),
            f32(NPIV, BLK, BLK),
            f32(8, NPIV, 32, 4, BLK),
            f32(8, 2, 32, 4, BLK),
            f32(NPIV, 2, 32, 4, BLK),
        ),
        in_specs=[pl.BlockSpec(memory_space=pltpu.HBM)] * 2 + [VM] * 2,
        out_specs=(VM,) * 5,
        scratch_shapes=[
            pltpu.VMEM((BLK, 256), jnp.float32),
            pltpu.VMEM((PIV, PIV), jnp.float32),
            pltpu.VMEM((NPIV, 8, 4, BLK), jnp.float32),
            pltpu.VMEM((8, NPIV, 4, BLK), jnp.float32),
            pltpu.VMEM((2, 32, 4, BLK), jnp.float32),
            dma((4,)), dma((2 + NPIV + NTILE,)), dma((16,)), dma((16,)), dma((NPIV,)),
        ],
        compiler_params=pltpu.CompilerParams(collective_id=1, has_side_effects=True, vmem_limit_bytes=40 * 1024 * 1024),
        name="factor_all",
    )(k, acc, panel, front)


def place_kernel(map_ref, buf_ref, acc_ref):
    acc_ref[...] = jnp.zeros_like(acc_ref)
    row = lax.axis_index("row")

    for q in range(4):
        targets = [map_ref[q, j, 0] for j in range(16)]
        spots = [(j % 8 * 4 + j // 16, (j // 8) % 2) for j in targets]

        def child_row(block_row):
            i = map_ref[q, block_row, 0]

            @pl.when(i % 8 == row)
            def _():
                slot = i // 8
                for block_col, (dest, half) in enumerate(spots):
                    acc_ref[dest, slot, half] += buf_ref[
                        block_row % 8, block_col % 8 * 4 + q, block_row // 8, block_col // 8
                    ]

        loop(0, 16, child_row)


def place(maps, buf):
    return pl.pallas_call(
        place_kernel,
        out_shape=jax.ShapeDtypeStruct((32, 8, 2, 4, BLK), jnp.float32),
        in_specs=[SM, VM],
        out_specs=VM,
        name="place",
    )(maps, buf)


NT = ((1,), (1,))
NN = ((1,), (0,))


def four(a, b, c, d):
    return jnp.concatenate([jnp.concatenate([a, b], axis=1), jnp.concatenate([c, d], axis=1)], axis=0)


def schur_kernel(
    rows_ref, top_ref, moved_ref, front_ref, low_ref, inv_ref, out_ref,
    lh, ll, yh, yl, uh, ul, x_ref,
):
    row, col, sub = (lax.axis_index(a) for a in ("row", "col", "sub"))
    high, rest = split(low_ref[...])
    lh[...] = high
    ll[...] = rest
    zero = jnp.zeros((BLK, BLK), jnp.float32)
    for p in range(3):
        first, second = inv_ref[2 * p], inv_ref[2 * p + 1]
        at = 256 * p
        cross = jnp.dot(low_ref[at + BLK : at + 256, at : at + BLK], first, precision=HI)
        cross = -jnp.dot(second, cross, precision=HI)
        high, rest = split(four(first, zero, cross, second))
        yh[p] = high
        yl[p] = rest
    for p in range(3):
        at = 256 * p
        x = four(top_ref[2 * p, 0], top_ref[2 * p, 1], top_ref[2 * p + 1, 0], top_ref[2 * p + 1, 1])
        if p:
            x = x - dot3((lh[at : at + 256, :at], ll[at : at + 256, :at]), (uh[:at, :], ul[:at, :]), NN)
        high, rest = split(dot3((yh[p], yl[p]), split(x), NN))
        uh[at : at + 256, :] = high
        ul[at : at + 256, :] = rest

    def tile(t):
        here = pl.ds(pl.multiple_of(t * 256, 256), 256)
        a, b = 2 * t, 2 * t + 1
        acc = front_ref[here, :] + four(moved_ref[a, 0], moved_ref[a, 1], moved_ref[b, 0], moved_ref[b, 1])
        xs = []
        for p in range(3):
            at = 256 * p
            x = four(rows_ref[a, 2 * p], rows_ref[a, 2 * p + 1], rows_ref[b, 2 * p], rows_ref[b, 2 * p + 1])
            for m in range(p):
                cut = slice(256 * m, 256 * m + 256)
                x = x - dot3(xs[m], (lh[at : at + 256, cut], ll[at : at + 256, cut]), NT)
            x = dot3(split(x), (yh[p], yl[p]), NT)
            x_ref[here, at : at + 256] = x
            xs.append(split(x))
            acc = acc - dot3(xs[p], (uh[at : at + 256, :], ul[at : at + 256, :]), NN)
        out_ref[here, :] = acc

    loop(0, 4, tile)

    @pl.when(row < NPIV)
    def _():
        out_ref[:BLK, :] = jnp.zeros((BLK, 256), jnp.float32)
        x_ref[:BLK, :] = low_ref[pl.ds(pl.multiple_of(row * BLK, BLK), BLK), :]

    @pl.when((sub == 0) & (col < NPIV))
    def _():
        out_ref[:, :BLK] = x_ref[:, pl.ds(pl.multiple_of(col * BLK, BLK), BLK)]


def schur(rows, top, moved, front, low, inv):
    return pl.pallas_call(
        schur_kernel,
        out_shape=jax.ShapeDtypeStruct((1024, 256), jnp.float32),
        in_specs=[VM] * 6,
        out_specs=VM,
        scratch_shapes=[
            pltpu.VMEM((PIV, PIV), jnp.bfloat16),
            pltpu.VMEM((PIV, PIV), jnp.bfloat16),
            pltpu.VMEM((3, 256, 256), jnp.bfloat16),
            pltpu.VMEM((3, 256, 256), jnp.bfloat16),
            pltpu.VMEM((PIV, 256), jnp.bfloat16),
            pltpu.VMEM((PIV, 256), jnp.bfloat16),
            pltpu.VMEM((1024, PIV), jnp.float32),
        ],
        compiler_params=pltpu.CompilerParams(vmem_limit_bytes=32 * 1024 * 1024),
        name="schur",
    )(rows, top, moved, front, low, inv)


def body(front, child, child_map):
    k, maps, buf, panel = gather_all(child, front, child_map)
    acc = place(maps, buf)
    low, inv, rows, moved, top = factor_all(k.reshape(NTILE, BLK, BLK), acc, panel, front)
    return schur(
        rows.reshape(8, NPIV, BLK, BLK),
        top.reshape(NPIV, 2, BLK, BLK),
        moved.reshape(8, 2, BLK, BLK),
        front,
        low,
        inv,
    )


def solution(mesh):
    placed = (P("row", ("col", "sub")), P("sub", "row", "col"), P("sub", None))
    return jax.shard_map(
        body, mesh=mesh, in_specs=placed, out_specs=P("row", ("col", "sub")), check_vma=False
    )
```

```python
import jax
import jax.numpy as jnp
from jax import lax
from jax.experimental import pallas as pl
from jax.experimental.pallas import tpu as pltpu
from jax.sharding import PartitionSpec as P

BLK = 128
NPIV = 6
PIV = NPIV * BLK
PLANE = ("col", "sub")
HI = lax.Precision.HIGHEST
VM = pl.BlockSpec(memory_space=pltpu.VMEM)
SM = pl.BlockSpec(memory_space=pltpu.SMEM)


def nt(a, b, precision=HI):
    return lax.dot_general(a, b, (((1,), (1,)), ((), ())), precision=precision, preferred_element_type=jnp.float32)
def tn(a, b, precision=HI):
    return lax.dot_general(a, b, (((0,), (0,)), ((), ())), precision=precision, preferred_element_type=jnp.float32)

def split(x):
    high = x.astype(jnp.bfloat16)
    return high, (x - high.astype(jnp.float32)).astype(jnp.bfloat16)


def dot3(a, b, dims):
    def one(x, y):
        return lax.dot_general(x, y, (dims, ((), ())), preferred_element_type=jnp.float32)

    return one(a[0], b[0]) + (one(a[0], b[1]) + one(a[1], b[0]))


def tn3(a, b):
    return dot3(split(a), split(b), ((0,), (0,)))


def nt3(a, b):
    return dot3(split(a), split(b), ((1,), (1,)))


def rsqrt(x):
    return lax.rsqrt(x)

def wide(x):
    return jnp.concatenate([x, x], axis=1)

def eliminate(a_ref):
    sub = lax.broadcasted_iota(jnp.int32, (8, 256), 0)
    ahead = []
    for g in range(16):
        if g == 0:
            ahead = [a_ref[8 * h : 8 * h + 8, :] for h in range(2 + 1)]
        elif g + 2 < 16:
            ahead.append(a_ref[8 * (g + 2) : 8 * (g + 2) + 8, :])
        rows = ahead.pop(0)
        left = rows[:, :BLK]
        e = {}
        for j in range(8):
            c = jnp.broadcast_to(left[:, 8 * g + j : 8 * g + j + 1], (8, BLK))
            for i in range(j, 8):
                e[j, i] = jnp.broadcast_to(c[i : i + 1, :], (8, BLK))
        r = [jnp.broadcast_to(rows[i : i + 1, :], (8, 256)) for i in range(8)]
        cols = [[jnp.broadcast_to(n[:, 8 * g + j : 8 * g + j + 1], (8, BLK)) for j in range(8)] for n in ahead]
        out = None
        for j in range(8):
            s = rsqrt(e[j, j])
            u = {i: e[j, i] * s for i in range(j + 1, 8)}
            for i in range(j + 1, 8):
                for m in range(i, 8):
                    e[i, m] = e[i, m] - u[i] * u[m]
            rj = r[j] * wide(s)
            for i in range(j + 1, 8):
                r[i] = r[i] - wide(u[i]) * rj
            for h in range(len(ahead)):
                cj = cols[h][j] * s
                for m in range(j + 1, 8):
                    cols[h][m] = cols[h][m] - cj * u[m]
                ahead[h] = ahead[h] - wide(cj) * rj
            out = rj if out is None else jnp.where(sub == j, rj, out)
        a_ref[8 * g : 8 * g + 8, :] = out
        low = 8 * (g + 1 + 2)
        if low < BLK:
            t = tn3(out[:, :BLK], out)
            a_ref[low:, :] = a_ref[low:, :] - t[low:, :]

def factor_begin(l_ref, m_ref):
    for i in range(NPIV - 1):
        m_ref[i * BLK : (i + 1) * BLK, (i + 1) * BLK :] = jnp.zeros((BLK, PIV - (i + 1) * BLK), jnp.float32)
    l_ref[...] = jnp.zeros_like(l_ref)


def diagonal(a_ref, block):
    r_iota = lax.broadcasted_iota(jnp.int32, (BLK, BLK), 0)
    c_iota = lax.broadcasted_iota(jnp.int32, (BLK, BLK), 1)
    a_ref[:, :BLK] = block
    a_ref[:, BLK:] = jnp.where(r_iota == c_iota, 1.0, 0.0)
    eliminate(a_ref)


def factor_finish(b, l_ref, y_ref, a_ref, m_ref):
    r_iota = lax.broadcasted_iota(jnp.int32, (BLK, BLK), 0)
    c_iota = lax.broadcasted_iota(jnp.int32, (BLK, BLK), 1)
    at = pl.ds(b * BLK if isinstance(b, int) else pl.multiple_of(b * BLK, BLK), BLK)
    y = a_ref[:, BLK:]
    y_ref[b] = y
    l_ref[at, at] = jnp.where(r_iota >= c_iota, a_ref[:, :BLK].T, 0.0)

    def solve(i, c):
        rows = pl.ds(pl.multiple_of(i * BLK, BLK), BLK)
        l_ref[rows, at] = nt(m_ref[rows, at], y)
        return c

    lax.fori_loop(b + 1, NPIV, solve, 0)

    def update(i, c):
        rows = pl.ds(pl.multiple_of(i * BLK, BLK), BLK)
        m_ref[rows, :] = m_ref[rows, :] - nt3(l_ref[rows, at], l_ref[:, at])
        return c

    lax.fori_loop(b + 1, NPIV, update, 0)


def factor_steps(l_ref, y_ref, a_ref, m_ref, progress):
    def step(b, carry):
        progress(b)
        at = pl.ds(pl.multiple_of(b * BLK, BLK), BLK)
        diagonal(a_ref, m_ref[at, at])
        factor_finish(b, l_ref, y_ref, a_ref, m_ref)
        return carry

    lax.fori_loop(1, NPIV, step, 0)


MESH = pl.DeviceIdType.MESH
TILES = [(i, j) for i in range(NPIV) for j in range(i + 1)]
NTILE = len(TILES)


class Place:
    def __init__(self):
        self.r, self.c, self.s = (lax.axis_index(a) for a in ("row", "col", "sub"))
        self.e = self.c * 4 + self.s
        self.core = self.c % 2
        self.chip = (self.c // 2) * 4 + self.s
        self.partner = (self.r, self.c + 1 - 2 * self.core, self.s)

    def plane(self, d):
        p = (self.e + d) % 32
        return p, (self.r, p // 4, p % 4)

    def same_core(self, d):
        p = (self.chip + d) % 16
        c = (p // 4) * 2 + self.core
        return c * 4 + p % 4, (self.r, c, p % 4)

    def line(self, d):
        return ((self.r + d) % 8, self.c, self.s)

    def greet(self, meanwhile):
        barrier = pltpu.get_barrier_semaphore()

        def plane(d, carry):
            pl.semaphore_signal(barrier, inc=1, device_id=self.plane(d)[1], device_id_type=MESH)
            return carry

        def line(d, carry):
            pl.semaphore_signal(barrier, inc=1, device_id=self.line(d), device_id_type=MESH)
            return carry

        lax.fori_loop(1, 32, plane, 0)
        lax.fori_loop(1, 8, line, 0)
        meanwhile()
        pl.semaphore_wait(barrier, 38)


def push(src, dst, ssem, rsem, device):
    return pltpu.make_async_remote_copy(
        src_ref=src, dst_ref=dst, send_sem=ssem, recv_sem=rsem, device_id=device, device_id_type=MESH
    )


def arrive(ref, sem):
    pltpu.make_async_copy(ref, ref, sem).wait()


def loop(low, high, f):
    def one(d, carry):
        f(d)
        return carry

    lax.fori_loop(low, high, one, 0)


def gather_kernel(
    tile_ref, whole_ref, list_ref, k_ref, maps_ref, buf_ref, panel_ref, first_ref,
    child_ref, strip_ref, front_ref, map_ref, z_ref, acc_ref, send, got, z_got, f_got, k_got, p_got, ring_got,
):
    at = Place()
    r, c, s, e = at.r, at.c, at.s, at.e
    has_front = (c < NPIV) & (s == 0)

    def prepare():
        fetch = pltpu.make_async_copy(whole_ref.at[:, pl.ds(0, BLK)], strip_ref, got.at[5])
        fetch.start()
        for i in range(2):
            for j in range(2):
                child_ref[:, i, j] = tile_ref[0, i * BLK : (i + 1) * BLK, j * BLK : (j + 1) * BLK].reshape(32, 4, BLK)
        for i in range(16):
            map_ref[i : i + 1, :] = jnp.full((1, BLK), list_ref[0, i], jnp.int32)
        for i in range(NPIV - 1):
            z_ref[i, 4 * (i + 1) : 24] = jnp.zeros((20 - 4 * i, 4, BLK), jnp.float32)
        fetch.wait()

        @pl.when(has_front)
        def _():
            for i in range(8):
                front_ref[i] = strip_ref[i * BLK : (i + 1) * BLK, :].reshape(32, 4, BLK)

    at.greet(prepare)
    seat = jnp.minimum(c, NPIV - 1)

    def child_copy(d):
        p, device = at.plane(d)
        return push(child_ref.at[p], buf_ref.at[r, e], send.at[0], got.at[0], device)

    def front_copy(d):
        p, device = at.plane(d)
        return push(front_ref.at[0, p], panel_ref.at[seat, 0], send.at[1], got.at[1], device)

    def rest_copy(d):
        p, device = at.plane(d)
        return push(front_ref.at[pl.ds(1, 7), p], panel_ref.at[seat, pl.ds(1, 7)], send.at[4], got.at[4], device)

    def map_copy(d):
        return push(map_ref, maps_ref.at[s], send.at[2], got.at[2], (r, c, (s + d) % 4))

    pltpu.make_async_copy(child_ref.at[e], buf_ref.at[r, e], got.at[0]).start()
    pltpu.make_async_copy(map_ref, maps_ref.at[s], got.at[2]).start()
    loop(1, 32, lambda d: child_copy(d).start())

    @pl.when(has_front)
    def _():
        pltpu.make_async_copy(front_ref.at[0, e], panel_ref.at[seat, 0], got.at[1]).start()
        loop(1, 32, lambda d: front_copy(d).start())

    for d in range(1, 4):
        map_copy(d).start()

    def z_copies(i, d):
        device = at.line(d)
        tiles, own = pl.ds(0, 4 * (i + 1)), pl.ds(0, i + 1)
        return (
            push(buf_ref.at[i, tiles, 0, 0], z_ref.at[i, tiles], send.at[3], z_got.at[i], device),
            push(panel_ref.at[own, 0], z_ref.at[i, pl.ds(24, i + 1)], send.at[3], f_got.at[i], device),
        )

    def ring_copy(way, k, h):
        block = (r + 8 - k) % 8 if way == 0 else (r + k) % 8
        half = buf_ref.at[block, :, h]
        return push(half, half, send.at[5 + way], ring_got.at[way, 2 * k + h], at.line(1 if way == 0 else 7))

    def ring_wait(way, k, h):
        block = (r + 7 - k) % 8 if way == 0 else (r + 1 + k) % 8
        arrive(buf_ref.at[block, :, h], ring_got.at[way, 2 * k + h])

    hops = [(way, k, h) for k in range(4) for h in range(2) for way in range(2) if k < 3 or h == way]

    def ring_step(k):
        for hop in hops:
            if hop[1] == k:
                if k:
                    ring_wait(hop[0], k - 1, hop[2])
                ring_copy(*hop).start()

    arrive(buf_ref.at[r], got.at[0])
    arrive(panel_ref.at[:, 0], got.at[1])

    for i in range(NPIV):
        @pl.when(r == i)
        def _():
            tiles, own = pl.ds(0, 4 * (i + 1)), pl.ds(0, i + 1)
            pltpu.make_async_copy(buf_ref.at[i, tiles, 0, 0], z_ref.at[i, tiles], z_got.at[i]).start()
            pltpu.make_async_copy(panel_ref.at[own, 0], z_ref.at[i, pl.ds(24, i + 1)], f_got.at[i]).start()
            for d in (4, 3, 5, 2, 6, 1, 7):
                for copy in z_copies(i, d):
                    copy.start()

    @pl.when(has_front)
    def _():
        pltpu.make_async_copy(front_ref.at[pl.ds(1, 7), e], panel_ref.at[seat, pl.ds(1, 7)], got.at[4]).start()
        loop(1, 32, lambda d: rest_copy(d).start())

    ring_step(0)
    arrive(maps_ref, got.at[2])
    for i in range(NPIV):
        arrive(z_ref.at[i, pl.ds(0, 4 * (i + 1))], z_got.at[i])
        arrive(z_ref.at[i, pl.ds(24, i + 1)], f_got.at[i])

    for t, (i, j) in enumerate(TILES):
        acc_ref[t] = z_ref[i, 24 + j]

    def add_child(q):
        wanted = maps_ref[q][:NPIV]
        strips = []
        for j in range(NPIV):
            strip = None
            for seat_j in range(j + 1):
                pick = jnp.where(wanted[seat_j : seat_j + 1] == j, 1.0, 0.0)[None]
                term = z_ref[:, seat_j * 4 + q] * pick
                strip = term if strip is None else strip + term
            strips.append(strip)
        for j in range(NPIV):
            for i in range(j, NPIV):
                pick = jnp.where(wanted == i, 1.0, 0.0)[:, None, :]
                acc_ref[i * (i + 1) // 2 + j] += jnp.sum(strips[j] * pick, axis=0)

    loop(0, 4, add_child)

    own_k = pltpu.make_async_copy(acc_ref, k_ref.at[:, e], got.at[3])
    own_k.start()

    def k_copy(d):
        return push(acc_ref, k_ref.at[:, e], send.at[7], k_got.at[d], at.same_core(d)[1])

    def pair_copy(d):
        where_e = at.same_core(16 - d)[0]
        return push(k_ref.at[:, where_e], k_ref.at[:, where_e], send.at[8], p_got.at[d], at.partner)

    def forward(d):
        k_copy(d).wait_recv()
        pair_copy(d).start()

    loop(1, 16, lambda d: k_copy(d).start())
    ring_step(1)
    own_k.wait()
    pair_copy(0).start()
    ring_step(2)
    loop(1, 16, forward)
    ring_step(3)
    loop(0, 16, lambda d: pair_copy(d).wait())
    diagonal(first_ref, k_ref[0].reshape(BLK, BLK))
    arrive(panel_ref.at[:, pl.ds(1, 7)], got.at[4])
    ring_wait(0, 2, 1)
    ring_wait(1, 2, 0)
    ring_wait(0, 3, 0)
    ring_wait(1, 3, 1)

    loop(1, 16, lambda d: k_copy(d).wait_send())
    loop(1, 32, lambda d: child_copy(d).wait_send())

    @pl.when(has_front)
    def _():
        loop(1, 32, lambda d: front_copy(d).wait_send())
        loop(1, 32, lambda d: rest_copy(d).wait_send())

    for d in range(1, 4):
        map_copy(d).wait_send()
    for i in range(NPIV):
        @pl.when(r == i)
        def _():
            for d in range(1, 8):
                for copy in z_copies(i, d):
                    copy.wait_send()

    for hop in hops:
        ring_copy(*hop).wait_send()


def gather_all(child, front, child_map):
    dma = pltpu.SemaphoreType.DMA
    return pl.pallas_call(
        gather_kernel,
        out_shape=(
            jax.ShapeDtypeStruct((NTILE, 32, 4, BLK), jnp.float32),
            jax.ShapeDtypeStruct((4, 16, BLK), jnp.int32),
            jax.ShapeDtypeStruct((8, 32, 2, 2, 4, BLK), jnp.float32),
            jax.ShapeDtypeStruct((NPIV, 8, 4, BLK), jnp.float32),
            jax.ShapeDtypeStruct((BLK, 2 * BLK), jnp.float32),
        ),
        in_specs=[VM, pl.BlockSpec(memory_space=pltpu.HBM), SM],
        out_specs=(VM,) * 5,
        scratch_shapes=[
            pltpu.VMEM((32, 2, 2, 4, BLK), jnp.float32),
            pltpu.VMEM((1024, BLK), jnp.float32),
            pltpu.VMEM((8, 32, 4, BLK), jnp.float32),
            pltpu.VMEM((16, BLK), jnp.int32),
            pltpu.VMEM((NPIV, 30, 4, BLK), jnp.float32),
            pltpu.VMEM((NTILE, 4, BLK), jnp.float32),
            dma((9,)), dma((6,)), dma((NPIV,)), dma((NPIV,)), dma((16,)), dma((16,)), dma((2, 8)),
        ],
        compiler_params=pltpu.CompilerParams(collective_id=0, has_side_effects=True),
        name="gather_all",
    )(child, front, child_map)


def factor_kernel(
    k_ref, acc_ref, panel_ref, front_ref, first_ref, low_ref, inv_ref, rows_ref, moved_ref, top_ref,
    a_ref, m_ref, piece_ref, share_ref, w_ref, send, got, r_got, p_got, t_got,
):
    at = Place()
    r, c, s, e = at.r, at.c, at.s, at.e
    spot = jnp.minimum(r, NPIV - 1)

    def prepare():
        fetch = [pltpu.make_async_copy(acc_ref.at[4 * j, :, 0], piece_ref.at[j], got.at[2 + j]) for j in range(NPIV)]
        tiles = [
            pltpu.make_async_copy(
                k_ref.at[t], m_ref.at[pl.ds(i * BLK, BLK), pl.ds(j * BLK, BLK)], got.at[2 + NPIV + t]
            )
            for t, (i, j) in enumerate(TILES)
        ]
        for copy in fetch + tiles:
            copy.start()
        factor_begin(low_ref, m_ref)
        for copy in fetch:
            copy.wait()
        for j in range(NPIV):
            for slot in range(8):
                share_ref[slot, j] = piece_ref[j, slot] + panel_ref[j, slot]
        for copy in tiles:
            copy.wait()
        factor_finish(0, low_ref, inv_ref, first_ref, m_ref)

    at.greet(prepare)

    top_part, rest_part = pl.ds(0, 1), pl.ds(1, 7)

    def move_copy(d, part, k):
        p, device = at.plane(d)
        return push(acc_ref.at[p, part], moved_ref.at[part, :, e], send.at[4 * k], got.at[k * 29], device)

    def own_move(part, k):
        return pltpu.make_async_copy(acc_ref.at[e, part], moved_ref.at[part, :, e], got.at[k * 29])

    own_move(top_part, 0).start()
    loop(1, 32, lambda d: move_copy(d, top_part, 0).start())

    own_rows = pltpu.make_async_copy(share_ref, rows_ref.at[:, :, e], got.at[1])

    def rows_copy(d):
        return push(share_ref, rows_ref.at[:, :, e], send.at[1], r_got.at[d], at.same_core(d)[1])

    def pair_copy(d):
        where_e = at.same_core(16 - d)[0]
        return push(rows_ref.at[:, :, where_e], rows_ref.at[:, :, where_e], send.at[2], p_got.at[d], at.partner)

    def top_copy(d):
        return push(w_ref, top_ref.at[spot], send.at[3], t_got.at[spot], at.line(d))

    own_rows.start()
    loop(1, 16, lambda d: rows_copy(d).start())
    own_move(rest_part, 1).start()
    loop(1, 32, lambda d: move_copy(d, rest_part, 1).start())

    def after_first():
        own_rows.wait()
        pair_copy(0).start()
        arrive(moved_ref.at[top_part], got.at[0])

        @pl.when(r < NPIV)
        def _():
            for i in range(2):
                w_ref[i] = moved_ref[0, i] + front_ref[:BLK, i * BLK : (i + 1) * BLK].reshape(32, 4, BLK)
            pltpu.make_async_copy(w_ref, top_ref.at[spot], t_got.at[spot]).start()
            for d in (4, 3, 5, 2, 6, 1, 7):
                top_copy(d).start()

    def forward(d):
        rows_copy(d).wait_recv()
        pair_copy(d).start()

    def progress(b):
        pl.when(b == 2)(after_first)
        pl.when(b == 4)(lambda: loop(1, 16, forward))

    factor_steps(low_ref, inv_ref, a_ref, m_ref, progress)

    loop(0, 16, lambda d: pair_copy(d).wait())
    arrive(moved_ref.at[rest_part], got.at[29])
    for i in range(NPIV):
        arrive(top_ref.at[i], t_got.at[i])
    loop(1, 16, lambda d: rows_copy(d).wait_send())
    loop(1, 32, lambda d: move_copy(d, top_part, 0).wait_send())
    loop(1, 32, lambda d: move_copy(d, rest_part, 1).wait_send())

    @pl.when(r < NPIV)
    def _():
        for d in range(1, 8):
            top_copy(d).wait_send()


def factor_all(k, acc, panel, front, first):
    dma = pltpu.SemaphoreType.DMA
    f32 = lambda *shape: jax.ShapeDtypeStruct(shape, jnp.float32)
    return pl.pallas_call(
        factor_kernel,
        out_shape=(
            f32(PIV, PIV),
            f32(NPIV, BLK, BLK),
            f32(8, NPIV, 32, 4, BLK),
            f32(8, 2, 32, 4, BLK),
            f32(NPIV, 2, 32, 4, BLK),
        ),
        in_specs=[pl.BlockSpec(memory_space=pltpu.HBM)] * 2 + [VM] * 3,
        out_specs=(VM,) * 5,
        scratch_shapes=[
            pltpu.VMEM((BLK, 256), jnp.float32),
            pltpu.VMEM((PIV, PIV), jnp.float32),
            pltpu.VMEM((NPIV, 8, 4, BLK), jnp.float32),
            pltpu.VMEM((8, NPIV, 4, BLK), jnp.float32),
            pltpu.VMEM((2, 32, 4, BLK), jnp.float32),
            dma((5,)), dma((3 + NPIV + NTILE,)), dma((16,)), dma((16,)), dma((NPIV,)),
        ],
        compiler_params=pltpu.CompilerParams(collective_id=1, has_side_effects=True, vmem_limit_bytes=40 * 1024 * 1024),
        name="factor_all",
    )(k, acc, panel, front, first)


def place_kernel(map_ref, buf_ref, acc_ref):
    acc_ref[...] = jnp.zeros_like(acc_ref)
    row = lax.axis_index("row")

    for q in range(4):
        targets = [map_ref[q, j, 0] for j in range(16)]
        spots = [(j % 8 * 4 + j // 16, (j // 8) % 2) for j in targets]

        def child_row(block_row):
            i = map_ref[q, block_row, 0]

            @pl.when(i % 8 == row)
            def _():
                slot = i // 8
                for block_col, (dest, half) in enumerate(spots):
                    acc_ref[dest, slot, half] += buf_ref[
                        block_row % 8, block_col % 8 * 4 + q, block_row // 8, block_col // 8
                    ]

        loop(0, 16, child_row)


def place(maps, buf):
    return pl.pallas_call(
        place_kernel,
        out_shape=jax.ShapeDtypeStruct((32, 8, 2, 4, BLK), jnp.float32),
        in_specs=[SM, VM],
        out_specs=VM,
        name="place",
    )(maps, buf)


NT = ((1,), (1,))
NN = ((1,), (0,))


def four(a, b, c, d):
    return jnp.concatenate([jnp.concatenate([a, b], axis=1), jnp.concatenate([c, d], axis=1)], axis=0)


def schur_kernel(
    rows_ref, top_ref, moved_ref, front_ref, low_ref, inv_ref, out_ref,
    lh, ll, yh, yl, uh, ul, x_ref,
):
    row, col, sub = (lax.axis_index(a) for a in ("row", "col", "sub"))
    high, rest = split(low_ref[...])
    lh[...] = high
    ll[...] = rest
    zero = jnp.zeros((BLK, BLK), jnp.float32)
    for p in range(3):
        first, second = inv_ref[2 * p], inv_ref[2 * p + 1]
        at = 256 * p
        cross = jnp.dot(low_ref[at + BLK : at + 256, at : at + BLK], first, precision=HI)
        cross = -jnp.dot(second, cross, precision=HI)
        high, rest = split(four(first, zero, cross, second))
        yh[p] = high
        yl[p] = rest
    for p in range(3):
        at = 256 * p
        x = four(top_ref[2 * p, 0], top_ref[2 * p, 1], top_ref[2 * p + 1, 0], top_ref[2 * p + 1, 1])
        if p:
            x = x - dot3((lh[at : at + 256, :at], ll[at : at + 256, :at]), (uh[:at, :], ul[:at, :]), NN)
        high, rest = split(dot3((yh[p], yl[p]), split(x), NN))
        uh[at : at + 256, :] = high
        ul[at : at + 256, :] = rest

    def tile(t):
        here = pl.ds(pl.multiple_of(t * 256, 256), 256)
        a, b = 2 * t, 2 * t + 1
        acc = front_ref[here, :] + four(moved_ref[a, 0], moved_ref[a, 1], moved_ref[b, 0], moved_ref[b, 1])
        xs = []
        for p in range(3):
            at = 256 * p
            x = four(rows_ref[a, 2 * p], rows_ref[a, 2 * p + 1], rows_ref[b, 2 * p], rows_ref[b, 2 * p + 1])
            for m in range(p):
                cut = slice(256 * m, 256 * m + 256)
                x = x - dot3(xs[m], (lh[at : at + 256, cut], ll[at : at + 256, cut]), NT)
            x = dot3(split(x), (yh[p], yl[p]), NT)
            x_ref[here, at : at + 256] = x
            xs.append(split(x))
            acc = acc - dot3(xs[p], (uh[at : at + 256, :], ul[at : at + 256, :]), NN)
        out_ref[here, :] = acc

    loop(0, 4, tile)

    @pl.when(row < NPIV)
    def _():
        out_ref[:BLK, :] = jnp.zeros((BLK, 256), jnp.float32)
        x_ref[:BLK, :] = low_ref[pl.ds(pl.multiple_of(row * BLK, BLK), BLK), :]

    @pl.when((sub == 0) & (col < NPIV))
    def _():
        out_ref[:, :BLK] = x_ref[:, pl.ds(pl.multiple_of(col * BLK, BLK), BLK)]


def schur(rows, top, moved, front, low, inv):
    return pl.pallas_call(
        schur_kernel,
        out_shape=jax.ShapeDtypeStruct((1024, 256), jnp.float32),
        in_specs=[VM] * 6,
        out_specs=VM,
        scratch_shapes=[
            pltpu.VMEM((PIV, PIV), jnp.bfloat16),
            pltpu.VMEM((PIV, PIV), jnp.bfloat16),
            pltpu.VMEM((3, 256, 256), jnp.bfloat16),
            pltpu.VMEM((3, 256, 256), jnp.bfloat16),
            pltpu.VMEM((PIV, 256), jnp.bfloat16),
            pltpu.VMEM((PIV, 256), jnp.bfloat16),
            pltpu.VMEM((1024, PIV), jnp.float32),
        ],
        compiler_params=pltpu.CompilerParams(vmem_limit_bytes=32 * 1024 * 1024),
        name="schur",
    )(rows, top, moved, front, low, inv)


def body(front, child, child_map):
    k, maps, buf, panel, first = gather_all(child, front, child_map)
    acc = place(maps, buf)
    low, inv, rows, moved, top = factor_all(k.reshape(NTILE, BLK, BLK), acc, panel, front, first)
    return schur(
        rows.reshape(8, NPIV, BLK, BLK),
        top.reshape(NPIV, 2, BLK, BLK),
        moved.reshape(8, 2, BLK, BLK),
        front,
        low,
        inv,
    )


def solution(mesh):
    placed = (P("row", ("col", "sub")), P("sub", "row", "col"), P("sub", None))
    return jax.shard_map(
        body, mesh=mesh, in_specs=placed, out_specs=P("row", ("col", "sub")), check_vma=False
    )
```

```python
import jax
import jax.numpy as jnp
from jax import lax
from jax.experimental import pallas as pl
from jax.experimental.pallas import tpu as pltpu
from jax.sharding import PartitionSpec as P

BLK = 128
NPIV = 6
PIV = NPIV * BLK
PLANE = ("col", "sub")
HI = lax.Precision.HIGHEST
VM = pl.BlockSpec(memory_space=pltpu.VMEM)
SM = pl.BlockSpec(memory_space=pltpu.SMEM)


def nt(a, b, precision=HI):
    return lax.dot_general(a, b, (((1,), (1,)), ((), ())), precision=precision, preferred_element_type=jnp.float32)
def tn(a, b, precision=HI):
    return lax.dot_general(a, b, (((0,), (0,)), ((), ())), precision=precision, preferred_element_type=jnp.float32)

def split(x):
    high = x.astype(jnp.bfloat16)
    return high, (x - high.astype(jnp.float32)).astype(jnp.bfloat16)


def dot3(a, b, dims):
    def one(x, y):
        return lax.dot_general(x, y, (dims, ((), ())), preferred_element_type=jnp.float32)

    return one(a[0], b[0]) + (one(a[0], b[1]) + one(a[1], b[0]))


def tn3(a, b):
    return dot3(split(a), split(b), ((0,), (0,)))


def nt3(a, b):
    return dot3(split(a), split(b), ((1,), (1,)))


def rsqrt(x):
    return lax.rsqrt(x)

def wide(x):
    return jnp.concatenate([x, x], axis=1)

def eliminate(a_ref):
    sub = lax.broadcasted_iota(jnp.int32, (8, 256), 0)
    ahead = []
    for g in range(16):
        if g == 0:
            ahead = [a_ref[8 * h : 8 * h + 8, :] for h in range(2 + 1)]
        elif g + 2 < 16:
            ahead.append(a_ref[8 * (g + 2) : 8 * (g + 2) + 8, :])
        rows = ahead.pop(0)
        left = rows[:, :BLK]
        e = {}
        for j in range(8):
            c = jnp.broadcast_to(left[:, 8 * g + j : 8 * g + j + 1], (8, BLK))
            for i in range(j, 8):
                e[j, i] = jnp.broadcast_to(c[i : i + 1, :], (8, BLK))
        r = [jnp.broadcast_to(rows[i : i + 1, :], (8, 256)) for i in range(8)]
        cols = [[jnp.broadcast_to(n[:, 8 * g + j : 8 * g + j + 1], (8, BLK)) for j in range(8)] for n in ahead]
        out = None
        for j in range(8):
            s = rsqrt(e[j, j])
            u = {i: e[j, i] * s for i in range(j + 1, 8)}
            for i in range(j + 1, 8):
                for m in range(i, 8):
                    e[i, m] = e[i, m] - u[i] * u[m]
            rj = r[j] * wide(s)
            for i in range(j + 1, 8):
                r[i] = r[i] - wide(u[i]) * rj
            for h in range(len(ahead)):
                cj = cols[h][j] * s
                for m in range(j + 1, 8):
                    cols[h][m] = cols[h][m] - cj * u[m]
                ahead[h] = ahead[h] - wide(cj) * rj
            out = rj if out is None else jnp.where(sub == j, rj, out)
        a_ref[8 * g : 8 * g + 8, :] = out
        low = 8 * (g + 1 + 2)
        if low < BLK:
            t = tn3(out[:, :BLK], out)
            a_ref[low:, :] = a_ref[low:, :] - t[low:, :]

def factor_begin(l_ref, m_ref):
    for i in range(NPIV - 1):
        m_ref[i * BLK : (i + 1) * BLK, (i + 1) * BLK :] = jnp.zeros((BLK, PIV - (i + 1) * BLK), jnp.float32)
    l_ref[...] = jnp.zeros_like(l_ref)


def diagonal(a_ref, block):
    r_iota = lax.broadcasted_iota(jnp.int32, (BLK, BLK), 0)
    c_iota = lax.broadcasted_iota(jnp.int32, (BLK, BLK), 1)
    a_ref[:, :BLK] = block
    a_ref[:, BLK:] = jnp.where(r_iota == c_iota, 1.0, 0.0)
    eliminate(a_ref)


def factor_finish(b, l_ref, y_ref, a_ref, m_ref):
    r_iota = lax.broadcasted_iota(jnp.int32, (BLK, BLK), 0)
    c_iota = lax.broadcasted_iota(jnp.int32, (BLK, BLK), 1)
    at = pl.ds(b * BLK if isinstance(b, int) else pl.multiple_of(b * BLK, BLK), BLK)
    y = a_ref[:, BLK:]
    y_ref[b] = y
    l_ref[at, at] = jnp.where(r_iota >= c_iota, a_ref[:, :BLK].T, 0.0)

    def solve(i, c):
        rows = pl.ds(pl.multiple_of(i * BLK, BLK), BLK)
        l_ref[rows, at] = nt(m_ref[rows, at], y)
        return c

    lax.fori_loop(b + 1, NPIV, solve, 0)

    def update(i, c):
        rows = pl.ds(pl.multiple_of(i * BLK, BLK), BLK)
        m_ref[rows, :] = m_ref[rows, :] - nt3(l_ref[rows, at], l_ref[:, at])
        return c

    lax.fori_loop(b + 1, NPIV, update, 0)


def factor_steps(l_ref, y_ref, a_ref, m_ref, progress):
    def step(b, carry):
        progress(b)
        at = pl.ds(pl.multiple_of(b * BLK, BLK), BLK)
        diagonal(a_ref, m_ref[at, at])
        factor_finish(b, l_ref, y_ref, a_ref, m_ref)
        return carry

    lax.fori_loop(1, NPIV, step, 0)


MESH = pl.DeviceIdType.MESH
TILES = [(i, j) for i in range(NPIV) for j in range(i + 1)]
NTILE = len(TILES)


class Place:
    def __init__(self):
        self.r, self.c, self.s = (lax.axis_index(a) for a in ("row", "col", "sub"))
        self.e = self.c * 4 + self.s
        self.core = self.c % 2
        self.chip = (self.c // 2) * 4 + self.s
        self.partner = (self.r, self.c + 1 - 2 * self.core, self.s)

    def plane(self, d):
        p = (self.e + d) % 32
        return p, (self.r, p // 4, p % 4)

    def same_core(self, d):
        p = (self.chip + d) % 16
        c = (p // 4) * 2 + self.core
        return c * 4 + p % 4, (self.r, c, p % 4)

    def line(self, d):
        return ((self.r + d) % 8, self.c, self.s)

    def greet(self, meanwhile):
        barrier = pltpu.get_barrier_semaphore()

        def plane(d, carry):
            pl.semaphore_signal(barrier, inc=1, device_id=self.plane(d)[1], device_id_type=MESH)
            return carry

        def line(d, carry):
            pl.semaphore_signal(barrier, inc=1, device_id=self.line(d), device_id_type=MESH)
            return carry

        lax.fori_loop(1, 32, plane, 0)
        lax.fori_loop(1, 8, line, 0)
        meanwhile()
        pl.semaphore_wait(barrier, 38)


def push(src, dst, ssem, rsem, device):
    return pltpu.make_async_remote_copy(
        src_ref=src, dst_ref=dst, send_sem=ssem, recv_sem=rsem, device_id=device, device_id_type=MESH
    )


def arrive(ref, sem):
    pltpu.make_async_copy(ref, ref, sem).wait()


def loop(low, high, f):
    def one(d, carry):
        f(d)
        return carry

    lax.fori_loop(low, high, one, 0)


def gather_kernel(
    tile_ref, whole_ref, list_ref, k_ref, maps_ref, buf_ref, panel_ref, first_ref,
    child_ref, strip_ref, front_ref, map_ref, z_ref, acc_ref, send, got, z_got, f_got, k_got, p_got, ring_got,
):
    at = Place()
    r, c, s, e = at.r, at.c, at.s, at.e
    has_front = (c < NPIV) & (s == 0)

    def prepare():
        fetch = pltpu.make_async_copy(whole_ref.at[:, pl.ds(0, BLK)], strip_ref, got.at[5])
        fetch.start()
        for i in range(2):
            for j in range(2):
                child_ref[:, i, j] = tile_ref[0, i * BLK : (i + 1) * BLK, j * BLK : (j + 1) * BLK].reshape(32, 4, BLK)
        for i in range(16):
            map_ref[i : i + 1, :] = jnp.full((1, BLK), list_ref[0, i], jnp.int32)
        for i in range(NPIV - 1):
            z_ref[i, 4 * (i + 1) : 24] = jnp.zeros((20 - 4 * i, 4, BLK), jnp.float32)
        fetch.wait()

        @pl.when(has_front)
        def _():
            for i in range(8):
                front_ref[i] = strip_ref[i * BLK : (i + 1) * BLK, :].reshape(32, 4, BLK)

    at.greet(prepare)
    seat = jnp.minimum(c, NPIV - 1)

    def child_copy(d, h):
        p, device = at.plane(d)
        return push(child_ref.at[p, h], buf_ref.at[r, e, h], send.at[9 * h], got.at[6 * h], device)

    def own_child(h):
        return pltpu.make_async_copy(child_ref.at[e, h], buf_ref.at[r, e, h], got.at[6 * h])

    def front_copy(d):
        p, device = at.plane(d)
        return push(front_ref.at[0, p], panel_ref.at[seat, 0], send.at[1], got.at[1], device)

    def rest_copy(d):
        p, device = at.plane(d)
        return push(front_ref.at[pl.ds(1, 7), p], panel_ref.at[seat, pl.ds(1, 7)], send.at[4], got.at[4], device)

    def map_copy(d):
        return push(map_ref, maps_ref.at[s], send.at[2], got.at[2], (r, c, (s + d) % 4))

    own_child(0).start()
    own_child(1).start()
    pltpu.make_async_copy(map_ref, maps_ref.at[s], got.at[2]).start()
    loop(1, 32, lambda d: child_copy(d, 0).start())

    @pl.when(has_front)
    def _():
        pltpu.make_async_copy(front_ref.at[0, e], panel_ref.at[seat, 0], got.at[1]).start()
        loop(1, 32, lambda d: front_copy(d).start())

    for d in range(1, 4):
        map_copy(d).start()
    loop(1, 32, lambda d: child_copy(d, 1).start())

    def z_copies(i, d):
        device = at.line(d)
        tiles, own = pl.ds(0, 4 * (i + 1)), pl.ds(0, i + 1)
        return (
            push(buf_ref.at[i, tiles, 0, 0], z_ref.at[i, tiles], send.at[3], z_got.at[i], device),
            push(panel_ref.at[own, 0], z_ref.at[i, pl.ds(24, i + 1)], send.at[3], f_got.at[i], device),
        )

    def ring_copy(way, k, h):
        block = (r + 8 - k) % 8 if way == 0 else (r + k) % 8
        half = buf_ref.at[block, :, h]
        return push(half, half, send.at[5 + way], ring_got.at[way, 2 * k + h], at.line(1 if way == 0 else 7))

    def ring_wait(way, k, h):
        block = (r + 7 - k) % 8 if way == 0 else (r + 1 + k) % 8
        arrive(buf_ref.at[block, :, h], ring_got.at[way, 2 * k + h])

    hops = [(way, k, h) for k in range(4) for h in range(2) for way in range(2) if k < 3 or h == way]

    def ring_step(k):
        for hop in hops:
            if hop[1] == k:
                if k:
                    ring_wait(hop[0], k - 1, hop[2])
                elif hop == (0, 0, 1):
                    arrive(buf_ref.at[r, :, 1], got.at[6])
                ring_copy(*hop).start()

    arrive(buf_ref.at[r, :, 0], got.at[0])
    arrive(panel_ref.at[:, 0], got.at[1])

    for i in range(NPIV):
        @pl.when(r == i)
        def _():
            tiles, own = pl.ds(0, 4 * (i + 1)), pl.ds(0, i + 1)
            pltpu.make_async_copy(buf_ref.at[i, tiles, 0, 0], z_ref.at[i, tiles], z_got.at[i]).start()
            pltpu.make_async_copy(panel_ref.at[own, 0], z_ref.at[i, pl.ds(24, i + 1)], f_got.at[i]).start()
            for d in (4, 3, 5, 2, 6, 1, 7):
                for copy in z_copies(i, d):
                    copy.start()

    @pl.when(has_front)
    def _():
        pltpu.make_async_copy(front_ref.at[pl.ds(1, 7), e], panel_ref.at[seat, pl.ds(1, 7)], got.at[4]).start()
        loop(1, 32, lambda d: rest_copy(d).start())

    ring_step(0)
    arrive(maps_ref, got.at[2])
    for i in range(NPIV):
        arrive(z_ref.at[i, pl.ds(0, 4 * (i + 1))], z_got.at[i])
        arrive(z_ref.at[i, pl.ds(24, i + 1)], f_got.at[i])

    for t, (i, j) in enumerate(TILES):
        acc_ref[t] = z_ref[i, 24 + j]

    def add_child(q):
        wanted = maps_ref[q][:NPIV]
        strips = []
        for j in range(NPIV):
            strip = None
            for seat_j in range(j + 1):
                pick = jnp.where(wanted[seat_j : seat_j + 1] == j, 1.0, 0.0)[None]
                term = z_ref[:, seat_j * 4 + q] * pick
                strip = term if strip is None else strip + term
            strips.append(strip)
        for j in range(NPIV):
            for i in range(j, NPIV):
                pick = jnp.where(wanted == i, 1.0, 0.0)[:, None, :]
                acc_ref[i * (i + 1) // 2 + j] += jnp.sum(strips[j] * pick, axis=0)

    loop(0, 4, add_child)

    own_k = pltpu.make_async_copy(acc_ref, k_ref.at[:, e], got.at[3])
    own_k.start()

    def k_copy(d):
        return push(acc_ref, k_ref.at[:, e], send.at[7], k_got.at[d], at.same_core(d)[1])

    def pair_copy(d):
        where_e = at.same_core(16 - d)[0]
        return push(k_ref.at[:, where_e], k_ref.at[:, where_e], send.at[8], p_got.at[d], at.partner)

    def forward(d):
        k_copy(d).wait_recv()
        pair_copy(d).start()

    loop(1, 16, lambda d: k_copy(d).start())
    ring_step(1)
    own_k.wait()
    pair_copy(0).start()
    ring_step(2)
    loop(1, 16, forward)
    ring_step(3)
    loop(0, 16, lambda d: pair_copy(d).wait())
    diagonal(first_ref, k_ref[0].reshape(BLK, BLK))
    arrive(panel_ref.at[:, pl.ds(1, 7)], got.at[4])
    ring_wait(0, 2, 1)
    ring_wait(1, 2, 0)
    ring_wait(0, 3, 0)
    ring_wait(1, 3, 1)

    loop(1, 16, lambda d: k_copy(d).wait_send())
    loop(1, 32, lambda d: child_copy(d, 0).wait_send())
    loop(1, 32, lambda d: child_copy(d, 1).wait_send())

    @pl.when(has_front)
    def _():
        loop(1, 32, lambda d: front_copy(d).wait_send())
        loop(1, 32, lambda d: rest_copy(d).wait_send())

    for d in range(1, 4):
        map_copy(d).wait_send()
    for i in range(NPIV):
        @pl.when(r == i)
        def _():
            for d in range(1, 8):
                for copy in z_copies(i, d):
                    copy.wait_send()

    for hop in hops:
        ring_copy(*hop).wait_send()


def gather_all(child, front, child_map):
    dma = pltpu.SemaphoreType.DMA
    return pl.pallas_call(
        gather_kernel,
        out_shape=(
            jax.ShapeDtypeStruct((NTILE, 32, 4, BLK), jnp.float32),
            jax.ShapeDtypeStruct((4, 16, BLK), jnp.int32),
            jax.ShapeDtypeStruct((8, 32, 2, 2, 4, BLK), jnp.float32),
            jax.ShapeDtypeStruct((NPIV, 8, 4, BLK), jnp.float32),
            jax.ShapeDtypeStruct((BLK, 2 * BLK), jnp.float32),
        ),
        in_specs=[VM, pl.BlockSpec(memory_space=pltpu.HBM), SM],
        out_specs=(VM,) * 5,
        scratch_shapes=[
            pltpu.VMEM((32, 2, 2, 4, BLK), jnp.float32),
            pltpu.VMEM((1024, BLK), jnp.float32),
            pltpu.VMEM((8, 32, 4, BLK), jnp.float32),
            pltpu.VMEM((16, BLK), jnp.int32),
            pltpu.VMEM((NPIV, 30, 4, BLK), jnp.float32),
            pltpu.VMEM((NTILE, 4, BLK), jnp.float32),
            dma((10,)), dma((7,)), dma((NPIV,)), dma((NPIV,)), dma((16,)), dma((16,)), dma((2, 8)),
        ],
        compiler_params=pltpu.CompilerParams(collective_id=0, has_side_effects=True, vmem_limit_bytes=20 * 1024 * 1024),
        name="gather_all",
    )(child, front, child_map)


def factor_kernel(
    k_ref, acc_ref, panel_ref, front_ref, first_ref, low_ref, inv_ref, rows_ref, moved_ref, top_ref,
    a_ref, m_ref, piece_ref, share_ref, w_ref, send, got, r_got, p_got, t_got,
):
    at = Place()
    r, c, s, e = at.r, at.c, at.s, at.e
    spot = jnp.minimum(r, NPIV - 1)

    def prepare():
        fetch = [pltpu.make_async_copy(acc_ref.at[4 * j, :, 0], piece_ref.at[j], got.at[2 + j]) for j in range(NPIV)]
        tiles = [
            pltpu.make_async_copy(
                k_ref.at[t], m_ref.at[pl.ds(i * BLK, BLK), pl.ds(j * BLK, BLK)], got.at[2 + NPIV + t]
            )
            for t, (i, j) in enumerate(TILES)
        ]
        for copy in fetch + tiles:
            copy.start()
        factor_begin(low_ref, m_ref)
        for copy in fetch:
            copy.wait()
        for j in range(NPIV):
            for slot in range(8):
                share_ref[slot, j] = piece_ref[j, slot] + panel_ref[j, slot]
        for copy in tiles:
            copy.wait()
        factor_finish(0, low_ref, inv_ref, first_ref, m_ref)

    at.greet(prepare)

    top_part, rest_part = pl.ds(0, 1), pl.ds(1, 7)

    def move_copy(d, part, k):
        p, device = at.plane(d)
        return push(acc_ref.at[p, part], moved_ref.at[part, :, e], send.at[4 * k], got.at[k * 29], device)

    def own_move(part, k):
        return pltpu.make_async_copy(acc_ref.at[e, part], moved_ref.at[part, :, e], got.at[k * 29])

    own_move(top_part, 0).start()
    loop(1, 32, lambda d: move_copy(d, top_part, 0).start())

    own_rows = pltpu.make_async_copy(share_ref, rows_ref.at[:, :, e], got.at[1])

    def rows_copy(d):
        return push(share_ref, rows_ref.at[:, :, e], send.at[1], r_got.at[d], at.same_core(d)[1])

    def pair_copy(d):
        where_e = at.same_core(16 - d)[0]
        return push(rows_ref.at[:, :, where_e], rows_ref.at[:, :, where_e], send.at[2], p_got.at[d], at.partner)

    def top_copy(d):
        return push(w_ref, top_ref.at[spot], send.at[3], t_got.at[spot], at.line(d))

    own_rows.start()
    loop(1, 16, lambda d: rows_copy(d).start())
    own_move(rest_part, 1).start()
    loop(1, 32, lambda d: move_copy(d, rest_part, 1).start())

    def after_first():
        own_rows.wait()
        pair_copy(0).start()
        arrive(moved_ref.at[top_part], got.at[0])

        @pl.when(r < NPIV)
        def _():
            for i in range(2):
                w_ref[i] = moved_ref[0, i] + front_ref[:BLK, i * BLK : (i + 1) * BLK].reshape(32, 4, BLK)
            pltpu.make_async_copy(w_ref, top_ref.at[spot], t_got.at[spot]).start()
            for d in (4, 3, 5, 2, 6, 1, 7):
                top_copy(d).start()

    def forward(d):
        rows_copy(d).wait_recv()
        pair_copy(d).start()

    def progress(b):
        pl.when(b == 2)(after_first)
        pl.when(b == 4)(lambda: loop(1, 16, forward))

    factor_steps(low_ref, inv_ref, a_ref, m_ref, progress)

    loop(0, 16, lambda d: pair_copy(d).wait())
    arrive(moved_ref.at[rest_part], got.at[29])
    for i in range(NPIV):
        arrive(top_ref.at[i], t_got.at[i])
    loop(1, 16, lambda d: rows_copy(d).wait_send())
    loop(1, 32, lambda d: move_copy(d, top_part, 0).wait_send())
    loop(1, 32, lambda d: move_copy(d, rest_part, 1).wait_send())

    @pl.when(r < NPIV)
    def _():
        for d in range(1, 8):
            top_copy(d).wait_send()


def factor_all(k, acc, panel, front, first):
    dma = pltpu.SemaphoreType.DMA
    f32 = lambda *shape: jax.ShapeDtypeStruct(shape, jnp.float32)
    return pl.pallas_call(
        factor_kernel,
        out_shape=(
            f32(PIV, PIV),
            f32(NPIV, BLK, BLK),
            f32(8, NPIV, 32, 4, BLK),
            f32(8, 2, 32, 4, BLK),
            f32(NPIV, 2, 32, 4, BLK),
        ),
        in_specs=[pl.BlockSpec(memory_space=pltpu.HBM)] * 2 + [VM] * 3,
        out_specs=(VM,) * 5,
        scratch_shapes=[
            pltpu.VMEM((BLK, 256), jnp.float32),
            pltpu.VMEM((PIV, PIV), jnp.float32),
            pltpu.VMEM((NPIV, 8, 4, BLK), jnp.float32),
            pltpu.VMEM((8, NPIV, 4, BLK), jnp.float32),
            pltpu.VMEM((2, 32, 4, BLK), jnp.float32),
            dma((5,)), dma((3 + NPIV + NTILE,)), dma((16,)), dma((16,)), dma((NPIV,)),
        ],
        compiler_params=pltpu.CompilerParams(collective_id=1, has_side_effects=True, vmem_limit_bytes=40 * 1024 * 1024),
        name="factor_all",
    )(k, acc, panel, front, first)


def place_kernel(map_ref, buf_ref, acc_ref):
    acc_ref[...] = jnp.zeros_like(acc_ref)
    row = lax.axis_index("row")

    for q in range(4):
        targets = [map_ref[q, j, 0] for j in range(16)]
        spots = [(j % 8 * 4 + j // 16, (j // 8) % 2) for j in targets]

        def child_row(block_row):
            i = map_ref[q, block_row, 0]

            @pl.when(i % 8 == row)
            def _():
                slot = i // 8
                for block_col, (dest, half) in enumerate(spots):
                    acc_ref[dest, slot, half] += buf_ref[
                        block_row % 8, block_col % 8 * 4 + q, block_row // 8, block_col // 8
                    ]

        loop(0, 16, child_row)


def place(maps, buf):
    return pl.pallas_call(
        place_kernel,
        out_shape=jax.ShapeDtypeStruct((32, 8, 2, 4, BLK), jnp.float32),
        in_specs=[SM, VM],
        out_specs=VM,
        compiler_params=pltpu.CompilerParams(vmem_limit_bytes=8 * 1024 * 1024),
        name="place",
    )(maps, buf)


NT = ((1,), (1,))
NN = ((1,), (0,))


def four(a, b, c, d):
    return jnp.concatenate([jnp.concatenate([a, b], axis=1), jnp.concatenate([c, d], axis=1)], axis=0)


def schur_kernel(
    rows_ref, top_ref, moved_ref, front_ref, low_ref, inv_ref, out_ref,
    lh, ll, yh, yl, uh, ul, x_ref,
):
    row, col, sub = (lax.axis_index(a) for a in ("row", "col", "sub"))
    high, rest = split(low_ref[...])
    lh[...] = high
    ll[...] = rest
    zero = jnp.zeros((BLK, BLK), jnp.float32)
    for p in range(3):
        first, second = inv_ref[2 * p], inv_ref[2 * p + 1]
        at = 256 * p
        cross = jnp.dot(low_ref[at + BLK : at + 256, at : at + BLK], first, precision=HI)
        cross = -jnp.dot(second, cross, precision=HI)
        high, rest = split(four(first, zero, cross, second))
        yh[p] = high
        yl[p] = rest
    for p in range(3):
        at = 256 * p
        x = four(top_ref[2 * p, 0], top_ref[2 * p, 1], top_ref[2 * p + 1, 0], top_ref[2 * p + 1, 1])
        if p:
            x = x - dot3((lh[at : at + 256, :at], ll[at : at + 256, :at]), (uh[:at, :], ul[:at, :]), NN)
        high, rest = split(dot3((yh[p], yl[p]), split(x), NN))
        uh[at : at + 256, :] = high
        ul[at : at + 256, :] = rest

    def stack(get):
        return jnp.concatenate([jnp.concatenate([get(i, 0), get(i, 1)], axis=1) for i in range(8)], axis=0)

    acc = front_ref[...] + stack(lambda i, j: moved_ref[i, j])
    xs = []
    for p in range(3):
        at = 256 * p
        x = stack(lambda i, j: rows_ref[i, 2 * p + j])
        for m in range(p):
            cut = slice(256 * m, 256 * m + 256)
            x = x - dot3(xs[m], (lh[at : at + 256, cut], ll[at : at + 256, cut]), NT)
        x = dot3(split(x), (yh[p], yl[p]), NT)
        x_ref[:, at : at + 256] = x
        xs.append(split(x))
        acc = acc - dot3(xs[p], (uh[at : at + 256, :], ul[at : at + 256, :]), NN)
    out_ref[...] = acc

    @pl.when(row < NPIV)
    def _():
        out_ref[:BLK, :] = jnp.zeros((BLK, 256), jnp.float32)
        x_ref[:BLK, :] = low_ref[pl.ds(pl.multiple_of(row * BLK, BLK), BLK), :]

    @pl.when((sub == 0) & (col < NPIV))
    def _():
        out_ref[:, :BLK] = x_ref[:, pl.ds(pl.multiple_of(col * BLK, BLK), BLK)]


def schur(rows, top, moved, front, low, inv):
    return pl.pallas_call(
        schur_kernel,
        out_shape=jax.ShapeDtypeStruct((1024, 256), jnp.float32),
        in_specs=[VM] * 6,
        out_specs=VM,
        scratch_shapes=[
            pltpu.VMEM((PIV, PIV), jnp.bfloat16),
            pltpu.VMEM((PIV, PIV), jnp.bfloat16),
            pltpu.VMEM((3, 256, 256), jnp.bfloat16),
            pltpu.VMEM((3, 256, 256), jnp.bfloat16),
            pltpu.VMEM((PIV, 256), jnp.bfloat16),
            pltpu.VMEM((PIV, 256), jnp.bfloat16),
            pltpu.VMEM((1024, PIV), jnp.float32),
        ],
        compiler_params=pltpu.CompilerParams(vmem_limit_bytes=32 * 1024 * 1024),
        name="schur",
    )(rows, top, moved, front, low, inv)


def body(front, child, child_map):
    k, maps, buf, panel, first = gather_all(child, front, child_map)
    acc = place(maps, buf)
    low, inv, rows, moved, top = factor_all(k.reshape(NTILE, BLK, BLK), acc, panel, front, first)
    return schur(
        rows.reshape(8, NPIV, BLK, BLK),
        top.reshape(NPIV, 2, BLK, BLK),
        moved.reshape(8, 2, BLK, BLK),
        front,
        low,
        inv,
    )


def solution(mesh):
    placed = (P("row", ("col", "sub")), P("sub", "row", "col"), P("sub", None))
    return jax.shard_map(
        body, mesh=mesh, in_specs=placed, out_specs=P("row", ("col", "sub")), check_vma=False
    )
```

```python
import jax
import jax.numpy as jnp
from jax import lax
from jax.experimental import pallas as pl
from jax.experimental.pallas import tpu as pltpu
from jax.sharding import PartitionSpec as P

BLK = 128
NPIV = 6
PIV = NPIV * BLK
PLANE = ("col", "sub")
HI = lax.Precision.HIGHEST
VM = pl.BlockSpec(memory_space=pltpu.VMEM)
SM = pl.BlockSpec(memory_space=pltpu.SMEM)


def nt(a, b, precision=HI):
    return lax.dot_general(a, b, (((1,), (1,)), ((), ())), precision=precision, preferred_element_type=jnp.float32)
def tn(a, b, precision=HI):
    return lax.dot_general(a, b, (((0,), (0,)), ((), ())), precision=precision, preferred_element_type=jnp.float32)

def split(x):
    high = x.astype(jnp.bfloat16)
    return high, (x - high.astype(jnp.float32)).astype(jnp.bfloat16)


def dot3(a, b, dims):
    def one(x, y):
        return lax.dot_general(x, y, (dims, ((), ())), preferred_element_type=jnp.float32)

    return one(a[0], b[0]) + (one(a[0], b[1]) + one(a[1], b[0]))


def tn3(a, b):
    return dot3(split(a), split(b), ((0,), (0,)))


def nt3(a, b):
    return dot3(split(a), split(b), ((1,), (1,)))


def rsqrt(x):
    return lax.rsqrt(x)

def wide(x):
    return jnp.concatenate([x, x], axis=1)

def eliminate(a_ref):
    sub = lax.broadcasted_iota(jnp.int32, (8, 256), 0)
    ahead = []
    for g in range(16):
        if g == 0:
            ahead = [a_ref[8 * h : 8 * h + 8, :] for h in range(2 + 1)]
        elif g + 2 < 16:
            ahead.append(a_ref[8 * (g + 2) : 8 * (g + 2) + 8, :])
        rows = ahead.pop(0)
        left = rows[:, :BLK]
        e = {}
        for j in range(8):
            c = jnp.broadcast_to(left[:, 8 * g + j : 8 * g + j + 1], (8, BLK))
            for i in range(j, 8):
                e[j, i] = jnp.broadcast_to(c[i : i + 1, :], (8, BLK))
        r = [jnp.broadcast_to(rows[i : i + 1, :], (8, 256)) for i in range(8)]
        cols = [[jnp.broadcast_to(n[:, 8 * g + j : 8 * g + j + 1], (8, BLK)) for j in range(8)] for n in ahead]
        out = None
        for j in range(8):
            s = rsqrt(e[j, j])
            u = {i: e[j, i] * s for i in range(j + 1, 8)}
            for i in range(j + 1, 8):
                for m in range(i, 8):
                    e[i, m] = e[i, m] - u[i] * u[m]
            rj = r[j] * wide(s)
            for i in range(j + 1, 8):
                r[i] = r[i] - wide(u[i]) * rj
            for h in range(len(ahead)):
                cj = cols[h][j] * s
                for m in range(j + 1, 8):
                    cols[h][m] = cols[h][m] - cj * u[m]
                ahead[h] = ahead[h] - wide(cj) * rj
            out = rj if out is None else jnp.where(sub == j, rj, out)
        a_ref[8 * g : 8 * g + 8, :] = out
        low = 8 * (g + 1 + 2)
        if low < BLK:
            t = tn3(out[:, :BLK], out)
            a_ref[low:, :] = a_ref[low:, :] - t[low:, :]

def factor_begin(l_ref, m_ref):
    for i in range(NPIV - 1):
        m_ref[i * BLK : (i + 1) * BLK, (i + 1) * BLK :] = jnp.zeros((BLK, PIV - (i + 1) * BLK), jnp.float32)
    l_ref[...] = jnp.zeros_like(l_ref)


def diagonal(a_ref, block):
    r_iota = lax.broadcasted_iota(jnp.int32, (BLK, BLK), 0)
    c_iota = lax.broadcasted_iota(jnp.int32, (BLK, BLK), 1)
    a_ref[:, :BLK] = block
    a_ref[:, BLK:] = jnp.where(r_iota == c_iota, 1.0, 0.0)
    eliminate(a_ref)


def factor_finish(b, l_ref, y_ref, a_ref, m_ref):
    r_iota = lax.broadcasted_iota(jnp.int32, (BLK, BLK), 0)
    c_iota = lax.broadcasted_iota(jnp.int32, (BLK, BLK), 1)
    at = pl.ds(b * BLK if isinstance(b, int) else pl.multiple_of(b * BLK, BLK), BLK)
    y = a_ref[:, BLK:]
    y_ref[b] = y
    l_ref[at, at] = jnp.where(r_iota >= c_iota, a_ref[:, :BLK].T, 0.0)

    def solve(i, c):
        rows = pl.ds(pl.multiple_of(i * BLK, BLK), BLK)
        l_ref[rows, at] = nt3(m_ref[rows, at], y)
        return c

    lax.fori_loop(b + 1, NPIV, solve, 0)

    def update(i, c):
        rows = pl.ds(pl.multiple_of(i * BLK, BLK), BLK)
        m_ref[rows, :] = m_ref[rows, :] - nt3(l_ref[rows, at], l_ref[:, at])
        return c

    lax.fori_loop(b + 1, NPIV, update, 0)


def factor_steps(l_ref, y_ref, a_ref, m_ref, progress):
    def step(b, carry):
        progress(b)
        at = pl.ds(pl.multiple_of(b * BLK, BLK), BLK)
        diagonal(a_ref, m_ref[at, at])
        factor_finish(b, l_ref, y_ref, a_ref, m_ref)
        return carry

    lax.fori_loop(1, NPIV, step, 0)


MESH = pl.DeviceIdType.MESH
TILES = [(i, j) for i in range(NPIV) for j in range(i + 1)]
NTILE = len(TILES)


class Place:
    def __init__(self):
        self.r, self.c, self.s = (lax.axis_index(a) for a in ("row", "col", "sub"))
        self.e = self.c * 4 + self.s
        self.core = self.c % 2
        self.chip = (self.c // 2) * 4 + self.s
        self.partner = (self.r, self.c + 1 - 2 * self.core, self.s)

    def plane(self, d):
        p = (self.e + d) % 32
        return p, (self.r, p // 4, p % 4)

    def same_core(self, d):
        p = (self.chip + d) % 16
        c = (p // 4) * 2 + self.core
        return c * 4 + p % 4, (self.r, c, p % 4)

    def line(self, d):
        return ((self.r + d) % 8, self.c, self.s)

    def greet(self, meanwhile):
        barrier = pltpu.get_barrier_semaphore()

        def plane(d, carry):
            pl.semaphore_signal(barrier, inc=1, device_id=self.plane(d)[1], device_id_type=MESH)
            return carry

        def line(d, carry):
            pl.semaphore_signal(barrier, inc=1, device_id=self.line(d), device_id_type=MESH)
            return carry

        lax.fori_loop(1, 32, plane, 0)
        lax.fori_loop(1, 8, line, 0)
        meanwhile()
        pl.semaphore_wait(barrier, 38)


def push(src, dst, ssem, rsem, device):
    return pltpu.make_async_remote_copy(
        src_ref=src, dst_ref=dst, send_sem=ssem, recv_sem=rsem, device_id=device, device_id_type=MESH
    )


def arrive(ref, sem):
    pltpu.make_async_copy(ref, ref, sem).wait()


def loop(low, high, f):
    def one(d, carry):
        f(d)
        return carry

    lax.fori_loop(low, high, one, 0)


def gather_kernel(
    child_hbm, whole_ref, list_ref, k_ref, maps_ref, buf_ref, panel_ref, first_ref,
    tile_ref, child_ref, strip_ref, front_ref, map_ref, z_ref, acc_ref, send, got, z_got, f_got, k_got, p_got, ring_got,
):
    at = Place()
    r, c, s, e = at.r, at.c, at.s, at.e
    has_front = (c < NPIV) & (s == 0)

    def prepare():
        fetch = pltpu.make_async_copy(whole_ref.at[:, pl.ds(0, BLK)], strip_ref, got.at[5])
        fetch.start()
        child_fetch = pltpu.make_async_copy(child_hbm.at[0], tile_ref, got.at[7])
        child_fetch.start()
        for i in range(16):
            map_ref[i : i + 1, :] = jnp.full((1, BLK), list_ref[0, i], jnp.int32)
        for i in range(NPIV - 1):
            z_ref[i, 4 * (i + 1) : 24] = jnp.zeros((20 - 4 * i, 4, BLK), jnp.float32)
        child_fetch.wait()
        for i in range(2):
            for j in range(2):
                child_ref[:, i, j] = tile_ref[i * BLK : (i + 1) * BLK, j * BLK : (j + 1) * BLK].reshape(32, 4, BLK)
        fetch.wait()

        @pl.when(has_front)
        def _():
            for i in range(8):
                front_ref[i] = strip_ref[i * BLK : (i + 1) * BLK, :].reshape(32, 4, BLK)

    at.greet(prepare)
    seat = jnp.minimum(c, NPIV - 1)

    def child_copy(d, h):
        p, device = at.plane(d)
        return push(child_ref.at[p, h], buf_ref.at[r, e, h], send.at[9 * h], got.at[6 * h], device)

    def own_child(h):
        return pltpu.make_async_copy(child_ref.at[e, h], buf_ref.at[r, e, h], got.at[6 * h])

    def front_copy(d):
        p, device = at.plane(d)
        return push(front_ref.at[0, p], panel_ref.at[seat, 0], send.at[1], got.at[1], device)

    def rest_copy(d):
        p, device = at.plane(d)
        return push(front_ref.at[pl.ds(1, 7), p], panel_ref.at[seat, pl.ds(1, 7)], send.at[4], got.at[4], device)

    def map_copy(d):
        return push(map_ref, maps_ref.at[s], send.at[2], got.at[2], (r, c, (s + d) % 4))

    own_child(0).start()
    own_child(1).start()
    pltpu.make_async_copy(map_ref, maps_ref.at[s], got.at[2]).start()
    loop(1, 32, lambda d: child_copy(d, 0).start())

    @pl.when(has_front)
    def _():
        pltpu.make_async_copy(front_ref.at[0, e], panel_ref.at[seat, 0], got.at[1]).start()
        loop(1, 32, lambda d: front_copy(d).start())

    for d in range(1, 4):
        map_copy(d).start()
    loop(1, 32, lambda d: child_copy(d, 1).start())

    def z_copies(i, d):
        device = at.line(d)
        tiles, own = pl.ds(0, 4 * (i + 1)), pl.ds(0, i + 1)
        return (
            push(buf_ref.at[i, tiles, 0, 0], z_ref.at[i, tiles], send.at[3], z_got.at[i], device),
            push(panel_ref.at[own, 0], z_ref.at[i, pl.ds(24, i + 1)], send.at[3], f_got.at[i], device),
        )

    def ring_copy(way, k, h):
        block = (r + 8 - k) % 8 if way == 0 else (r + k) % 8
        half = buf_ref.at[block, :, h]
        return push(half, half, send.at[5 + way], ring_got.at[way, 2 * k + h], at.line(1 if way == 0 else 7))

    def ring_wait(way, k, h):
        block = (r + 7 - k) % 8 if way == 0 else (r + 1 + k) % 8
        arrive(buf_ref.at[block, :, h], ring_got.at[way, 2 * k + h])

    hops = [(way, k, h) for k in range(4) for h in range(2) for way in range(2) if k < 3 or h == way]

    def ring_step(k):
        for hop in hops:
            if hop[1] == k:
                if k:
                    ring_wait(hop[0], k - 1, hop[2])
                elif hop == (0, 0, 1):
                    arrive(buf_ref.at[r, :, 1], got.at[6])
                ring_copy(*hop).start()

    arrive(buf_ref.at[r, :, 0], got.at[0])
    arrive(panel_ref.at[:, 0], got.at[1])

    for i in range(NPIV):
        @pl.when(r == i)
        def _():
            tiles, own = pl.ds(0, 4 * (i + 1)), pl.ds(0, i + 1)
            pltpu.make_async_copy(buf_ref.at[i, tiles, 0, 0], z_ref.at[i, tiles], z_got.at[i]).start()
            pltpu.make_async_copy(panel_ref.at[own, 0], z_ref.at[i, pl.ds(24, i + 1)], f_got.at[i]).start()
            for d in (4, 3, 5, 2, 6, 1, 7):
                for copy in z_copies(i, d):
                    copy.start()

    @pl.when(has_front)
    def _():
        pltpu.make_async_copy(front_ref.at[pl.ds(1, 7), e], panel_ref.at[seat, pl.ds(1, 7)], got.at[4]).start()
        loop(1, 32, lambda d: rest_copy(d).start())

    ring_step(0)
    arrive(maps_ref, got.at[2])
    for i in range(NPIV):
        arrive(z_ref.at[i, pl.ds(0, 4 * (i + 1))], z_got.at[i])
        arrive(z_ref.at[i, pl.ds(24, i + 1)], f_got.at[i])

    for t, (i, j) in enumerate(TILES):
        acc_ref[t] = z_ref[i, 24 + j]

    def add_child(q):
        wanted = maps_ref[q][:NPIV]
        strips = []
        for j in range(NPIV):
            strip = None
            for seat_j in range(j + 1):
                pick = jnp.where(wanted[seat_j : seat_j + 1] == j, 1.0, 0.0)[None]
                term = z_ref[:, seat_j * 4 + q] * pick
                strip = term if strip is None else strip + term
            strips.append(strip)
        for j in range(NPIV):
            for i in range(j, NPIV):
                pick = jnp.where(wanted == i, 1.0, 0.0)[:, None, :]
                acc_ref[i * (i + 1) // 2 + j] += jnp.sum(strips[j] * pick, axis=0)

    loop(0, 4, add_child)

    own_k = pltpu.make_async_copy(acc_ref, k_ref.at[:, e], got.at[3])
    own_k.start()

    def k_copy(d):
        return push(acc_ref, k_ref.at[:, e], send.at[7], k_got.at[d], at.same_core(d)[1])

    def pair_copy(d):
        where_e = at.same_core(16 - d)[0]
        return push(k_ref.at[:, where_e], k_ref.at[:, where_e], send.at[8], p_got.at[d], at.partner)

    def forward(d):
        k_copy(d).wait_recv()
        pair_copy(d).start()

    loop(1, 16, lambda d: k_copy(d).start())
    ring_step(1)
    own_k.wait()
    pair_copy(0).start()
    ring_step(2)
    loop(1, 16, forward)
    ring_step(3)
    loop(0, 16, lambda d: pair_copy(d).wait())
    diagonal(first_ref, k_ref[0].reshape(BLK, BLK))
    arrive(panel_ref.at[:, pl.ds(1, 7)], got.at[4])
    ring_wait(0, 2, 1)
    ring_wait(1, 2, 0)
    ring_wait(0, 3, 0)
    ring_wait(1, 3, 1)

    loop(1, 16, lambda d: k_copy(d).wait_send())
    loop(1, 32, lambda d: child_copy(d, 0).wait_send())
    loop(1, 32, lambda d: child_copy(d, 1).wait_send())

    @pl.when(has_front)
    def _():
        loop(1, 32, lambda d: front_copy(d).wait_send())
        loop(1, 32, lambda d: rest_copy(d).wait_send())

    for d in range(1, 4):
        map_copy(d).wait_send()
    for i in range(NPIV):
        @pl.when(r == i)
        def _():
            for d in range(1, 8):
                for copy in z_copies(i, d):
                    copy.wait_send()

    for hop in hops:
        ring_copy(*hop).wait_send()


def gather_all(child, front, child_map):
    dma = pltpu.SemaphoreType.DMA
    return pl.pallas_call(
        gather_kernel,
        out_shape=(
            jax.ShapeDtypeStruct((NTILE, 32, 4, BLK), jnp.float32),
            jax.ShapeDtypeStruct((4, 16, BLK), jnp.int32),
            jax.ShapeDtypeStruct((8, 32, 2, 2, 4, BLK), jnp.float32),
            jax.ShapeDtypeStruct((NPIV, 8, 4, BLK), jnp.float32),
            jax.ShapeDtypeStruct((BLK, 2 * BLK), jnp.float32),
        ),
        in_specs=[pl.BlockSpec(memory_space=pltpu.HBM)] * 2 + [SM],
        out_specs=(VM,) * 5,
        scratch_shapes=[
            pltpu.VMEM((256, 256), jnp.float32),
            pltpu.VMEM((32, 2, 2, 4, BLK), jnp.float32),
            pltpu.VMEM((1024, BLK), jnp.float32),
            pltpu.VMEM((8, 32, 4, BLK), jnp.float32),
            pltpu.VMEM((16, BLK), jnp.int32),
            pltpu.VMEM((NPIV, 30, 4, BLK), jnp.float32),
            pltpu.VMEM((NTILE, 4, BLK), jnp.float32),
            dma((10,)), dma((8,)), dma((NPIV,)), dma((NPIV,)), dma((16,)), dma((16,)), dma((2, 8)),
        ],
        compiler_params=pltpu.CompilerParams(collective_id=0, has_side_effects=True, vmem_limit_bytes=20 * 1024 * 1024),
        name="gather_all",
    )(child, front, child_map)


def factor_kernel(
    k_ref, acc_ref, panel_ref, front_ref, first_ref, low_ref, inv_ref, rows_ref, moved_ref, top_ref,
    a_ref, m_ref, piece_ref, share_ref, w_ref, send, got, r_got, p_got, t_got,
):
    at = Place()
    r, c, s, e = at.r, at.c, at.s, at.e
    spot = jnp.minimum(r, NPIV - 1)

    def prepare():
        fetch = [pltpu.make_async_copy(acc_ref.at[4 * j, :, 0], piece_ref.at[j], got.at[2 + j]) for j in range(NPIV)]
        tiles = [
            pltpu.make_async_copy(
                k_ref.at[t], m_ref.at[pl.ds(i * BLK, BLK), pl.ds(j * BLK, BLK)], got.at[2 + NPIV + t]
            )
            for t, (i, j) in enumerate(TILES)
        ]
        for copy in fetch + tiles:
            copy.start()
        factor_begin(low_ref, m_ref)
        for copy in fetch:
            copy.wait()
        for j in range(NPIV):
            for slot in range(8):
                share_ref[slot, j] = piece_ref[j, slot] + panel_ref[j, slot]
        for copy in tiles:
            copy.wait()
        factor_finish(0, low_ref, inv_ref, first_ref, m_ref)

    at.greet(prepare)

    top_part, rest_part = pl.ds(0, 1), pl.ds(1, 7)

    def move_copy(d, part, k):
        p, device = at.plane(d)
        return push(acc_ref.at[p, part], moved_ref.at[part, :, e], send.at[4 * k], got.at[k * 29], device)

    def own_move(part, k):
        return pltpu.make_async_copy(acc_ref.at[e, part], moved_ref.at[part, :, e], got.at[k * 29])

    own_move(top_part, 0).start()
    loop(1, 32, lambda d: move_copy(d, top_part, 0).start())

    own_rows = pltpu.make_async_copy(share_ref, rows_ref.at[:, :, e], got.at[1])

    def rows_copy(d):
        return push(share_ref, rows_ref.at[:, :, e], send.at[1], r_got.at[d], at.same_core(d)[1])

    def pair_copy(d):
        where_e = at.same_core(16 - d)[0]
        return push(rows_ref.at[:, :, where_e], rows_ref.at[:, :, where_e], send.at[2], p_got.at[d], at.partner)

    def top_copy(d):
        return push(w_ref, top_ref.at[spot], send.at[3], t_got.at[spot], at.line(d))

    own_rows.start()
    loop(1, 16, lambda d: rows_copy(d).start())
    own_move(rest_part, 1).start()
    loop(1, 32, lambda d: move_copy(d, rest_part, 1).start())

    def after_first():
        own_rows.wait()
        pair_copy(0).start()
        arrive(moved_ref.at[top_part], got.at[0])

        @pl.when(r < NPIV)
        def _():
            for i in range(2):
                w_ref[i] = moved_ref[0, i] + front_ref[:BLK, i * BLK : (i + 1) * BLK].reshape(32, 4, BLK)
            pltpu.make_async_copy(w_ref, top_ref.at[spot], t_got.at[spot]).start()
            for d in (4, 3, 5, 2, 6, 1, 7):
                top_copy(d).start()

    def forward(d):
        rows_copy(d).wait_recv()
        pair_copy(d).start()

    def progress(b):
        pl.when(b == 2)(after_first)
        pl.when(b == 4)(lambda: loop(1, 16, forward))

    factor_steps(low_ref, inv_ref, a_ref, m_ref, progress)

    loop(0, 16, lambda d: pair_copy(d).wait())
    arrive(moved_ref.at[rest_part], got.at[29])
    for i in range(NPIV):
        arrive(top_ref.at[i], t_got.at[i])
    loop(1, 16, lambda d: rows_copy(d).wait_send())
    loop(1, 32, lambda d: move_copy(d, top_part, 0).wait_send())
    loop(1, 32, lambda d: move_copy(d, rest_part, 1).wait_send())

    @pl.when(r < NPIV)
    def _():
        for d in range(1, 8):
            top_copy(d).wait_send()


def factor_all(k, acc, panel, front, first):
    dma = pltpu.SemaphoreType.DMA
    f32 = lambda *shape: jax.ShapeDtypeStruct(shape, jnp.float32)
    return pl.pallas_call(
        factor_kernel,
        out_shape=(
            f32(PIV, PIV),
            f32(NPIV, BLK, BLK),
            f32(8, NPIV, 32, 4, BLK),
            f32(8, 2, 32, 4, BLK),
            f32(NPIV, 2, 32, 4, BLK),
        ),
        in_specs=[pl.BlockSpec(memory_space=pltpu.HBM)] * 2 + [VM] * 3,
        out_specs=(VM,) * 5,
        scratch_shapes=[
            pltpu.VMEM((BLK, 256), jnp.float32),
            pltpu.VMEM((PIV, PIV), jnp.float32),
            pltpu.VMEM((NPIV, 8, 4, BLK), jnp.float32),
            pltpu.VMEM((8, NPIV, 4, BLK), jnp.float32),
            pltpu.VMEM((2, 32, 4, BLK), jnp.float32),
            dma((5,)), dma((3 + NPIV + NTILE,)), dma((16,)), dma((16,)), dma((NPIV,)),
        ],
        compiler_params=pltpu.CompilerParams(collective_id=1, has_side_effects=True, vmem_limit_bytes=40 * 1024 * 1024),
        name="factor_all",
    )(k, acc, panel, front, first)


def place_kernel(map_ref, buf_ref, acc_ref):
    acc_ref[...] = jnp.zeros_like(acc_ref)
    row = lax.axis_index("row")

    for q in range(4):
        targets = [map_ref[q, j, 0] for j in range(16)]
        spots = [(j % 8 * 4 + j // 16, (j // 8) % 2) for j in targets]

        def child_row(block_row):
            i = map_ref[q, block_row, 0]

            @pl.when(i % 8 == row)
            def _():
                slot = i // 8
                for block_col, (dest, half) in enumerate(spots):
                    acc_ref[dest, slot, half] += buf_ref[
                        block_row % 8, block_col % 8 * 4 + q, block_row // 8, block_col // 8
                    ]

        loop(0, 16, child_row)


def place(maps, buf):
    return pl.pallas_call(
        place_kernel,
        out_shape=jax.ShapeDtypeStruct((32, 8, 2, 4, BLK), jnp.float32),
        in_specs=[SM, VM],
        out_specs=VM,
        compiler_params=pltpu.CompilerParams(vmem_limit_bytes=8 * 1024 * 1024),
        name="place",
    )(maps, buf)


NT = ((1,), (1,))
NN = ((1,), (0,))


def four(a, b, c, d):
    return jnp.concatenate([jnp.concatenate([a, b], axis=1), jnp.concatenate([c, d], axis=1)], axis=0)


def schur_kernel(
    rows_ref, top_ref, moved_ref, front_ref, low_ref, inv_ref, out_ref,
    lh, ll, yh, yl, uh, ul, x_ref,
):
    row, col, sub = (lax.axis_index(a) for a in ("row", "col", "sub"))
    high, rest = split(low_ref[...])
    lh[...] = high
    ll[...] = rest
    zero = jnp.zeros((BLK, BLK), jnp.float32)
    for p in range(3):
        first, second = inv_ref[2 * p], inv_ref[2 * p + 1]
        at = 256 * p
        cross = jnp.dot(low_ref[at + BLK : at + 256, at : at + BLK], first, precision=HI)
        cross = -jnp.dot(second, cross, precision=HI)
        high, rest = split(four(first, zero, cross, second))
        yh[p] = high
        yl[p] = rest
    for p in range(3):
        at = 256 * p
        x = four(top_ref[2 * p, 0], top_ref[2 * p, 1], top_ref[2 * p + 1, 0], top_ref[2 * p + 1, 1])
        if p:
            x = x - dot3((lh[at : at + 256, :at], ll[at : at + 256, :at]), (uh[:at, :], ul[:at, :]), NN)
        high, rest = split(dot3((yh[p], yl[p]), split(x), NN))
        uh[at : at + 256, :] = high
        ul[at : at + 256, :] = rest

    def stack(get):
        return jnp.concatenate([jnp.concatenate([get(i, 0), get(i, 1)], axis=1) for i in range(8)], axis=0)

    acc = front_ref[...] + stack(lambda i, j: moved_ref[i, j])
    xs = []
    for p in range(3):
        at = 256 * p
        x = stack(lambda i, j: rows_ref[i, 2 * p + j])
        for m in range(p):
            cut = slice(256 * m, 256 * m + 256)
            x = x - dot3(xs[m], (lh[at : at + 256, cut], ll[at : at + 256, cut]), NT)
        x = dot3(split(x), (yh[p], yl[p]), NT)
        x_ref[:, at : at + 256] = x
        xs.append(split(x))
        acc = acc - dot3(xs[p], (uh[at : at + 256, :], ul[at : at + 256, :]), NN)
    out_ref[...] = acc

    @pl.when(row < NPIV)
    def _():
        out_ref[:BLK, :] = jnp.zeros((BLK, 256), jnp.float32)
        x_ref[:BLK, :] = low_ref[pl.ds(pl.multiple_of(row * BLK, BLK), BLK), :]

    @pl.when((sub == 0) & (col < NPIV))
    def _():
        out_ref[:, :BLK] = x_ref[:, pl.ds(pl.multiple_of(col * BLK, BLK), BLK)]


def schur(rows, top, moved, front, low, inv):
    return pl.pallas_call(
        schur_kernel,
        out_shape=jax.ShapeDtypeStruct((1024, 256), jnp.float32),
        in_specs=[VM] * 6,
        out_specs=VM,
        scratch_shapes=[
            pltpu.VMEM((PIV, PIV), jnp.bfloat16),
            pltpu.VMEM((PIV, PIV), jnp.bfloat16),
            pltpu.VMEM((3, 256, 256), jnp.bfloat16),
            pltpu.VMEM((3, 256, 256), jnp.bfloat16),
            pltpu.VMEM((PIV, 256), jnp.bfloat16),
            pltpu.VMEM((PIV, 256), jnp.bfloat16),
            pltpu.VMEM((1024, PIV), jnp.float32),
        ],
        compiler_params=pltpu.CompilerParams(vmem_limit_bytes=32 * 1024 * 1024),
        name="schur",
    )(rows, top, moved, front, low, inv)


def body(front, child, child_map):
    k, maps, buf, panel, first = gather_all(
        pltpu.with_memory_space_constraint(child, pltpu.HBM),
        pltpu.with_memory_space_constraint(front, pltpu.HBM),
        child_map,
    )
    acc = place(maps, buf)
    low, inv, rows, moved, top = factor_all(k.reshape(NTILE, BLK, BLK), acc, panel, front, first)
    return schur(
        rows.reshape(8, NPIV, BLK, BLK),
        top.reshape(NPIV, 2, BLK, BLK),
        moved.reshape(8, 2, BLK, BLK),
        front,
        low,
        inv,
    )


def solution(mesh):
    placed = (P("row", ("col", "sub")), P("sub", "row", "col"), P("sub", None))
    return jax.shard_map(
        body, mesh=mesh, in_specs=placed, out_specs=P("row", ("col", "sub")), check_vma=False
    )
```

```python
import jax
import jax.numpy as jnp
from jax import lax
from jax.experimental import pallas as pl
from jax.experimental.pallas import tpu as pltpu
from jax.sharding import PartitionSpec as P

BLK = 128
NPIV = 6
PIV = NPIV * BLK
PLANE = ("col", "sub")
HI = lax.Precision.HIGHEST
VM = pl.BlockSpec(memory_space=pltpu.VMEM)
SM = pl.BlockSpec(memory_space=pltpu.SMEM)


def nt(a, b, precision=HI):
    return lax.dot_general(a, b, (((1,), (1,)), ((), ())), precision=precision, preferred_element_type=jnp.float32)
def tn(a, b, precision=HI):
    return lax.dot_general(a, b, (((0,), (0,)), ((), ())), precision=precision, preferred_element_type=jnp.float32)

def split(x):
    high = x.astype(jnp.bfloat16)
    return high, (x - high.astype(jnp.float32)).astype(jnp.bfloat16)


def dot3(a, b, dims):
    def one(x, y):
        return lax.dot_general(x, y, (dims, ((), ())), preferred_element_type=jnp.float32)

    return one(a[0], b[0]) + (one(a[0], b[1]) + one(a[1], b[0]))


def tn3(a, b):
    return dot3(split(a), split(b), ((0,), (0,)))


def nt3(a, b):
    return dot3(split(a), split(b), ((1,), (1,)))


def rsqrt(x):
    return lax.rsqrt(x)

def wide(x):
    return jnp.concatenate([x, x], axis=1)

def eliminate(a_ref):
    sub = lax.broadcasted_iota(jnp.int32, (8, 256), 0)
    ahead = []
    for g in range(16):
        if g == 0:
            ahead = [a_ref[8 * h : 8 * h + 8, :] for h in range(2 + 1)]
        elif g + 2 < 16:
            ahead.append(a_ref[8 * (g + 2) : 8 * (g + 2) + 8, :])
        rows = ahead.pop(0)
        left = rows[:, :BLK]
        e = {}
        for j in range(8):
            c = jnp.broadcast_to(left[:, 8 * g + j : 8 * g + j + 1], (8, BLK))
            for i in range(j, 8):
                e[j, i] = jnp.broadcast_to(c[i : i + 1, :], (8, BLK))
        r = [jnp.broadcast_to(rows[i : i + 1, :], (8, 256)) for i in range(8)]
        cols = [[jnp.broadcast_to(n[:, 8 * g + j : 8 * g + j + 1], (8, BLK)) for j in range(8)] for n in ahead]
        out = None
        for j in range(8):
            s = rsqrt(e[j, j])
            u = {i: e[j, i] * s for i in range(j + 1, 8)}
            for i in range(j + 1, 8):
                for m in range(i, 8):
                    e[i, m] = e[i, m] - u[i] * u[m]
            rj = r[j] * wide(s)
            for i in range(j + 1, 8):
                r[i] = r[i] - wide(u[i]) * rj
            for h in range(len(ahead)):
                cj = cols[h][j] * s
                for m in range(j + 1, 8):
                    cols[h][m] = cols[h][m] - cj * u[m]
                ahead[h] = ahead[h] - wide(cj) * rj
            out = rj if out is None else jnp.where(sub == j, rj, out)
        a_ref[8 * g : 8 * g + 8, :] = out
        low = 8 * (g + 1 + 2)
        if low < BLK:
            t = tn3(out[:, :BLK], out)
            a_ref[low:, :] = a_ref[low:, :] - t[low:, :]

def factor_begin(l_ref, m_ref):
    for i in range(NPIV - 1):
        m_ref[i * BLK : (i + 1) * BLK, (i + 1) * BLK :] = jnp.zeros((BLK, PIV - (i + 1) * BLK), jnp.float32)
    l_ref[...] = jnp.zeros_like(l_ref)


def diagonal(a_ref, block):
    r_iota = lax.broadcasted_iota(jnp.int32, (BLK, BLK), 0)
    c_iota = lax.broadcasted_iota(jnp.int32, (BLK, BLK), 1)
    a_ref[:, :BLK] = block
    a_ref[:, BLK:] = jnp.where(r_iota == c_iota, 1.0, 0.0)
    eliminate(a_ref)


def factor_finish(b, l_ref, y_ref, a_ref, m_ref):
    r_iota = lax.broadcasted_iota(jnp.int32, (BLK, BLK), 0)
    c_iota = lax.broadcasted_iota(jnp.int32, (BLK, BLK), 1)
    at = pl.ds(b * BLK if isinstance(b, int) else pl.multiple_of(b * BLK, BLK), BLK)
    y = a_ref[:, BLK:]
    y_ref[b] = y
    l_ref[at, at] = jnp.where(r_iota >= c_iota, a_ref[:, :BLK].T, 0.0)

    ys = split(y)

    def solve(i, c):
        rows = pl.ds(pl.multiple_of(i * BLK, BLK), BLK)
        l_ref[rows, at] = dot3(split(m_ref[rows, at]), ys, ((1,), (1,)))
        return c

    lax.fori_loop(b + 1, NPIV, solve, 0)

    column = split(l_ref[:, at])

    def update(i, c):
        rows = pl.ds(pl.multiple_of(i * BLK, BLK), BLK)
        m_ref[rows, :] = m_ref[rows, :] - dot3(split(l_ref[rows, at]), column, ((1,), (1,)))
        return c

    lax.fori_loop(b + 1, NPIV, update, 0)


def factor_steps(l_ref, y_ref, a_ref, m_ref, progress):
    def step(b, carry):
        progress(b)
        at = pl.ds(pl.multiple_of(b * BLK, BLK), BLK)
        diagonal(a_ref, m_ref[at, at])
        factor_finish(b, l_ref, y_ref, a_ref, m_ref)
        return carry

    lax.fori_loop(1, NPIV, step, 0)


MESH = pl.DeviceIdType.MESH
TILES = [(i, j) for i in range(NPIV) for j in range(i + 1)]
NTILE = len(TILES)


class Place:
    def __init__(self):
        self.r, self.c, self.s = (lax.axis_index(a) for a in ("row", "col", "sub"))
        self.e = self.c * 4 + self.s
        self.core = self.c % 2
        self.chip = (self.c // 2) * 4 + self.s
        self.partner = (self.r, self.c + 1 - 2 * self.core, self.s)

    def plane(self, d):
        p = (self.e + d) % 32
        return p, (self.r, p // 4, p % 4)

    def same_core(self, d):
        p = (self.chip + d) % 16
        c = (p // 4) * 2 + self.core
        return c * 4 + p % 4, (self.r, c, p % 4)

    def line(self, d):
        return ((self.r + d) % 8, self.c, self.s)

    def greet(self, meanwhile):
        barrier = pltpu.get_barrier_semaphore()

        def plane(d, carry):
            pl.semaphore_signal(barrier, inc=1, device_id=self.plane(d)[1], device_id_type=MESH)
            return carry

        def line(d, carry):
            pl.semaphore_signal(barrier, inc=1, device_id=self.line(d), device_id_type=MESH)
            return carry

        lax.fori_loop(1, 32, plane, 0)
        lax.fori_loop(1, 8, line, 0)
        meanwhile()
        pl.semaphore_wait(barrier, 38)


def push(src, dst, ssem, rsem, device):
    return pltpu.make_async_remote_copy(
        src_ref=src, dst_ref=dst, send_sem=ssem, recv_sem=rsem, device_id=device, device_id_type=MESH
    )


def arrive(ref, sem):
    pltpu.make_async_copy(ref, ref, sem).wait()


def loop(low, high, f):
    def one(d, carry):
        f(d)
        return carry

    lax.fori_loop(low, high, one, 0)


def gather_kernel(
    child_hbm, whole_ref, list_hbm, k_ref, maps_ref, buf_ref, panel_ref, first_ref,
    list_ref, tile_ref, child_ref, strip_ref, front_ref, map_ref, z_ref, acc_ref, send, got, z_got, f_got, k_got, p_got, ring_got,
):
    at = Place()
    r, c, s, e = at.r, at.c, at.s, at.e
    has_front = (c < NPIV) & (s == 0)

    def prepare():
        fetch = pltpu.make_async_copy(whole_ref.at[:, pl.ds(0, BLK)], strip_ref, got.at[5])
        fetch.start()
        child_fetch = pltpu.make_async_copy(child_hbm.at[0], tile_ref, got.at[7])
        child_fetch.start()
        list_fetch = pltpu.make_async_copy(list_hbm, list_ref, got.at[8])
        list_fetch.start()
        list_fetch.wait()
        for i in range(16):
            map_ref[i : i + 1, :] = jnp.full((1, BLK), list_ref[0, i], jnp.int32)
        for i in range(NPIV - 1):
            z_ref[i, 4 * (i + 1) : 24] = jnp.zeros((20 - 4 * i, 4, BLK), jnp.float32)
        child_fetch.wait()
        for i in range(2):
            for j in range(2):
                child_ref[:, i, j] = tile_ref[i * BLK : (i + 1) * BLK, j * BLK : (j + 1) * BLK].reshape(32, 4, BLK)
        fetch.wait()

        @pl.when(has_front)
        def _():
            for i in range(8):
                front_ref[i] = strip_ref[i * BLK : (i + 1) * BLK, :].reshape(32, 4, BLK)

    at.greet(prepare)
    seat = jnp.minimum(c, NPIV - 1)

    def child_copy(d, h):
        p, device = at.plane(d)
        return push(child_ref.at[p, h], buf_ref.at[r, e, h], send.at[9 * h], got.at[6 * h], device)

    def own_child(h):
        return pltpu.make_async_copy(child_ref.at[e, h], buf_ref.at[r, e, h], got.at[6 * h])

    def front_copy(d):
        p, device = at.plane(d)
        return push(front_ref.at[0, p], panel_ref.at[seat, 0], send.at[1], got.at[1], device)

    def rest_copy(d):
        p, device = at.plane(d)
        return push(front_ref.at[pl.ds(1, 7), p], panel_ref.at[seat, pl.ds(1, 7)], send.at[4], got.at[4], device)

    def map_copy(d):
        return push(map_ref, maps_ref.at[s], send.at[2], got.at[2], (r, c, (s + d) % 4))

    own_child(0).start()
    own_child(1).start()
    pltpu.make_async_copy(map_ref, maps_ref.at[s], got.at[2]).start()
    loop(1, 32, lambda d: child_copy(d, 0).start())

    @pl.when(has_front)
    def _():
        pltpu.make_async_copy(front_ref.at[0, e], panel_ref.at[seat, 0], got.at[1]).start()
        loop(1, 32, lambda d: front_copy(d).start())

    for d in range(1, 4):
        map_copy(d).start()
    loop(1, 32, lambda d: child_copy(d, 1).start())

    def z_copies(i, d):
        device = at.line(d)
        tiles, own = pl.ds(0, 4 * (i + 1)), pl.ds(0, i + 1)
        return (
            push(buf_ref.at[i, tiles, 0, 0], z_ref.at[i, tiles], send.at[3], z_got.at[i], device),
            push(panel_ref.at[own, 0], z_ref.at[i, pl.ds(24, i + 1)], send.at[3], f_got.at[i], device),
        )

    def ring_copy(way, k, h):
        block = (r + 8 - k) % 8 if way == 0 else (r + k) % 8
        half = buf_ref.at[block, :, h]
        return push(half, half, send.at[5 + way], ring_got.at[way, 2 * k + h], at.line(1 if way == 0 else 7))

    def ring_wait(way, k, h):
        block = (r + 7 - k) % 8 if way == 0 else (r + 1 + k) % 8
        arrive(buf_ref.at[block, :, h], ring_got.at[way, 2 * k + h])

    hops = [(way, k, h) for k in range(4) for h in range(2) for way in range(2) if k < 3 or h == way]

    def ring_step(k):
        for hop in hops:
            if hop[1] == k:
                if k:
                    ring_wait(hop[0], k - 1, hop[2])
                elif hop == (0, 0, 1):
                    arrive(buf_ref.at[r, :, 1], got.at[6])
                ring_copy(*hop).start()

    arrive(buf_ref.at[r, :, 0], got.at[0])
    arrive(panel_ref.at[:, 0], got.at[1])

    for i in range(NPIV):
        @pl.when(r == i)
        def _():
            tiles, own = pl.ds(0, 4 * (i + 1)), pl.ds(0, i + 1)
            pltpu.make_async_copy(buf_ref.at[i, tiles, 0, 0], z_ref.at[i, tiles], z_got.at[i]).start()
            pltpu.make_async_copy(panel_ref.at[own, 0], z_ref.at[i, pl.ds(24, i + 1)], f_got.at[i]).start()
            for d in (4, 3, 5, 2, 6, 1, 7):
                for copy in z_copies(i, d):
                    copy.start()

    @pl.when(has_front)
    def _():
        pltpu.make_async_copy(front_ref.at[pl.ds(1, 7), e], panel_ref.at[seat, pl.ds(1, 7)], got.at[4]).start()
        loop(1, 32, lambda d: rest_copy(d).start())

    ring_step(0)
    arrive(maps_ref, got.at[2])
    for i in range(NPIV):
        arrive(z_ref.at[i, pl.ds(0, 4 * (i + 1))], z_got.at[i])
        arrive(z_ref.at[i, pl.ds(24, i + 1)], f_got.at[i])

    for t, (i, j) in enumerate(TILES):
        acc_ref[t] = z_ref[i, 24 + j]

    def add_child(q):
        wanted = maps_ref[q][:NPIV]
        strips = []
        for j in range(NPIV):
            strip = None
            for seat_j in range(j + 1):
                pick = jnp.where(wanted[seat_j : seat_j + 1] == j, 1.0, 0.0)[None]
                term = z_ref[:, seat_j * 4 + q] * pick
                strip = term if strip is None else strip + term
            strips.append(strip)
        for j in range(NPIV):
            for i in range(j, NPIV):
                pick = jnp.where(wanted == i, 1.0, 0.0)[:, None, :]
                acc_ref[i * (i + 1) // 2 + j] += jnp.sum(strips[j] * pick, axis=0)

    loop(0, 4, add_child)

    own_k = pltpu.make_async_copy(acc_ref, k_ref.at[:, e], got.at[3])
    own_k.start()

    def k_copy(d):
        return push(acc_ref, k_ref.at[:, e], send.at[7], k_got.at[d], at.same_core(d)[1])

    def pair_copy(d):
        where_e = at.same_core(16 - d)[0]
        return push(k_ref.at[:, where_e], k_ref.at[:, where_e], send.at[8], p_got.at[d], at.partner)

    def forward(d):
        k_copy(d).wait_recv()
        pair_copy(d).start()

    loop(1, 16, lambda d: k_copy(d).start())
    ring_step(1)
    own_k.wait()
    pair_copy(0).start()
    ring_step(2)
    loop(1, 16, forward)
    ring_step(3)
    loop(0, 16, lambda d: pair_copy(d).wait())
    diagonal(first_ref, k_ref[0].reshape(BLK, BLK))
    arrive(panel_ref.at[:, pl.ds(1, 7)], got.at[4])
    ring_wait(0, 2, 1)
    ring_wait(1, 2, 0)
    ring_wait(0, 3, 0)
    ring_wait(1, 3, 1)

    loop(1, 16, lambda d: k_copy(d).wait_send())
    loop(1, 32, lambda d: child_copy(d, 0).wait_send())
    loop(1, 32, lambda d: child_copy(d, 1).wait_send())

    @pl.when(has_front)
    def _():
        loop(1, 32, lambda d: front_copy(d).wait_send())
        loop(1, 32, lambda d: rest_copy(d).wait_send())

    for d in range(1, 4):
        map_copy(d).wait_send()
    for i in range(NPIV):
        @pl.when(r == i)
        def _():
            for d in range(1, 8):
                for copy in z_copies(i, d):
                    copy.wait_send()

    for hop in hops:
        ring_copy(*hop).wait_send()


def gather_all(child, front, child_map):
    dma = pltpu.SemaphoreType.DMA
    return pl.pallas_call(
        gather_kernel,
        out_shape=(
            jax.ShapeDtypeStruct((NTILE, 32, 4, BLK), jnp.float32),
            jax.ShapeDtypeStruct((4, 16, BLK), jnp.int32),
            jax.ShapeDtypeStruct((8, 32, 2, 2, 4, BLK), jnp.float32),
            jax.ShapeDtypeStruct((NPIV, 8, 4, BLK), jnp.float32),
            jax.ShapeDtypeStruct((BLK, 2 * BLK), jnp.float32),
        ),
        in_specs=[pl.BlockSpec(memory_space=pltpu.HBM)] * 3,
        out_specs=(VM,) * 5,
        scratch_shapes=[
            pltpu.SMEM((1, 16), jnp.int32),
            pltpu.VMEM((256, 256), jnp.float32),
            pltpu.VMEM((32, 2, 2, 4, BLK), jnp.float32),
            pltpu.VMEM((1024, BLK), jnp.float32),
            pltpu.VMEM((8, 32, 4, BLK), jnp.float32),
            pltpu.VMEM((16, BLK), jnp.int32),
            pltpu.VMEM((NPIV, 30, 4, BLK), jnp.float32),
            pltpu.VMEM((NTILE, 4, BLK), jnp.float32),
            dma((10,)), dma((9,)), dma((NPIV,)), dma((NPIV,)), dma((16,)), dma((16,)), dma((2, 8)),
        ],
        compiler_params=pltpu.CompilerParams(collective_id=0, has_side_effects=True, vmem_limit_bytes=20 * 1024 * 1024),
        name="gather_all",
    )(child, front, child_map)


def factor_kernel(
    k_ref, acc_ref, panel_ref, front_ref, first_ref, low_ref, inv_ref, rows_ref, moved_ref, top_ref,
    a_ref, m_ref, piece_ref, share_ref, w_ref, send, got, r_got, p_got, t_got,
):
    at = Place()
    r, c, s, e = at.r, at.c, at.s, at.e
    spot = jnp.minimum(r, NPIV - 1)

    def prepare():
        fetch = [pltpu.make_async_copy(acc_ref.at[4 * j, :, 0], piece_ref.at[j], got.at[2 + j]) for j in range(NPIV)]
        tiles = [
            pltpu.make_async_copy(
                k_ref.at[t], m_ref.at[pl.ds(i * BLK, BLK), pl.ds(j * BLK, BLK)], got.at[2 + NPIV + t]
            )
            for t, (i, j) in enumerate(TILES)
        ]
        for copy in fetch + tiles:
            copy.start()
        factor_begin(low_ref, m_ref)
        for copy in fetch:
            copy.wait()
        for j in range(NPIV):
            for slot in range(8):
                share_ref[slot, j] = piece_ref[j, slot] + panel_ref[j, slot]
        for copy in tiles:
            copy.wait()
        factor_finish(0, low_ref, inv_ref, first_ref, m_ref)

    at.greet(prepare)

    top_part, rest_part = pl.ds(0, 1), pl.ds(1, 7)

    def move_copy(d, part, k):
        p, device = at.plane(d)
        return push(acc_ref.at[p, part], moved_ref.at[part, :, e], send.at[4 * k], got.at[k * 29], device)

    def own_move(part, k):
        return pltpu.make_async_copy(acc_ref.at[e, part], moved_ref.at[part, :, e], got.at[k * 29])

    own_move(top_part, 0).start()
    loop(1, 32, lambda d: move_copy(d, top_part, 0).start())

    own_rows = pltpu.make_async_copy(share_ref, rows_ref.at[:, :, e], got.at[1])

    def rows_copy(d):
        return push(share_ref, rows_ref.at[:, :, e], send.at[1], r_got.at[d], at.same_core(d)[1])

    def pair_copy(d):
        where_e = at.same_core(16 - d)[0]
        return push(rows_ref.at[:, :, where_e], rows_ref.at[:, :, where_e], send.at[2], p_got.at[d], at.partner)

    def top_copy(d):
        return push(w_ref, top_ref.at[spot], send.at[3], t_got.at[spot], at.line(d))

    own_rows.start()
    loop(1, 16, lambda d: rows_copy(d).start())
    own_move(rest_part, 1).start()
    loop(1, 32, lambda d: move_copy(d, rest_part, 1).start())

    def after_first():
        own_rows.wait()
        pair_copy(0).start()
        arrive(moved_ref.at[top_part], got.at[0])

        @pl.when(r < NPIV)
        def _():
            for i in range(2):
                w_ref[i] = moved_ref[0, i] + front_ref[:BLK, i * BLK : (i + 1) * BLK].reshape(32, 4, BLK)
            pltpu.make_async_copy(w_ref, top_ref.at[spot], t_got.at[spot]).start()
            for d in (4, 3, 5, 2, 6, 1, 7):
                top_copy(d).start()

    def forward(d):
        rows_copy(d).wait_recv()
        pair_copy(d).start()

    def progress(b):
        pl.when(b == 2)(after_first)
        pl.when(b == 4)(lambda: loop(1, 16, forward))

    factor_steps(low_ref, inv_ref, a_ref, m_ref, progress)

    loop(0, 16, lambda d: pair_copy(d).wait())
    arrive(moved_ref.at[rest_part], got.at[29])
    for i in range(NPIV):
        arrive(top_ref.at[i], t_got.at[i])
    loop(1, 16, lambda d: rows_copy(d).wait_send())
    loop(1, 32, lambda d: move_copy(d, top_part, 0).wait_send())
    loop(1, 32, lambda d: move_copy(d, rest_part, 1).wait_send())

    @pl.when(r < NPIV)
    def _():
        for d in range(1, 8):
            top_copy(d).wait_send()


def factor_all(k, acc, panel, front, first):
    dma = pltpu.SemaphoreType.DMA
    f32 = lambda *shape: jax.ShapeDtypeStruct(shape, jnp.float32)
    return pl.pallas_call(
        factor_kernel,
        out_shape=(
            f32(PIV, PIV),
            f32(NPIV, BLK, BLK),
            f32(8, NPIV, 32, 4, BLK),
            f32(8, 2, 32, 4, BLK),
            f32(NPIV, 2, 32, 4, BLK),
        ),
        in_specs=[pl.BlockSpec(memory_space=pltpu.HBM)] * 2 + [VM] * 3,
        out_specs=(VM,) * 5,
        scratch_shapes=[
            pltpu.VMEM((BLK, 256), jnp.float32),
            pltpu.VMEM((PIV, PIV), jnp.float32),
            pltpu.VMEM((NPIV, 8, 4, BLK), jnp.float32),
            pltpu.VMEM((8, NPIV, 4, BLK), jnp.float32),
            pltpu.VMEM((2, 32, 4, BLK), jnp.float32),
            dma((5,)), dma((3 + NPIV + NTILE,)), dma((16,)), dma((16,)), dma((NPIV,)),
        ],
        compiler_params=pltpu.CompilerParams(collective_id=1, has_side_effects=True, vmem_limit_bytes=40 * 1024 * 1024),
        name="factor_all",
    )(k, acc, panel, front, first)


def place_kernel(map_ref, buf_ref, acc_ref):
    acc_ref[...] = jnp.zeros_like(acc_ref)
    row = lax.axis_index("row")

    for q in range(4):
        targets = [map_ref[q, j, 0] for j in range(16)]
        spots = [(j % 8 * 4 + j // 16, (j // 8) % 2) for j in targets]

        def child_row(block_row):
            i = map_ref[q, block_row, 0]

            @pl.when(i % 8 == row)
            def _():
                slot = i // 8
                for block_col, (dest, half) in enumerate(spots):
                    acc_ref[dest, slot, half] += buf_ref[
                        block_row % 8, block_col % 8 * 4 + q, block_row // 8, block_col // 8
                    ]

        loop(0, 16, child_row)


def place(maps, buf):
    return pl.pallas_call(
        place_kernel,
        out_shape=jax.ShapeDtypeStruct((32, 8, 2, 4, BLK), jnp.float32),
        in_specs=[SM, VM],
        out_specs=VM,
        compiler_params=pltpu.CompilerParams(vmem_limit_bytes=8 * 1024 * 1024),
        name="place",
    )(maps, buf)


NT = ((1,), (1,))
NN = ((1,), (0,))


def four(a, b, c, d):
    return jnp.concatenate([jnp.concatenate([a, b], axis=1), jnp.concatenate([c, d], axis=1)], axis=0)


def schur_kernel(
    rows_ref, top_ref, moved_ref, front_ref, low_ref, inv_ref, out_ref,
    lh, ll, yh, yl, uh, ul, x_ref,
):
    row, col, sub = (lax.axis_index(a) for a in ("row", "col", "sub"))
    high, rest = split(low_ref[...])
    lh[...] = high
    ll[...] = rest
    zero = jnp.zeros((BLK, BLK), jnp.float32)
    for p in range(3):
        first, second = inv_ref[2 * p], inv_ref[2 * p + 1]
        at = 256 * p
        cross = jnp.dot(low_ref[at + BLK : at + 256, at : at + BLK], first, precision=HI)
        cross = -jnp.dot(second, cross, precision=HI)
        high, rest = split(four(first, zero, cross, second))
        yh[p] = high
        yl[p] = rest
    for p in range(3):
        at = 256 * p
        x = four(top_ref[2 * p, 0], top_ref[2 * p, 1], top_ref[2 * p + 1, 0], top_ref[2 * p + 1, 1])
        if p:
            x = x - dot3((lh[at : at + 256, :at], ll[at : at + 256, :at]), (uh[:at, :], ul[:at, :]), NN)
        high, rest = split(dot3((yh[p], yl[p]), split(x), NN))
        uh[at : at + 256, :] = high
        ul[at : at + 256, :] = rest

    def stack(get):
        return jnp.concatenate([jnp.concatenate([get(i, 0), get(i, 1)], axis=1) for i in range(8)], axis=0)

    acc = front_ref[...] + stack(lambda i, j: moved_ref[i, j])
    xs = []
    for p in range(3):
        at = 256 * p
        x = stack(lambda i, j: rows_ref[i, 2 * p + j])
        for m in range(p):
            cut = slice(256 * m, 256 * m + 256)
            x = x - dot3(xs[m], (lh[at : at + 256, cut], ll[at : at + 256, cut]), NT)
        x = dot3(split(x), (yh[p], yl[p]), NT)
        x_ref[:, at : at + 256] = x
        xs.append(split(x))
        acc = acc - dot3(xs[p], (uh[at : at + 256, :], ul[at : at + 256, :]), NN)
    out_ref[...] = acc

    @pl.when(row < NPIV)
    def _():
        out_ref[:BLK, :] = jnp.zeros((BLK, 256), jnp.float32)
        x_ref[:BLK, :] = low_ref[pl.ds(pl.multiple_of(row * BLK, BLK), BLK), :]

    @pl.when((sub == 0) & (col < NPIV))
    def _():
        out_ref[:, :BLK] = x_ref[:, pl.ds(pl.multiple_of(col * BLK, BLK), BLK)]


def schur(rows, top, moved, front, low, inv):
    return pl.pallas_call(
        schur_kernel,
        out_shape=jax.ShapeDtypeStruct((1024, 256), jnp.float32),
        in_specs=[VM] * 6,
        out_specs=VM,
        scratch_shapes=[
            pltpu.VMEM((PIV, PIV), jnp.bfloat16),
            pltpu.VMEM((PIV, PIV), jnp.bfloat16),
            pltpu.VMEM((3, 256, 256), jnp.bfloat16),
            pltpu.VMEM((3, 256, 256), jnp.bfloat16),
            pltpu.VMEM((PIV, 256), jnp.bfloat16),
            pltpu.VMEM((PIV, 256), jnp.bfloat16),
            pltpu.VMEM((1024, PIV), jnp.float32),
        ],
        compiler_params=pltpu.CompilerParams(vmem_limit_bytes=32 * 1024 * 1024),
        name="schur",
    )(rows, top, moved, front, low, inv)


def body(front, child, child_map):
    k, maps, buf, panel, first = gather_all(
        pltpu.with_memory_space_constraint(child, pltpu.HBM),
        pltpu.with_memory_space_constraint(front, pltpu.HBM),
        pltpu.with_memory_space_constraint(child_map, pltpu.HBM),
    )
    acc = place(maps, buf)
    low, inv, rows, moved, top = factor_all(k.reshape(NTILE, BLK, BLK), acc, panel, front, first)
    return schur(
        rows.reshape(8, NPIV, BLK, BLK),
        top.reshape(NPIV, 2, BLK, BLK),
        moved.reshape(8, 2, BLK, BLK),
        front,
        low,
        inv,
    )


def solution(mesh):
    placed = (P("row", ("col", "sub")), P("sub", "row", "col"), P("sub", None))
    return jax.shard_map(
        body, mesh=mesh, in_specs=placed, out_specs=P("row", ("col", "sub")), check_vma=False
    )
```
